32 devices in a mesh: groups: 2 (over y), tiles: 4 (over z), chan: 2 (over x), rep: 2 (over core).
Axes of the slice: x: 2, y: 2, z: 4, core: 2. Of those that a mesh axis runs over, the one named last changes fastest.
Arguments:
- fields: bfloat16 [4, 12, 128, 256], P(('groups', 'rep'), 'tiles'), parts along dimension 0, may hold values from -6 to 6
- tile_rows: int32 [4, 3], replicated, may hold values from -1 to 5, as said below
- weights: bfloat16 [9, 128, 128], P(None, 'chan'), may hold values from -0.1875 to 0.1875
- bias: float32 [128], P('chan'), may hold values from -3 to 3
- cotangent: bfloat16 [4, 12, 128, 256], P(('groups', 'rep'), 'tiles', 'chan'), parts along dimension 0, may hold values from -6 to 6
Outputs:
- result: bfloat16 [4, 12, 128, 256], P(('groups', 'rep'), 'tiles', 'chan'), parts along dimension 0
- grad_fields: bfloat16 [4, 12, 128, 256], P(('groups', 'rep'), 'tiles', 'chan'), parts along dimension 0
- grad_weights: float32 [18, 128, 128], P('groups', 'chan'), parts along dimension 0
- grad_bias: float32 [256], P(('groups', 'chan')), parts along dimension 0
The draws below stay inside these ranges and needn't reach their ends.
There are 2 independent parts, one for each index of `groups`. The reference program is written for one: setup_inputs(seed, part) draws one part's arguments, and reference() takes and returns one part's arrays. A program takes and returns all parts, laid end to end along the dimension named above; an argument that names none is the same for every part. Nothing has to cross between parts.
Inputs may be any that keep to these rules, and one draw needn't show every extreme that they name: tile_rows[d, k] is the tile row of the tile in slot k of tile column d, or -1 for an empty slot; the rows of one column are distinct, every column holds one tile or more, and some column holds 3.
All inputs are finite; a program needn't handle non-finite values.
Results may differ from the reference program's by a relative error of at most 0.005.
Values may be sent and summed in bfloat16 or wider, within the bound.
No kernel may reach another device: no remote copies, remote signals or barrier semaphores. Data moves between devices by JAX's collectives and lax.ppermute only.
A program may use at most 64 MiB of HBM per device.

```python
import math
import jax
import jax.numpy as jnp
from jax import lax

C = 128
TS = 16
SLOTS = 3
TY = 6
SLOTS_ALL = 12
SAMPLES = 2
N_TILES = 4


def draw_tile_rows(key, part):
    column_ids = jnp.arange(N_TILES)
    full_column = jax.random.randint(jax.random.fold_in(key, 1), (), 0, N_TILES)
    thin_column = (full_column + 2) % N_TILES
    mirror_column = N_TILES - 1 - full_column
    tile_counts = jax.random.randint(jax.random.fold_in(key, 2), (N_TILES,), 1, SLOTS + 1)
    tile_counts = jnp.where(column_ids == full_column, SLOTS, tile_counts)
    tile_counts = jnp.where(column_ids == thin_column, 1, tile_counts)
    column_keys = jax.random.split(jax.random.fold_in(key, 3), N_TILES)

    def one_column(column_key):
        row_key, other_key, slot_key = jax.random.split(column_key, 3)
        drawn = jax.random.permutation(row_key, 2 * SLOTS)[:SLOTS]
        others = jax.random.permutation(other_key, 2 * SLOTS - 1)
        slot_order = jax.random.permutation(slot_key, SLOTS)
        crest_rows = jnp.where(slot_order == 0, 2 * SLOTS - 1, others[jnp.maximum(slot_order - 1, 0)])
        return (drawn, crest_rows, slot_order)
    drawn, crest_rows, slot_order = jax.vmap(one_column)(column_keys)
    with_crest = (column_ids == full_column) | (column_ids == mirror_column)
    chosen_rows = jnp.where(with_crest[:, None], crest_rows, drawn)
    return jnp.where(slot_order < tile_counts[:, None], chosen_rows, -1).astype(jnp.int32)


def shard_levels(key, shape, shards, smallest, top_value):
    def one(position, shards_of):
        steps = jax.random.uniform(jax.random.fold_in(jax.random.fold_in(key, 6), position), (shards_of,), jnp.float32, smallest / len(shards), top_value / len(shards))
        return jnp.repeat(jnp.exp(steps), shape[position] // shards_of).reshape((-1,) + (1,) * (len(shape) - position - 1))

    loudness = one(*shards[0])
    for cut in shards[1:]:
        loudness = loudness * one(*cut)
    return loudness


def centred(rng, shape, spread, most, cuts=(), dtype=jnp.bfloat16):
    factor_of = shard_levels(rng, shape, cuts, -0.22, 0.18) if cuts else 1.0
    entries = jax.random.normal(rng, shape, jnp.float32) * spread * factor_of
    return jnp.minimum(jnp.maximum(entries, -most), most).astype(dtype)


def setup_inputs(seed: int = 0, part: int = 0) -> dict:
    keys = jax.random.split(jax.random.key(seed), 6)
    part_keys = jax.random.split(jax.random.fold_in(keys[5], part), 6)
    fields = centred(part_keys[0], (SAMPLES, SLOTS_ALL, C, TS * TS), 1.0, 6.0, ((0, 2), (1, 4)))
    tile_rows = draw_tile_rows(jax.random.fold_in(keys[5], 71), part)
    weights = centred(keys[2], (9, C, C), (9 * C) ** -0.5, 0.1875, ((1, 2),))
    bias = centred(keys[3], (C,), 0.5, 3.0, ((0, 2),), jnp.float32)
    cotangent = centred(part_keys[4], (SAMPLES, SLOTS_ALL, C, TS * TS), 1.0, 6.0, ((0, 2), (1, 4), (2, 2)))
    return dict(fields=fields, tile_rows=tile_rows, weights=weights, bias=bias, cotangent=cotangent)


def match_rows(wanted, held_rows, occupied):
    matches = (wanted[:, :, None] == held_rows[:, None, :]) & occupied[:, :, None] & (held_rows[:, None, :] >= 0)
    return matches.astype(jnp.float32)

def select_rows(selector, values):
    return jnp.einsum('nkl,nl...->nk...', selector, values.astype(jnp.float32), precision=lax.Precision.HIGHEST)

def make_lookups(tile_rows):
    left_rows = jnp.roll(tile_rows, 1, axis=0)
    right_rows = jnp.roll(tile_rows, -1, axis=0)
    occupied = tile_rows >= 0
    at_top = (tile_rows == TY - 1).astype(jnp.float32)
    return (match_rows(tile_rows, left_rows, occupied), match_rows(tile_rows, right_rows, occupied), match_rows(tile_rows - 1, tile_rows, occupied), match_rows(tile_rows + 1, tile_rows, occupied), at_top)

def pad_tiles(values, lookups):
    west_match, east_match, below, above, at_top = lookups
    from_left = jnp.roll(values[..., -1], 1, axis=0)
    from_right = jnp.roll(values[..., 0], -1, axis=0)
    west_pad = select_rows(west_match, from_left).astype(jnp.bfloat16)
    east_pad = select_rows(east_match, from_right).astype(jnp.bfloat16)
    widened = jnp.concatenate([west_pad[..., None], values, east_pad[..., None]], axis=-1)
    south_pad = select_rows(below, widened[:, :, :, -1, :])
    north_pad = select_rows(above, widened[:, :, :, 0, :])
    top_row = jnp.einsum('nl,nlcw->ncw', at_top, widened[:, :, :, -1, :].astype(jnp.float32), precision=lax.Precision.HIGHEST)
    mirrored = jnp.flip(top_row, axis=(0, 2))
    north_pad = north_pad + at_top[:, :, None, None] * mirrored[:, None]
    return jnp.concatenate([south_pad[:, :, :, None].astype(jnp.bfloat16), widened, north_pad[:, :, :, None].astype(jnp.bfloat16)], axis=3)

def pad_adjoint(pad_grads, lookups):
    west_match, east_match, below, above, at_top = lookups
    south_grads = pad_grads[:, :, :, 0, :]
    north_grads = pad_grads[:, :, :, -1, :]
    widened = pad_grads[:, :, :, 1:-1, :]
    top_row = jnp.einsum('nk,nkcw->ncw', at_top, north_grads, precision=lax.Precision.HIGHEST)
    crest_back = jnp.flip(top_row, axis=2).astype(jnp.bfloat16)
    returned = jnp.flip(crest_back, axis=0).astype(jnp.float32)
    upper_add = jnp.einsum('nkl,nkcw->nlcw', below, south_grads, precision=lax.Precision.HIGHEST)
    upper_add = upper_add + at_top[:, :, None, None] * returned[:, None]
    lower_add = jnp.einsum('nkl,nkcw->nlcw', above, north_grads, precision=lax.Precision.HIGHEST)
    widened = widened.at[:, :, :, -1, :].add(upper_add).at[:, :, :, 0, :].add(lower_add)
    west_back = widened[..., 0].astype(jnp.bfloat16)
    east_back = widened[..., -1].astype(jnp.bfloat16)
    from_left = jnp.roll(east_back, 1, axis=0)
    from_right = jnp.roll(west_back, -1, axis=0)
    interior = widened[..., 1:-1]
    interior = interior.at[..., 0].add(select_rows(west_match, from_left))
    interior = interior.at[..., -1].add(select_rows(east_match, from_right))
    return interior

def convolve(operand, kernel):
    return lax.conv_general_dilated(operand.astype(jnp.float32), kernel.astype(jnp.float32), (1, 1), 'VALID', precision=lax.Precision.HIGHEST)

def reference(fields, tile_rows, weights, bias, cotangent):
    lookups = make_lookups(tile_rows)
    occupied = (tile_rows >= 0)[:, :, None, None, None]
    shaped = weights.reshape(3, 3, C, C)
    kernel = shaped.transpose(2, 3, 0, 1)
    flipped = jnp.flip(shaped, (0, 1)).transpose(3, 2, 0, 1)
    results = []
    grads = []
    weight_total = jnp.zeros((9, C, C), jnp.float32)
    bias_total = jnp.zeros((C,), jnp.float32)
    tiles_all = N_TILES * SLOTS
    for sample in range(SAMPLES):
        inputs = jnp.where(occupied, fields[sample].reshape(N_TILES, SLOTS, C, TS, TS), 0).astype(jnp.bfloat16)
        padded = pad_tiles(inputs, lookups)
        flat_padded = padded.reshape(tiles_all, C, TS + 2, TS + 2)
        pre_act = convolve(flat_padded, kernel).reshape(N_TILES, SLOTS, C, TS, TS) + bias[None, None, :, None, None]
        result = jnp.where(occupied, inputs.astype(jnp.float32) + jax.nn.gelu(pre_act), 0).astype(jnp.bfloat16)
        upstream = jnp.where(occupied, cotangent[sample].reshape(N_TILES, SLOTS, C, TS, TS).astype(jnp.float32), 0.0)
        pullback = jax.vjp(jax.nn.gelu, pre_act)[1]
        slopes = pullback(upstream)[0].astype(jnp.bfloat16)
        flat_slopes = slopes.reshape(tiles_all, C, TS, TS)
        wide_slopes = jnp.pad(flat_slopes, ((0, 0), (0, 0), (2, 2), (2, 2)))
        pad_grads = convolve(wide_slopes, flipped).reshape(N_TILES, SLOTS, C, TS + 2, TS + 2)
        back = pad_adjoint(pad_grads, lookups)
        grad = jnp.where(occupied, upstream + back, 0.0).astype(jnp.bfloat16)
        results.append(result.reshape(tiles_all, C, TS * TS))
        grads.append(grad.reshape(tiles_all, C, TS * TS))
        slopes_wide = flat_slopes.astype(jnp.float32)
        tap_grads = []
        for row_shift in range(3):
            for col_shift in range(3):
                window = flat_padded[:, :, row_shift:row_shift + TS, col_shift:col_shift + TS].astype(jnp.float32)
                tap_grads.append(jnp.einsum('tcjk,tojk->oc', window, slopes_wide, precision=lax.Precision.HIGHEST))
        weight_total = weight_total + jnp.stack(tap_grads)
        bias_total = bias_total + lax.optimization_barrier(jnp.sum(slopes_wide, axis=(0, 2, 3)))
    grad_scale = 1.0 / math.sqrt(SAMPLES * N_TILES * SLOTS * TS * TS)
    return (jnp.stack(results), jnp.stack(grads), weight_total * grad_scale, bias_total * grad_scale)
```

```python
import math

import jax
import jax.numpy as jnp
from jax import lax
from jax.experimental import pallas as pl
from jax.experimental.pallas import tpu as pltpu
from jax.sharding import PartitionSpec as P

C = 128
TS = 16
SLOTS = 3
CELLS = TS * TS
FRAME = 384
EDGE = TS + 2
EAST = SLOTS * EDGE
FOLD = 2 * SLOTS * EDGE
F32 = jnp.float32
BF16 = jnp.bfloat16
GELU_C = math.sqrt(2.0 / math.pi)
GELU_K = 0.044715


def iota(shape, dim):
    return lax.broadcasted_iota(jnp.int32, shape, dim)


def halo_plans(count):
    if count == 4:
        return [
            (lambda d: (d + 1) % 4, ("west", "fold")),
            (lambda d: (d + 3) % 4, ("east", "fold")),
            (lambda d: (d + 2) % 4, ("corner_w", "corner_e")),
            (None, ("corner_w", "corner_e")),
        ]
    return [
        (lambda d: (d + 1) % count, ("west",)),
        (lambda d: (d + count - 1) % count, ("east",)),
        (lambda d: count - 1 - d, ("fold",)),
        (lambda d: (count - d) % count, ("corner_w",)),
        (lambda d: (2 * count - 2 - d) % count, ("corner_e",)),
    ]


def slot_of(rows, column, row):
    found = jnp.int32(-1)
    for k in range(SLOTS):
        found = jnp.where((rows[column, k] == row) & (row >= 0), k, found)
    return found


def halo_sources(rows, count, source, target, roles):
    lane = iota((8, 128), 1)
    top = 2 * SLOTS - 1
    src = jnp.full((8, 128), -1, jnp.int32)
    for role, base, near, here in (
        ("west", 0, TS - 1, (source + 1) % count),
        ("east", EAST, 0, (source + count - 1) % count),
    ):
        if role not in roles:
            continue
        for k in range(SLOTS):
            row = rows[target, k]
            row_here = jnp.where(target == here, row, -8)
            same = slot_of(rows, source, row_here)
            south = jnp.where(slot_of(rows, target, row_here - 1) >= 0, slot_of(rows, source, row_here - 1), -1)
            above = jnp.where(row_here >= 0, row_here + 1, -8)
            north = jnp.where(slot_of(rows, target, above) >= 0, slot_of(rows, source, above), -1)
            p = lane - (base + k * EDGE)
            mid = jnp.where(same >= 0, same * CELLS + near - TS, -CELLS * 8)
            src = jnp.where((p >= 1) & (p <= TS), jnp.maximum(mid + TS * p, -1), src)
            src = jnp.where(p == 0, jnp.where(south >= 0, south * CELLS + CELLS - TS + near, -1), src)
            src = jnp.where(p == TS + 1, jnp.where(north >= 0, north * CELLS + near, -1), src)
    mine = slot_of(rows, source, jnp.int32(top))
    theirs = slot_of(rows, target, jnp.int32(top))
    both = (mine >= 0) & (theirs >= 0)
    if "fold" in roles:
        ok = both & (target == count - 1 - source)
        c = lane - FOLD
        last = jnp.where(ok, mine * CELLS + CELLS - 1, -CELLS * 8)
        src = jnp.where((c >= 0) & (c < TS), jnp.maximum(last - c, -1), src)
    through = both & (slot_of(rows, count - 1 - target, jnp.int32(top)) >= 0)
    for role, base, near, here in (
        ("corner_w", 0, 0, (count - source) % count),
        ("corner_e", EAST, TS - 1, (2 * count - 2 - source) % count),
    ):
        if role not in roles:
            continue
        ok = through & (target == here)
        spot = jnp.where(ok, base + theirs * EDGE + TS + 1, -1)
        src = jnp.where(lane == spot, mine * CELLS + CELLS - TS + near, src)
    return src


def halo_map(rows, count, source, plan):
    route, roles = plan
    target = source if route is None else route(source)
    src = halo_sources(rows, count, source, target, roles)
    hits = iota((SLOTS * CELLS, 128), 0) == src[0:1, :]
    return jnp.where(hits, 1.0, 0.0).astype(BF16)


def dot(lhs, rhs, dims=((1,), (0,))):
    return lax.dot_general(lhs, rhs, (dims, ((), ())), preferred_element_type=F32)


def pack_kernel(rows, fields, weights, bias, cot, *outs, count):
    own = weights.shape[1]
    position = lax.axis_index("tiles")
    cells = jnp.concatenate([fields[0, k] for k in range(SLOTS)], axis=1)
    plans = halo_plans(count)
    for plan, out in zip(plans, outs[: len(plans)]):
        out[...] = dot(cells, halo_map(rows, count, position, plan)).astype(BF16)
    shared = outs[len(plans)]
    for t in range(9):
        shared[t * own : (t + 1) * own, :] = weights[t]
    at = 9 * own
    for k in range(SLOTS):
        for half in range(2):
            shared[at : at + own, :] = cot[0, k, :, half * 128 : half * 128 + 128]
            at += own
    line = jnp.concatenate([bias[...], jnp.zeros((1, 128 - own), F32)], axis=1)
    high = line.astype(BF16).astype(F32)
    middle = (line - high).astype(BF16).astype(F32)
    low = line - high - middle
    shared[at : at + 16, :] = jnp.concatenate([high, middle, low, jnp.zeros((13, 128), F32)], axis=0).astype(BF16)


def main_kernel(rows, fields, weights, bias, cot, *refs, count, n_halos, n_others, half_rows):
    halos = refs[:n_halos]
    others = refs[n_halos : n_halos + n_others]
    result, base, edges, keep, send, turned = refs[n_halos + n_others :]
    own = weights.shape[1]
    position = lax.axis_index("tiles")
    chan = lax.axis_index("chan")
    rep = lax.axis_index("rep")
    top = 2 * SLOTS - 1
    lane = iota((1, FRAME), 1)
    column = lane % TS
    lane128 = iota((1, 128), 1)

    row = [rows[position, k] for k in range(SLOTS)]
    full = [jnp.where(r >= 0, 1.0, 0.0).astype(F32) for r in row]
    at_top = [jnp.where(r == top, 1.0, 0.0).astype(F32) for r in row]
    above = [
        [jnp.where((row[k] >= 0) & (row[l] == row[k] + 1), 1.0, 0.0).astype(F32) for l in range(SLOTS)]
        for k in range(SLOTS)
    ]

    eye = iota((own, 128), 0) == iota((own, 128), 1)

    def column_of(line):
        return jnp.sum(jnp.where(eye, line, 0.0), axis=1, keepdims=True)

    parts = []
    line = jnp.concatenate([bias[...], jnp.zeros((1, 128 - own), F32)], axis=1)
    taps = [weights[t] for t in range(9)]
    cots = [cot[0, k].astype(F32) for k in range(SLOTS)]
    parts.append((taps, cots, column_of(line)))
    for ref in others:
        taps = [ref[t * own : (t + 1) * own, :] for t in range(9)]
        cots = []
        at = 9 * own
        for k in range(SLOTS):
            cots.append(jnp.concatenate([ref[at : at + own, :], ref[at + own : at + 2 * own, :]], axis=1).astype(F32))
            at += 2 * own
        pieces = ref[at : at + 16, :].astype(F32)
        parts.append((taps, cots, column_of(pieces[0:1] + pieces[1:2] + pieces[2:3])))
    kernels = [
        jnp.concatenate([jnp.concatenate(taps[3 * a : 3 * a + 3], axis=1) for a in range(3)], axis=0)
        for taps, _, _ in parts
    ]
    turned[...] = jnp.transpose(jnp.concatenate(kernels, axis=0).astype(F32)).astype(BF16)
    start = pl.multiple_of(chan * own, own)
    back_kernel = jnp.concatenate([turned[pl.ds(b * C + start, own), :] for b in range(3)], axis=0)

    halo = halos[0][...].astype(F32)
    for ref in halos[1:]:
        halo = halo + ref[...].astype(F32)
    p_at = iota((128, FRAME), 0)
    west_at = jnp.where(p_at == 0, FRAME - TS, TS * (p_at - 1))
    frame_lane = iota((128, FRAME), 1)
    spread_west = jnp.where((p_at < EDGE) & (frame_lane == west_at), 1.0, 0.0).astype(BF16)
    spread_east = jnp.where((p_at < EDGE) & (frame_lane == west_at + TS - 1), 1.0, 0.0).astype(BF16)

    tiles = [fields[0, k].astype(F32) * full[k] for k in range(SLOTS)]
    fold = pltpu.roll(halo, 128 - FOLD, 1)
    grads = jnp.zeros((3 * own, 3 * C), F32)
    slope_sum = jnp.zeros((own, CELLS), F32)
    edge_sum = jnp.zeros((own, 128), F32)
    pads = []
    for k in range(SLOTS):
        north = at_top[k] * fold
        south = jnp.zeros((C, 128), F32)
        for l in range(SLOTS):
            if l != k:
                north = north + above[k][l] * tiles[l][:, :128]
                south = south + above[l][k] * tiles[l][:, 128:]
        ends = jnp.where(lane128 < TS, north, jnp.where(lane128 >= 128 - TS, south, 0.0))
        centre = jnp.concatenate([tiles[k], ends], axis=1)
        west = dot(pltpu.roll(halo, (128 - k * EDGE) % 128, 1).astype(BF16), spread_west)
        east = dot(pltpu.roll(halo, (128 - EAST - k * EDGE) % 128, 1).astype(BF16), spread_east)
        left = jnp.where(column == 0, west, pltpu.roll(centre, 1, 1))
        right = jnp.where(column == TS - 1, east, pltpu.roll(centre, FRAME - 1, 1))
        window = jnp.concatenate([left, centre, right], axis=0).astype(BF16)
        frames = []
        for n, (taps, cots, bias_column) in enumerate(parts):
            sums = dot(kernels[n], window)
            pre = (
                pltpu.roll(sums[:own], TS, 1)[:, :CELLS]
                + sums[own : 2 * own, :CELLS]
                + pltpu.roll(sums[2 * own :], FRAME - TS, 1)[:, :CELLS]
                + bias_column
            )
            square = pre * pre
            tanh = jnp.tanh(GELU_C * (pre * (1.0 + GELU_K * square)))
            half = 0.5 * (1.0 + tanh)
            up = cots[k] * full[k]
            slope = half + 0.5 * pre * (1.0 - tanh * tanh) * (GELU_C * (1.0 + 3.0 * GELU_K * square))
            slopes = (up * slope).astype(BF16).astype(F32)
            if n == 0:
                own_in = fields[0, k, pl.ds(start, own), :].astype(F32)
                result[0, k] = (full[k] * (own_in + pre * half)).astype(BF16)
                slope_sum = slope_sum + slopes
            wide = jnp.concatenate([slopes, jnp.zeros((own, FRAME - CELLS), F32)], axis=1)
            frames.append(
                jnp.concatenate([pltpu.roll(wide, FRAME - TS, 1), wide, pltpu.roll(wide, TS, 1)], axis=0).astype(BF16)
            )
        grads = grads + dot(frames[0], window, ((1,), (1,)))
        spread = dot(back_kernel, jnp.concatenate(frames, axis=0))
        first, second, third = spread[:own], spread[own : 2 * own], spread[2 * own :]
        pad = (
            second
            + jnp.where(column < TS - 1, pltpu.roll(first, FRAME - 1, 1), 0.0)
            + jnp.where(column > 0, pltpu.roll(third, 1, 1), 0.0)
        )
        pads.append(pad)
        edge_sum = edge_sum + pltpu.roll(dot(first.astype(BF16), spread_west, ((1,), (1,))), k * EDGE, 1)
        edge_sum = edge_sum + pltpu.roll(dot(third.astype(BF16), spread_east, ((1,), (1,))), EAST + k * EDGE, 1)
        crest = jnp.where(lane128 < TS, pad[:, CELLS:], 0.0) * at_top[k]
        edge_sum = edge_sum + pltpu.roll(crest, FOLD, 1)
    edges[...] = edge_sum.astype(BF16)
    for k in range(SLOTS):
        first = pads[k][:, :128]
        second = pads[k][:, 128:CELLS]
        for l in range(SLOTS):
            if l != k:
                ends = pads[l][:, CELLS:]
                first = first + jnp.where(lane128 < TS, ends, 0.0) * above[l][k]
                second = second + jnp.where(lane128 >= 128 - TS, ends, 0.0) * above[k][l]
        base[k] = parts[0][1][k] * full[k] + jnp.concatenate([first, second], axis=1)
    blocks = [grads[a * own : (a + 1) * own, b * C : (b + 1) * C] for a in range(3) for b in range(3)]
    bias_line = jnp.sum(jnp.where(eye, jnp.sum(slope_sum, axis=1, keepdims=True), 0.0), axis=0, keepdims=True)
    blocks.append(bias_line)
    blocks.append(jnp.zeros((2 * half_rows - 9 * own - 1, 128), F32))
    sums = jnp.concatenate(blocks, axis=0)
    low, high = sums[:half_rows], sums[half_rows:]
    keep[...] = jnp.where(rep == 0, low, high)
    send[...] = jnp.where(rep == 0, high, low)


def finish_kernel(rows, base, *refs, count):
    out = refs[-1]
    position = lax.axis_index("tiles")
    total = None
    for plan, ref in zip(halo_plans(count), refs[:-1]):
        part = dot(ref[...], halo_map(rows, count, position, plan), ((1,), (1,)))
        total = part if total is None else total + part
    for k in range(SLOTS):
        out[0, k] = (base[k] + total[:, k * CELLS : (k + 1) * CELLS]).astype(BF16)


def gather_kernel(mine, theirs, weights_out, bias_out):
    rep = lax.axis_index("rep")
    own = weights_out.shape[1]
    low = jnp.where(rep == 0, mine[...], theirs[...])
    high = jnp.where(rep == 0, theirs[...], mine[...])
    sums = jnp.concatenate([low, high], axis=0)
    for t in range(9):
        weights_out[t] = sums[t * own : (t + 1) * own]
    bias_out[...] = sums[9 * own : 9 * own + 1, :own]


SMEM = pl.BlockSpec(memory_space=pltpu.SMEM)
VMEM = pl.BlockSpec(memory_space=pltpu.VMEM)


def call(kernel, n_in, outs, scratch=(), rows_first=True):
    return pl.pallas_call(
        kernel,
        in_specs=([SMEM] if rows_first else []) + [VMEM] * n_in,
        out_specs=[VMEM] * len(outs),
        out_shape=outs,
        scratch_shapes=list(scratch),
        compiler_params=pltpu.CompilerParams(vmem_limit_bytes=48 << 20),
    )


def struct(shape, dtype):
    return jax.ShapeDtypeStruct(shape, dtype)


def on_device(fields, tile_rows, weights, bias, cotangent):
    own = weights.shape[1]
    count = lax.axis_size("tiles")
    chans = lax.axis_size("chan")
    reps = lax.axis_size("rep")
    plans = halo_plans(count)
    shared_rows = 9 * own + 2 * SLOTS * own + 16
    half_rows = -(-(9 * own + 1) // 32) * 16
    bias_line = bias.reshape(1, own)

    packed = call(
        lambda *refs: pack_kernel(*refs, count=count),
        4,
        [struct((C, 128), BF16)] * len(plans) + [struct((shared_rows, 128), BF16)],
    )(tile_rows, fields, weights, bias_line, cotangent)
    halos = []
    for (route, _), message in zip(plans, packed):
        if route is None:
            halos.append(message)
        else:
            halos.append(lax.ppermute(message, "tiles", [(i, route(i)) for i in range(count)]))
    others = [
        lax.ppermute(packed[-1], "chan", [(i, (i + s) % chans) for i in range(chans)]) for s in range(1, chans)
    ]

    result, base, edges, keep, send = call(
        lambda *refs: main_kernel(
            *refs, count=count, n_halos=len(halos), n_others=len(others), half_rows=half_rows
        ),
        4 + len(halos) + len(others),
        [
            struct((1, SLOTS, own, CELLS), BF16),
            struct((SLOTS, own, CELLS), F32),
            struct((own, 128), BF16),
            struct((half_rows, 128), F32),
            struct((half_rows, 128), F32),
        ],
        [pltpu.VMEM((3 * C, 3 * C), BF16)],
    )(tile_rows, fields, weights, bias_line, cotangent, *halos, *others)

    returned = [
        edges if route is None else lax.ppermute(edges, "tiles", [(route(i), i) for i in range(count)])
        for route, _ in plans
    ]
    grad_fields = call(
        lambda *refs: finish_kernel(*refs, count=count),
        1 + len(returned),
        [struct((1, SLOTS, own, CELLS), BF16)],
    )(tile_rows, base, *returned)[0]

    sums = keep + lax.ppermute(send, "rep", [(0, 1), (1, 0)])
    stride = 1
    while stride < count:
        rounded = sums.astype(BF16)
        other = lax.ppermute(rounded, "tiles", [(i, i ^ stride) for i in range(count)])
        sums = rounded.astype(F32) + other.astype(F32)
        stride *= 2
    grad_scale = 1.0 / math.sqrt(reps * fields.shape[0] * count * SLOTS * CELLS)
    sums = sums * grad_scale
    grad_weights, grad_bias = call(
        gather_kernel,
        2,
        [struct((9, own, C), F32), struct((1, own), F32)],
        rows_first=False,
    )(sums, lax.ppermute(sums, "rep", [(0, 1), (1, 0)]))
    return (result, grad_fields, grad_weights, grad_bias.reshape(own))


def solution(mesh):
    in_specs = (
        P(("groups", "rep"), "tiles", None, None),
        P(),
        P(None, "chan", None),
        P("chan"),
        P(("groups", "rep"), "tiles", "chan", None),
    )
    out_specs = (
        P(("groups", "rep"), "tiles", "chan", None),
        P(("groups", "rep"), "tiles", "chan", None),
        P("groups", "chan", None),
        P(("groups", "chan")),
    )
    return jax.shard_map(
        on_device, mesh=mesh, in_specs=in_specs, out_specs=out_specs, check_vma=False
    )
```

```python
import math

import jax
import jax.numpy as jnp
from jax import lax
from jax.experimental import pallas as pl
from jax.experimental.pallas import tpu as pltpu
from jax.sharding import PartitionSpec as P

C = 128
TS = 16
SLOTS = 3
CELLS = TS * TS
FRAME = 384
EDGE = TS + 2
EAST = SLOTS * EDGE
FOLD = 2 * SLOTS * EDGE
F32 = jnp.float32
BF16 = jnp.bfloat16
GELU_C = math.sqrt(2.0 / math.pi)
GELU_K = 0.044715


def iota(shape, dim):
    return lax.broadcasted_iota(jnp.int32, shape, dim)


def halo_plans(count):
    if count == 4:
        return [
            (lambda d: (d + 1) % 4, ("west", "fold")),
            (lambda d: (d + 3) % 4, ("east", "fold")),
            (lambda d: (d + 2) % 4, ("corner_w", "corner_e")),
            (None, ("corner_w", "corner_e")),
        ]
    return [
        (lambda d: (d + 1) % count, ("west",)),
        (lambda d: (d + count - 1) % count, ("east",)),
        (lambda d: count - 1 - d, ("fold",)),
        (lambda d: (count - d) % count, ("corner_w",)),
        (lambda d: (2 * count - 2 - d) % count, ("corner_e",)),
    ]


def slot_of(rows, column, row):
    found = jnp.int32(-1)
    for k in range(SLOTS):
        found = jnp.where((rows[column, k] == row) & (row >= 0), k, found)
    return found


def halo_sources(rows, count, source, target, roles):
    lane = iota((8, 128), 1)
    top = 2 * SLOTS - 1
    src = jnp.full((8, 128), -1, jnp.int32)
    for role, base, near, here in (
        ("west", 0, TS - 1, (source + 1) % count),
        ("east", EAST, 0, (source + count - 1) % count),
    ):
        if role not in roles:
            continue
        for k in range(SLOTS):
            row = rows[target, k]
            row_here = jnp.where(target == here, row, -8)
            same = slot_of(rows, source, row_here)
            south = jnp.where(slot_of(rows, target, row_here - 1) >= 0, slot_of(rows, source, row_here - 1), -1)
            above = jnp.where(row_here >= 0, row_here + 1, -8)
            north = jnp.where(slot_of(rows, target, above) >= 0, slot_of(rows, source, above), -1)
            p = lane - (base + k * EDGE)
            mid = jnp.where(same >= 0, same * CELLS + near - TS, -CELLS * 8)
            src = jnp.where((p >= 1) & (p <= TS), jnp.maximum(mid + TS * p, -1), src)
            src = jnp.where(p == 0, jnp.where(south >= 0, south * CELLS + CELLS - TS + near, -1), src)
            src = jnp.where(p == TS + 1, jnp.where(north >= 0, north * CELLS + near, -1), src)
    mine = slot_of(rows, source, jnp.int32(top))
    theirs = slot_of(rows, target, jnp.int32(top))
    both = (mine >= 0) & (theirs >= 0)
    if "fold" in roles:
        ok = both & (target == count - 1 - source)
        c = lane - FOLD
        last = jnp.where(ok, mine * CELLS + CELLS - 1, -CELLS * 8)
        src = jnp.where((c >= 0) & (c < TS), jnp.maximum(last - c, -1), src)
    through = both & (slot_of(rows, count - 1 - target, jnp.int32(top)) >= 0)
    for role, base, near, here in (
        ("corner_w", 0, 0, (count - source) % count),
        ("corner_e", EAST, TS - 1, (2 * count - 2 - source) % count),
    ):
        if role not in roles:
            continue
        ok = through & (target == here)
        spot = jnp.where(ok, base + theirs * EDGE + TS + 1, -1)
        src = jnp.where(lane == spot, mine * CELLS + CELLS - TS + near, src)
    return src


def halo_map(rows, count, source, plan):
    route, roles = plan
    target = source if route is None else route(source)
    src = halo_sources(rows, count, source, target, roles)
    hits = iota((SLOTS * CELLS, 128), 0) == src[0:1, :]
    return jnp.where(hits, 1.0, 0.0).astype(BF16)


def dot(lhs, rhs, dims=((1,), (0,))):
    return lax.dot_general(lhs, rhs, (dims, ((), ())), preferred_element_type=F32)


def message_views(ref, own):
    taps = [ref.at[t * own : (t + 1) * own] for t in range(9)]
    base = 9 * own
    halves = [
        [ref.at[base + (2 * k + h) * own : base + (2 * k + h + 1) * own] for h in range(2)] for k in range(SLOTS)
    ]
    at = base + 2 * SLOTS * own
    return taps, halves, ref.at[at : at + 16]


def pack_kernel(rows_hbm, fields_hbm, weights_hbm, bias_hbm, cot_hbm, *refs, count):
    n = len(halo_plans(count))
    rows_out, fields_out, shared = refs[:3]
    outs = refs[3 : 3 + n]
    maps = refs[3 + n : 3 + 2 * n]
    rows, bias, sem = refs[3 + 2 * n :]
    own = weights_hbm.shape[1]
    taps, halves, pieces = message_views(shared, own)
    get_rows = pltpu.make_async_copy(rows_hbm, rows, sem.at[0])
    get_rows.start()
    get_fields = pltpu.make_async_copy(fields_hbm.at[0], fields_out, sem.at[1])
    get_fields.start()
    get_bias = pltpu.make_async_copy(bias_hbm, bias, sem.at[2])
    get_bias.start()
    more = [pltpu.make_async_copy(weights_hbm.at[t], taps[t], sem.at[3 + t]) for t in range(9)]
    for k in range(SLOTS):
        for h in range(2):
            source = cot_hbm.at[0, k, :, h * 128 : h * 128 + 128]
            more.append(pltpu.make_async_copy(source, halves[k][h], sem.at[12 + 2 * k + h]))
    for copy in more:
        copy.start()
    get_rows.wait()
    position = lax.axis_index("tiles")
    plans = halo_plans(count)
    for plan, out in zip(plans, maps):
        out[...] = halo_map(rows, count, position, plan)
    put_rows = pltpu.make_async_copy(rows, rows_out, sem.at[0])
    put_rows.start()
    get_fields.wait()
    cells = jnp.concatenate([fields_out[k] for k in range(SLOTS)], axis=1)
    for out, hits in zip(outs, maps):
        out[...] = dot(cells, hits[...]).astype(BF16)
    get_bias.wait()
    line = jnp.concatenate([bias[...], jnp.zeros((1, 128 - own), F32)], axis=1)
    high = line.astype(BF16).astype(F32)
    middle = (line - high).astype(BF16).astype(F32)
    low = line - high - middle
    pieces[...] = jnp.concatenate([high, middle, low, jnp.zeros((13, 128), F32)], axis=0).astype(BF16)
    for copy in more:
        copy.wait()
    put_rows.wait()


def flag(condition):
    return jnp.where(condition, 1.0, 0.0).astype(F32)


def slot_flags(rows):
    position = lax.axis_index("tiles")
    row = [rows[position, k] for k in range(SLOTS)]
    full = [flag(r >= 0) for r in row]
    at_top = [flag(r == 2 * SLOTS - 1) for r in row]
    above = [[flag((row[k] >= 0) & (row[l] == row[k] + 1)) for l in range(SLOTS)] for k in range(SLOTS)]
    return full, at_top, above


def window_kernel(rows, fields, shared, windows, spreads, kernel):
    own = kernel.shape[0] // 3
    full, _, above = slot_flags(rows)
    column = iota((1, FRAME), 1) % TS
    lane128 = iota((1, 128), 1)
    tiles = [fields[k].astype(F32) * full[k] for k in range(SLOTS)]
    for k in range(SLOTS):
        north = jnp.zeros((C, 128), F32)
        south = jnp.zeros((C, 128), F32)
        for l in range(SLOTS):
            if l != k:
                north = north + above[k][l] * tiles[l][:, :128]
                south = south + above[l][k] * tiles[l][:, 128:]
        ends = jnp.where(lane128 < TS, north, jnp.where(lane128 >= 128 - TS, south, 0.0))
        centre = jnp.concatenate([tiles[k], ends], axis=1)
        windows[k, :C] = jnp.where(column == 0, 0.0, pltpu.roll(centre, 1, 1)).astype(BF16)
        windows[k, C : 2 * C] = centre.astype(BF16)
        windows[k, 2 * C :] = jnp.where(column == TS - 1, 0.0, pltpu.roll(centre, FRAME - 1, 1)).astype(BF16)
    p_at = iota((128, FRAME), 0)
    frame_lane = iota((128, FRAME), 1)
    for side in range(2):
        for k in range(SLOTS):
            p = p_at - (side * EAST + k * EDGE)
            spot = jnp.where(p == 0, FRAME - TS, TS * (p - 1)) + side * (TS - 1)
            hits = (p >= 0) & (p < EDGE) & (frame_lane == spot)
            spreads[side, k] = jnp.where(hits, 1.0, 0.0).astype(BF16)
    taps, _, _ = message_views(shared, own)
    for a in range(3):
        for b in range(3):
            kernel[a * own : (a + 1) * own, b * C : (b + 1) * C] = taps[3 * a + b][...]


def column_of(pieces, own):
    eye = iota((own, 128), 0) == iota((own, 128), 1)
    parts = pieces[...].astype(F32)
    line = parts[0:1] + parts[1:2] + parts[2:3]
    return jnp.sum(jnp.where(eye, line, 0.0), axis=1, keepdims=True)


def activation(kernel, window, bias_column, up):
    own = bias_column.shape[0]
    sums = dot(kernel, window)
    pre = (
        pltpu.roll(sums[:own], TS, 1)[:, :CELLS]
        + sums[own : 2 * own, :CELLS]
        + pltpu.roll(sums[2 * own :], FRAME - TS, 1)[:, :CELLS]
        + bias_column
    )
    square = pre * pre
    tanh = jnp.tanh(GELU_C * (pre * (1.0 + GELU_K * square)))
    half = 0.5 + 0.5 * tanh
    slope = half + (0.5 * pre) * (1.0 - tanh * tanh) * (GELU_C + (3.0 * GELU_C * GELU_K) * square)
    return pre * half, (up * slope).astype(BF16).astype(F32)


def frame_of(slopes):
    own = slopes.shape[0]
    wide = jnp.concatenate([slopes, jnp.zeros((own, FRAME - CELLS), F32)], axis=1)
    return jnp.concatenate([pltpu.roll(wide, FRAME - TS, 1), wide, pltpu.roll(wide, TS, 1)], axis=0).astype(BF16)


def upstream_of(halves, k, full):
    return jnp.concatenate([halves[k][0][...], halves[k][1][...]], axis=1).astype(F32) * full[k]


def forward_kernel(rows, fields, shared, kernel, spreads, windows, *refs, n_halos, half_rows):
    halos = refs[:n_halos]
    full_windows, frames, result, keep, send = refs[n_halos:]
    own = kernel.shape[0] // 3
    full, at_top, _ = slot_flags(rows)
    start = pl.multiple_of(lax.axis_index("chan") * own, own)
    rep = lax.axis_index("rep")
    lane128 = iota((1, 128), 1)
    _, halves, pieces = message_views(shared, own)
    bias_column = column_of(pieces, own)
    halo = halos[0][...].astype(F32)
    for ref in halos[1:]:
        halo = halo + ref[...].astype(F32)
    turned = pltpu.roll(halo, 128 - FOLD, 1)
    fold = jnp.where(lane128 < TS, turned, 0.0)
    fold_left = jnp.where((lane128 > 0) & (lane128 < TS), pltpu.roll(turned, 1, 1), 0.0)
    fold_right = jnp.where(lane128 < TS - 1, pltpu.roll(turned, 127, 1), 0.0)
    halo = halo.astype(BF16)
    grads = jnp.zeros((3 * own, 3 * C), F32)
    slope_sum = jnp.zeros((own, CELLS), F32)
    for k in range(SLOTS):
        west = dot(halo, spreads[0, k])
        east = dot(halo, spreads[1, k])
        rest = jnp.zeros((C, CELLS), F32)
        left = windows[k, :C] + (west + jnp.concatenate([rest, at_top[k] * fold_left], axis=1)).astype(BF16)
        right = windows[k, 2 * C :] + (east + jnp.concatenate([rest, at_top[k] * fold_right], axis=1)).astype(BF16)
        centre = windows[k, C : 2 * C] + jnp.concatenate([rest, at_top[k] * fold], axis=1).astype(BF16)
        window = jnp.concatenate([left, centre, right], axis=0)
        full_windows[k] = window
        up = upstream_of(halves, k, full)
        gelu, slopes = activation(kernel[...], window, bias_column, up)
        result[k] = (full[k] * (fields[k, pl.ds(start, own), :].astype(F32) + gelu)).astype(BF16)
        slope_sum = slope_sum + slopes
        frame = frame_of(slopes)
        frames[k] = frame
        grads = grads + dot(frame, window, ((1,), (1,)))
    blocks = [grads[a * own : (a + 1) * own, b * C : (b + 1) * C] for a in range(3) for b in range(3)]
    eye = iota((own, 128), 0) == iota((own, 128), 1)
    bias_line = jnp.sum(jnp.where(eye, jnp.sum(slope_sum, axis=1, keepdims=True), 0.0), axis=0, keepdims=True)
    blocks.append(bias_line)
    blocks.append(jnp.zeros((2 * half_rows - 9 * own - 1, 128), F32))
    sums = jnp.concatenate(blocks, axis=0)
    low, high = sums[:half_rows], sums[half_rows:]
    keep[...] = jnp.where(rep == 0, low, high)
    send[...] = jnp.where(rep == 0, high, low)


def backward_kernel(rows, shared, kernel, spreads, windows, frames, result, *refs, n_others):
    others = refs[:n_others]
    base, edges, result_out, turned, sem = refs[n_others:]
    own = kernel.shape[0] // 3
    put = pltpu.make_async_copy(result, result_out.at[0], sem)
    put.start()
    full, at_top, above = slot_flags(rows)
    start = pl.multiple_of(lax.axis_index("chan") * own, own)
    column = iota((1, FRAME), 1) % TS
    lane128 = iota((1, 128), 1)
    kernels = [kernel[...]]
    columns, ups = [], []
    for ref in others:
        taps, halves, pieces = message_views(ref, own)
        kernels.append(
            jnp.concatenate(
                [jnp.concatenate([taps[3 * a + b][...] for b in range(3)], axis=1) for a in range(3)], axis=0
            )
        )
        columns.append(column_of(pieces, own))
        ups.append(halves)
    turned[...] = jnp.transpose(jnp.concatenate(kernels, axis=0).astype(F32)).astype(BF16)
    back_kernel = jnp.concatenate([turned[pl.ds(b * C + start, own), :] for b in range(3)], axis=0)
    edge_sum = jnp.zeros((own, 128), F32)
    pads = []
    for k in range(SLOTS):
        stack = [frames[k]]
        for other_kernel, bias_column, halves in zip(kernels[1:], columns, ups):
            _, slopes = activation(other_kernel, windows[k], bias_column, upstream_of(halves, k, full))
            stack.append(frame_of(slopes))
        spread = dot(back_kernel, jnp.concatenate(stack, axis=0))
        first, second, third = spread[:own], spread[own : 2 * own], spread[2 * own :]
        pad = (
            second
            + jnp.where(column < TS - 1, pltpu.roll(first, FRAME - 1, 1), 0.0)
            + jnp.where(column > 0, pltpu.roll(third, 1, 1), 0.0)
        )
        pads.append(pad)
        edge_sum = edge_sum + dot(first.astype(BF16), spreads[0, k], ((1,), (1,)))
        edge_sum = edge_sum + dot(third.astype(BF16), spreads[1, k], ((1,), (1,)))
        crest = jnp.where(lane128 < TS, pad[:, CELLS:], 0.0) * at_top[k]
        edge_sum = edge_sum + pltpu.roll(crest, FOLD, 1)
    edges[...] = edge_sum.astype(BF16)
    _, halves, _ = message_views(shared, own)
    for k in range(SLOTS):
        first = pads[k][:, :128]
        second = pads[k][:, 128:CELLS]
        for l in range(SLOTS):
            if l != k:
                ends = pads[l][:, CELLS:]
                first = first + jnp.where(lane128 < TS, ends, 0.0) * above[l][k]
                second = second + jnp.where(lane128 >= 128 - TS, ends, 0.0) * above[k][l]
        base[k] = upstream_of(halves, k, full) + jnp.concatenate([first, second], axis=1)
    put.wait()


def finish_kernel(base, *refs):
    out = refs[-1]
    n = len(refs) // 2
    total = None
    for received, hits in zip(refs[:n], refs[n:]):
        part = dot(received[...], hits[...], ((1,), (1,)))
        total = part if total is None else total + part
    for k in range(SLOTS):
        out[0, k] = (base[k] + total[:, k * CELLS : (k + 1) * CELLS]).astype(BF16)


def gather_kernel(mine, theirs, weights_out, bias_out):
    rep = lax.axis_index("rep")
    own = weights_out.shape[1]
    low = jnp.where(rep == 0, mine[...], theirs[...])
    high = jnp.where(rep == 0, theirs[...], mine[...])
    sums = jnp.concatenate([low, high], axis=0)
    for t in range(9):
        weights_out[t] = sums[t * own : (t + 1) * own]
    bias_out[...] = sums[9 * own : 9 * own + 1, :own]


SMEM = pl.BlockSpec(memory_space=pltpu.SMEM)
VMEM = pl.BlockSpec(memory_space=pltpu.VMEM)
HBM = pl.BlockSpec(memory_space=pltpu.HBM)


def call(kernel, specs, outs, scratch=(), out_specs=None, cost=None):
    return pl.pallas_call(
        kernel,
        in_specs=specs,
        out_specs=out_specs or [VMEM] * len(outs),
        out_shape=outs,
        scratch_shapes=list(scratch),
        cost_estimate=cost,
        compiler_params=pltpu.CompilerParams(vmem_limit_bytes=40 << 20),
    )


def struct(shape, dtype):
    return jax.ShapeDtypeStruct(shape, dtype)


def on_device(fields, tile_rows, weights, bias, cotangent):
    own = weights.shape[1]
    count = lax.axis_size("tiles")
    chans = lax.axis_size("chan")
    reps = lax.axis_size("rep")
    plans = halo_plans(count)
    n = len(plans)
    shared_rows = 9 * own + 2 * SLOTS * own + 16
    half_rows = -(-(9 * own + 1) // 32) * 16
    swap = [(0, 1), (1, 0)]

    rows, tiles, shared, *packed = call(
        lambda *refs: pack_kernel(*refs, count=count),
        [HBM] * 5,
        [struct(tile_rows.shape, jnp.int32), struct((SLOTS, C, CELLS), BF16), struct((shared_rows, 128), BF16)]
        + [struct((C, 128), BF16)] * n
        + [struct((SLOTS * CELLS, 128), BF16)] * n,
        [
            pltpu.SMEM(tile_rows.shape, jnp.int32),
            pltpu.VMEM((1, own), F32),
            pltpu.SemaphoreType.DMA((12 + 2 * SLOTS,)),
        ],
    )(*(pltpu.with_memory_space_constraint(x, pltpu.HBM) for x in (tile_rows, fields, weights, bias.reshape(1, own), cotangent)))
    messages, maps = packed[:n], packed[n:]
    halos = []
    for (route, _), message in zip(plans, messages):
        if route is None:
            halos.append(message)
        else:
            halos.append(lax.ppermute(message, "tiles", [(i, route(i)) for i in range(count)]))
    others = [lax.ppermute(shared, "chan", [(i, (i + s) % chans) for i in range(chans)]) for s in range(1, chans)]

    windows, spreads, kernel = call(
        window_kernel,
        [SMEM, VMEM, VMEM],
        [
            struct((SLOTS, 3 * C, FRAME), BF16),
            struct((2, SLOTS, 128, FRAME), BF16),
            struct((3 * own, 3 * C), BF16),
        ],
    )(rows, tiles, shared)

    windows, frames, result, keep, send = call(
        lambda *refs: forward_kernel(*refs, n_halos=n, half_rows=half_rows),
        [SMEM] + [VMEM] * (5 + n),
        [
            struct((SLOTS, 3 * C, FRAME), BF16),
            struct((SLOTS, 3 * own, FRAME), BF16),
            struct((SLOTS, own, CELLS), BF16),
            struct((half_rows, 128), F32),
            struct((half_rows, 128), F32),
        ],
    )(rows, tiles, shared, kernel, spreads, windows, *halos)

    send, others = lax.optimization_barrier((send, others))
    sums = keep + lax.ppermute(send, "rep", swap)
    rounded = sums.astype(BF16)
    frames, rounded = lax.optimization_barrier((frames, rounded))

    base, edges, result = call(
        lambda *refs: backward_kernel(*refs, n_others=len(others)),
        [SMEM] + [VMEM] * (6 + len(others)),
        [
            struct((SLOTS, own, CELLS), F32),
            struct((own, 128), BF16),
            struct((1, SLOTS, own, CELLS), BF16),
        ],
        [pltpu.VMEM((3 * C, 3 * own * chans), BF16), pltpu.SemaphoreType.DMA],
        out_specs=[VMEM, VMEM, HBM],
    )(rows, shared, kernel, spreads, windows, frames, result, *others)

    stride = 1
    while stride < count:
        other = lax.ppermute(rounded, "tiles", [(i, i ^ stride) for i in range(count)])
        sums = rounded.astype(F32) + other.astype(F32)
        rounded = sums.astype(BF16)
        if stride == 1:
            rounded, edges = lax.optimization_barrier((rounded, edges))
        stride *= 2
    grad_scale = 1.0 / math.sqrt(reps * fields.shape[0] * count * SLOTS * CELLS)
    sums = sums * grad_scale
    returned = [
        edges if route is None else lax.ppermute(edges, "tiles", [(route(i), i) for i in range(count)])
        for route, _ in plans
    ]
    sums, returned = lax.optimization_barrier((sums, returned))
    grad_fields = call(
        finish_kernel,
        [VMEM] * (1 + 2 * n),
        [struct((1, SLOTS, own, CELLS), BF16)],
    )(base, *returned, *maps)[0]
    grad_weights, grad_bias = call(
        gather_kernel,
        [VMEM, VMEM],
        [struct((9, own, C), F32), struct((1, own), F32)],
    )(sums, lax.ppermute(sums, "rep", swap))
    return (result, grad_fields, grad_weights, grad_bias.reshape(own))


def solution(mesh):
    in_specs = (
        P(("groups", "rep"), "tiles", None, None),
        P(),
        P(None, "chan", None),
        P("chan"),
        P(("groups", "rep"), "tiles", "chan", None),
    )
    out_specs = (
        P(("groups", "rep"), "tiles", "chan", None),
        P(("groups", "rep"), "tiles", "chan", None),
        P("groups", "chan", None),
        P(("groups", "chan")),
    )
    return jax.shard_map(
        on_device, mesh=mesh, in_specs=in_specs, out_specs=out_specs, check_vma=False
    )
```

```python
import math

import jax
import jax.numpy as jnp
from jax import lax
from jax.experimental import pallas as pl
from jax.experimental.pallas import tpu as pltpu
from jax.sharding import PartitionSpec as P

C = 128
TS = 16
SLOTS = 3
CELLS = TS * TS
FRAME = 384
EDGE = TS + 2
EAST = SLOTS * EDGE
FOLD = 2 * SLOTS * EDGE
F32 = jnp.float32
BF16 = jnp.bfloat16
GELU_C = math.sqrt(2.0 / math.pi)
GELU_K = 0.044715


def iota(shape, dim):
    return lax.broadcasted_iota(jnp.int32, shape, dim)


def halo_plans(count):
    if count == 4:
        return [
            (lambda d: 3 - d, ("side", "fold")),
            (lambda d: d ^ 2, ("corner",)),
            (lambda d: d ^ 1, ("side",)),
            (None, ("corner",)),
        ]
    return [
        (lambda d: (d + 1) % count, ("west",)),
        (lambda d: (d + count - 1) % count, ("east",)),
        (lambda d: count - 1 - d, ("fold",)),
        (lambda d: (count - d) % count, ("corner_west",)),
        (lambda d: (2 * count - 2 - d) % count, ("corner_east",)),
    ]


def sum_routes(count):
    if count == 4:
        return [lambda d: d ^ 1, lambda d: 3 - d]
    return [lambda d, s=1 << i: d ^ s for i in range(count.bit_length() - 1)]


def halo_sources(rows, count, source, target, roles):
    lane = iota((8, 128), 1)
    top = 2 * SLOTS - 1
    east = (lane >= EAST) & (lane < FOLD)
    at = lane - jnp.where(east, EAST, 0)
    k = jnp.where(at >= EDGE, 1, 0) + jnp.where(at >= 2 * EDGE, 1, 0)
    p = at - EDGE * k
    rim = lane < FOLD
    row = jnp.where(k == 0, rows[target, 0], jnp.where(k == 1, rows[target, 1], rows[target, 2]))
    row = jnp.where(rim, row, -1)
    src = jnp.full((8, 128), -1, jnp.int32)
    sides = [name for name in ("west", "east") if name in roles or "side" in roles]
    if sides:
        wanted = row + jnp.where(p == TS + 1, 1, 0) - jnp.where(p == 0, 1, 0)
        slot = jnp.full((8, 128), -1, jnp.int32)
        present = (p > 0) & (p <= TS)
        for l in range(SLOTS):
            slot = jnp.where(wanted == rows[source, l], l, slot)
            present = present | (wanted == rows[target, l])
        cell = jnp.where(p == 0, CELLS - TS, jnp.where(p == TS + 1, 0, TS * (p - 1))) + jnp.where(east, 0, TS - 1)
        good = present & (row >= 0) & (wanted >= 0) & (slot >= 0)
        from_west = target == (source + 1) % count if "west" in sides else False
        from_east = target == (source + count - 1) % count if "east" in sides else False
        good = good & ((jnp.logical_not(east) & from_west) | (east & from_east))
        src = jnp.where(good, slot * CELLS + cell, src)

    def top_slot(column):
        found = jnp.int32(-1)
        for l in range(SLOTS):
            found = jnp.where(rows[column, l] == top, l, found)
        return found

    if sides and len(sides) == len(roles) and "side" not in roles or roles == ("side",):
        return src
    mine = top_slot(source)
    if "fold" in roles:
        good = (lane >= FOLD) & (lane < FOLD + TS) & (mine >= 0) & (target == count - 1 - source)
        src = jnp.where(good, mine * CELLS + (CELLS - 1 + FOLD) - lane, src)
    corners = [name for name in ("west", "east") if "corner" in roles or f"corner_{name}" in roles]
    if corners:
        good = (row == top) & (p == TS + 1) & (mine >= 0) & (top_slot(count - 1 - target) >= 0)
        from_west = target == (count - source) % count if "west" in corners else False
        from_east = target == (2 * count - 2 - source) % count if "east" in corners else False
        good = good & ((jnp.logical_not(east) & from_west) | (east & from_east))
        src = jnp.where(good, mine * CELLS + CELLS - TS + jnp.where(east, TS - 1, 0), src)
    return src


def halo_map(rows, count, source, plan):
    route, roles = plan
    target = source if route is None else route(source)
    src = halo_sources(rows, count, source, target, roles)
    hits = iota((SLOTS * CELLS, 128), 0) == src[0:1, :]
    return jnp.where(hits, 1.0, 0.0).astype(BF16)


def dot(lhs, rhs, dims=((1,), (0,))):
    return lax.dot_general(lhs, rhs, (dims, ((), ())), preferred_element_type=F32)


def message_views(ref, own):
    taps = [ref.at[t * own : (t + 1) * own] for t in range(9)]
    base = 9 * own
    halves = [
        [ref.at[base + (2 * k + h) * own : base + (2 * k + h + 1) * own] for h in range(2)] for k in range(SLOTS)
    ]
    at = base + 2 * SLOTS * own
    return taps, halves, ref.at[at : at + 16]


def pack_kernel(rows_hbm, fields_hbm, *refs, count):
    n = len(halo_plans(count))
    rows_out, fields_out = refs[:2]
    outs = refs[2 : 2 + n]
    maps = refs[2 + n : 2 + 2 * n]
    rows, sem = refs[2 + 2 * n :]
    get_rows = pltpu.make_async_copy(rows_hbm, rows, sem.at[0])
    get_rows.start()
    get_fields = pltpu.make_async_copy(fields_hbm.at[0], fields_out, sem.at[1])
    get_fields.start()
    get_rows.wait()
    position = lax.axis_index("tiles")
    plans = halo_plans(count)
    for plan, out in zip(plans, maps):
        out[...] = halo_map(rows, count, position, plan)
    put_rows = pltpu.make_async_copy(rows, rows_out, sem.at[0])
    put_rows.start()
    get_fields.wait()
    cells = jnp.concatenate([fields_out[k] for k in range(SLOTS)], axis=1)
    for out, hits in zip(outs, maps):
        out[...] = dot(cells, hits[...]).astype(BF16)
    put_rows.wait()


def flag(condition):
    return jnp.where(condition, 1.0, 0.0).astype(F32)


def slot_flags(rows):
    position = lax.axis_index("tiles")
    row = [rows[position, k] for k in range(SLOTS)]
    full = [flag(r >= 0) for r in row]
    at_top = [flag(r == 2 * SLOTS - 1) for r in row]
    above = [[flag((row[k] >= 0) & (row[l] == row[k] + 1)) for l in range(SLOTS)] for k in range(SLOTS)]
    return full, at_top, above


def window_kernel(rows, fields, weights_hbm, bias_hbm, cot_hbm, windows, spreads, kernel, shared, bias, sem):
    own = kernel.shape[0] // 3
    taps, halves, pieces = message_views(shared, own)
    get_bias = pltpu.make_async_copy(bias_hbm, bias, sem.at[0])
    get_bias.start()
    more = [pltpu.make_async_copy(weights_hbm.at[t], taps[t], sem.at[1 + t]) for t in range(9)]
    for k in range(SLOTS):
        for h in range(2):
            source = cot_hbm.at[0, k, :, h * 128 : h * 128 + 128]
            more.append(pltpu.make_async_copy(source, halves[k][h], sem.at[10 + 2 * k + h]))
    for copy in more:
        copy.start()
    full, _, above = slot_flags(rows)
    column = iota((1, FRAME), 1) % TS
    lane128 = iota((1, 128), 1)
    tiles = [fields[k].astype(F32) * full[k] for k in range(SLOTS)]
    for k in range(SLOTS):
        north = jnp.zeros((C, 128), F32)
        south = jnp.zeros((C, 128), F32)
        for l in range(SLOTS):
            if l != k:
                north = north + above[k][l] * tiles[l][:, :128]
                south = south + above[l][k] * tiles[l][:, 128:]
        ends = jnp.where(lane128 < TS, north, jnp.where(lane128 >= 128 - TS, south, 0.0))
        centre = jnp.concatenate([tiles[k], ends], axis=1)
        windows[k, :C] = jnp.where(column == 0, 0.0, pltpu.roll(centre, 1, 1)).astype(BF16)
        windows[k, C : 2 * C] = centre.astype(BF16)
        windows[k, 2 * C :] = jnp.where(column == TS - 1, 0.0, pltpu.roll(centre, FRAME - 1, 1)).astype(BF16)
    p_at = iota((128, FRAME), 0)
    frame_lane = iota((128, FRAME), 1)
    for side in range(2):
        for k in range(SLOTS):
            p = p_at - (side * EAST + k * EDGE)
            spot = jnp.where(p == 0, FRAME - TS, TS * (p - 1)) + side * (TS - 1)
            hits = (p >= 0) & (p < EDGE) & (frame_lane == spot)
            spreads[side, k] = jnp.where(hits, 1.0, 0.0).astype(BF16)
    get_bias.wait()
    line = jnp.concatenate([bias[...], jnp.zeros((1, 128 - own), F32)], axis=1)
    high = line.astype(BF16).astype(F32)
    middle = (line - high).astype(BF16).astype(F32)
    low = line - high - middle
    pieces[...] = jnp.concatenate([high, middle, low, jnp.zeros((13, 128), F32)], axis=0).astype(BF16)
    for copy in more:
        copy.wait()
    for a in range(3):
        for b in range(3):
            kernel[a * own : (a + 1) * own, b * C : (b + 1) * C] = taps[3 * a + b][...]


def column_of(pieces, own):
    eye = iota((own, 128), 0) == iota((own, 128), 1)
    parts = pieces[...].astype(F32)
    line = parts[0:1] + parts[1:2] + parts[2:3]
    return jnp.sum(jnp.where(eye, line, 0.0), axis=1, keepdims=True)


def activation(kernel, window, bias_column, up):
    own = bias_column.shape[0]
    sums = dot(kernel, window)
    pre = (
        pltpu.roll(sums[:own], TS, 1)[:, :CELLS]
        + sums[own : 2 * own, :CELLS]
        + pltpu.roll(sums[2 * own :], FRAME - TS, 1)[:, :CELLS]
        + bias_column
    )
    square = pre * pre
    tanh = jnp.tanh(GELU_C * (pre * (1.0 + GELU_K * square)))
    half = 0.5 + 0.5 * tanh
    slope = half + (0.5 * pre) * (1.0 - tanh * tanh) * (GELU_C + (3.0 * GELU_C * GELU_K) * square)
    return pre * half, (up * slope).astype(BF16).astype(F32)


def frame_of(slopes):
    own = slopes.shape[0]
    wide = jnp.concatenate([slopes, jnp.zeros((own, FRAME - CELLS), F32)], axis=1)
    return jnp.concatenate([pltpu.roll(wide, FRAME - TS, 1), wide, pltpu.roll(wide, TS, 1)], axis=0).astype(BF16)


def upstream_of(halves, k, full):
    return jnp.concatenate([halves[k][0][...], halves[k][1][...]], axis=1).astype(F32) * full[k]


def forward_kernel(rows, fields, shared, kernel, spreads, windows, *refs, n_halos, half_rows):
    halos = refs[:n_halos]
    full_windows, frames, result, keep, send = refs[n_halos:]
    own = kernel.shape[0] // 3
    full, at_top, _ = slot_flags(rows)
    start = pl.multiple_of(lax.axis_index("chan") * own, own)
    rep = lax.axis_index("rep")
    lane128 = iota((1, 128), 1)
    _, halves, pieces = message_views(shared, own)
    bias_column = column_of(pieces, own)
    halo = halos[0][...].astype(F32)
    for ref in halos[1:]:
        halo = halo + ref[...].astype(F32)
    turned = pltpu.roll(halo, 128 - FOLD, 1)
    fold = jnp.where(lane128 < TS, turned, 0.0)
    fold_left = jnp.where((lane128 > 0) & (lane128 < TS), pltpu.roll(turned, 1, 1), 0.0)
    fold_right = jnp.where(lane128 < TS - 1, pltpu.roll(turned, 127, 1), 0.0)
    halo = halo.astype(BF16)
    grads = jnp.zeros((3 * own, 3 * C), F32)
    slope_sum = jnp.zeros((own, CELLS), F32)
    for k in range(SLOTS):
        west = dot(halo, spreads[0, k])
        east = dot(halo, spreads[1, k])
        rest = jnp.zeros((C, CELLS), F32)
        left = windows[k, :C] + (west + jnp.concatenate([rest, at_top[k] * fold_left], axis=1)).astype(BF16)
        right = windows[k, 2 * C :] + (east + jnp.concatenate([rest, at_top[k] * fold_right], axis=1)).astype(BF16)
        centre = windows[k, C : 2 * C] + jnp.concatenate([rest, at_top[k] * fold], axis=1).astype(BF16)
        window = jnp.concatenate([left, centre, right], axis=0)
        full_windows[k] = window
        up = upstream_of(halves, k, full)
        gelu, slopes = activation(kernel[...], window, bias_column, up)
        result[k] = (full[k] * (fields[k, pl.ds(start, own), :].astype(F32) + gelu)).astype(BF16)
        slope_sum = slope_sum + slopes
        frame = frame_of(slopes)
        frames[k] = frame
        grads = grads + dot(frame, window, ((1,), (1,)))
    blocks = [grads[a * own : (a + 1) * own, b * C : (b + 1) * C] for a in range(3) for b in range(3)]
    eye = iota((own, 128), 0) == iota((own, 128), 1)
    bias_line = jnp.sum(jnp.where(eye, jnp.sum(slope_sum, axis=1, keepdims=True), 0.0), axis=0, keepdims=True)
    blocks.append(bias_line)
    blocks.append(jnp.zeros((2 * half_rows - 9 * own - 1, 128), F32))
    sums = jnp.concatenate(blocks, axis=0)
    low, high = sums[:half_rows], sums[half_rows:]
    keep[...] = jnp.where(rep == 0, low, high)
    send[...] = jnp.where(rep == 0, high, low)


def backward_kernel(rows, shared, kernel, spreads, windows, frames, result, *refs, n_others):
    others = refs[:n_others]
    base, edges, result_out, turned, sem = refs[n_others:]
    own = kernel.shape[0] // 3
    put = pltpu.make_async_copy(result, result_out.at[0], sem)
    put.start()
    full, at_top, above = slot_flags(rows)
    start = pl.multiple_of(lax.axis_index("chan") * own, own)
    column = iota((1, FRAME), 1) % TS
    lane128 = iota((1, 128), 1)
    kernels = [kernel[...]]
    columns, ups = [], []
    for ref in others:
        taps, halves, pieces = message_views(ref, own)
        kernels.append(
            jnp.concatenate(
                [jnp.concatenate([taps[3 * a + b][...] for b in range(3)], axis=1) for a in range(3)], axis=0
            )
        )
        columns.append(column_of(pieces, own))
        ups.append(halves)
    turned[...] = jnp.transpose(jnp.concatenate(kernels, axis=0).astype(F32)).astype(BF16)
    back_kernel = jnp.concatenate([turned[pl.ds(b * C + start, own), :] for b in range(3)], axis=0)
    edge_sum = jnp.zeros((own, 128), F32)
    pads = []
    for k in range(SLOTS):
        stack = [frames[k]]
        for other_kernel, bias_column, halves in zip(kernels[1:], columns, ups):
            _, slopes = activation(other_kernel, windows[k], bias_column, upstream_of(halves, k, full))
            stack.append(frame_of(slopes))
        spread = dot(back_kernel, jnp.concatenate(stack, axis=0))
        first, second, third = spread[:own], spread[own : 2 * own], spread[2 * own :]
        pad = (
            second
            + jnp.where(column < TS - 1, pltpu.roll(first, FRAME - 1, 1), 0.0)
            + jnp.where(column > 0, pltpu.roll(third, 1, 1), 0.0)
        )
        pads.append(pad)
        edge_sum = edge_sum + dot(first.astype(BF16), spreads[0, k], ((1,), (1,)))
        edge_sum = edge_sum + dot(third.astype(BF16), spreads[1, k], ((1,), (1,)))
        crest = jnp.where(lane128 < TS, pad[:, CELLS:], 0.0) * at_top[k]
        edge_sum = edge_sum + pltpu.roll(crest, FOLD, 1)
    edges[...] = edge_sum.astype(BF16)
    _, halves, _ = message_views(shared, own)
    for k in range(SLOTS):
        first = pads[k][:, :128]
        second = pads[k][:, 128:CELLS]
        for l in range(SLOTS):
            if l != k:
                ends = pads[l][:, CELLS:]
                first = first + jnp.where(lane128 < TS, ends, 0.0) * above[l][k]
                second = second + jnp.where(lane128 >= 128 - TS, ends, 0.0) * above[k][l]
        base[k] = upstream_of(halves, k, full) + jnp.concatenate([first, second], axis=1)
    put.wait()


def finish_kernel(base, *refs):
    out = refs[-1]
    n = len(refs) // 2
    total = None
    for received, hits in zip(refs[:n], refs[n:]):
        part = dot(received[...], hits[...], ((1,), (1,)))
        total = part if total is None else total + part
    for k in range(SLOTS):
        out[0, k] = (base[k] + total[:, k * CELLS : (k + 1) * CELLS]).astype(BF16)


def gather_kernel(mine, theirs, weights_out, bias_out):
    rep = lax.axis_index("rep")
    own = weights_out.shape[1]
    low = jnp.where(rep == 0, mine[...], theirs[...])
    high = jnp.where(rep == 0, theirs[...], mine[...])
    sums = jnp.concatenate([low, high], axis=0)
    for t in range(9):
        weights_out[t] = sums[t * own : (t + 1) * own]
    bias_out[...] = sums[9 * own : 9 * own + 1, :own]


SMEM = pl.BlockSpec(memory_space=pltpu.SMEM)
VMEM = pl.BlockSpec(memory_space=pltpu.VMEM)
HBM = pl.BlockSpec(memory_space=pltpu.HBM)


def call(kernel, specs, outs, scratch=(), out_specs=None, cost=None):
    return pl.pallas_call(
        kernel,
        in_specs=specs,
        out_specs=out_specs or [VMEM] * len(outs),
        out_shape=outs,
        scratch_shapes=list(scratch),
        cost_estimate=cost,
        compiler_params=pltpu.CompilerParams(vmem_limit_bytes=40 << 20),
    )


def struct(shape, dtype):
    return jax.ShapeDtypeStruct(shape, dtype)


def on_device(fields, tile_rows, weights, bias, cotangent):
    own = weights.shape[1]
    count = lax.axis_size("tiles")
    chans = lax.axis_size("chan")
    reps = lax.axis_size("rep")
    plans = halo_plans(count)
    n = len(plans)
    shared_rows = 9 * own + 2 * SLOTS * own + 16
    half_rows = -(-(9 * own + 1) // 32) * 16
    swap = [(0, 1), (1, 0)]

    pinned = [
        pltpu.with_memory_space_constraint(x, pltpu.HBM)
        for x in (tile_rows, fields, weights, bias.reshape(1, own), cotangent)
    ]
    rows, tiles, *packed = call(
        lambda *refs: pack_kernel(*refs, count=count),
        [HBM] * 2,
        [struct(tile_rows.shape, jnp.int32), struct((SLOTS, C, CELLS), BF16)]
        + [struct((C, 128), BF16)] * n
        + [struct((SLOTS * CELLS, 128), BF16)] * n,
        [pltpu.SMEM(tile_rows.shape, jnp.int32), pltpu.SemaphoreType.DMA((2,))],
    )(*pinned[:2])
    messages, maps = packed[:n], packed[n:]
    halos = []
    for (route, _), message in zip(plans, messages):
        if route is None:
            halos.append(message)
        else:
            halos.append(lax.ppermute(message, "tiles", [(i, route(i)) for i in range(count)]))

    windows, spreads, kernel, shared = call(
        window_kernel,
        [SMEM, VMEM] + [HBM] * 3,
        [
            struct((SLOTS, 3 * C, FRAME), BF16),
            struct((2, SLOTS, 128, FRAME), BF16),
            struct((3 * own, 3 * C), BF16),
            struct((shared_rows, 128), BF16),
        ],
        [pltpu.VMEM((1, own), F32), pltpu.SemaphoreType.DMA((10 + 2 * SLOTS,))],
    )(rows, tiles, *pinned[2:])
    others = [lax.ppermute(shared, "chan", [(i, (i + s) % chans) for i in range(chans)]) for s in range(1, chans)]

    windows, frames, result, keep, send = call(
        lambda *refs: forward_kernel(*refs, n_halos=n, half_rows=half_rows),
        [SMEM] + [VMEM] * (5 + n),
        [
            struct((SLOTS, 3 * C, FRAME), BF16),
            struct((SLOTS, 3 * own, FRAME), BF16),
            struct((SLOTS, own, CELLS), BF16),
            struct((half_rows, 128), F32),
            struct((half_rows, 128), F32),
        ],
        cost=pl.CostEstimate(flops=4 * 10**9, transcendentals=0, bytes_accessed=0),
    )(rows, tiles, shared, kernel, spreads, windows, *halos)

    send, others = lax.optimization_barrier((send, others))
    sums = keep + lax.ppermute(send, "rep", swap)
    rounded = sums.astype(BF16)
    frames, rounded = lax.optimization_barrier((frames, rounded))

    base, edges, result = call(
        lambda *refs: backward_kernel(*refs, n_others=len(others)),
        [SMEM] + [VMEM] * (6 + len(others)),
        [
            struct((SLOTS, own, CELLS), F32),
            struct((own, 128), BF16),
            struct((1, SLOTS, own, CELLS), BF16),
        ],
        [pltpu.VMEM((3 * C, 3 * own * chans), BF16), pltpu.SemaphoreType.DMA],
        out_specs=[VMEM, VMEM, HBM],
    )(rows, shared, kernel, spreads, windows, frames, result, *others)

    merged = None
    routes = sum_routes(count)
    for step, route in enumerate(routes):
        pairs = [(i, route(i)) for i in range(count)]
        if step == 1:
            rounded, edges = lax.optimization_barrier((rounded, edges))
        if count == 4 and step == 1:
            both = lax.ppermute(jnp.concatenate([rounded, edges], axis=0), "tiles", pairs)
            other, merged = both[:half_rows], both[half_rows:]
        else:
            other = lax.ppermute(rounded, "tiles", pairs)
        sums = rounded.astype(F32) + other.astype(F32)
        rounded = sums.astype(BF16)
    grad_scale = 1.0 / math.sqrt(reps * fields.shape[0] * count * SLOTS * CELLS)
    sums = sums * grad_scale
    returned = []
    for i, (route, _) in enumerate(plans):
        if route is None:
            returned.append(edges)
        elif merged is not None and i == 0:
            returned.append(merged)
        else:
            returned.append(lax.ppermute(edges, "tiles", [(route(j), j) for j in range(count)]))
    sums, returned = lax.optimization_barrier((sums, returned))
    grad_fields = call(
        finish_kernel,
        [VMEM] * (1 + 2 * n),
        [struct((1, SLOTS, own, CELLS), BF16)],
    )(base, *returned, *maps)[0]
    grad_weights, grad_bias = call(
        gather_kernel,
        [VMEM, VMEM],
        [struct((9, own, C), F32), struct((1, own), F32)],
    )(sums, lax.ppermute(sums, "rep", swap))
    return (result, grad_fields, grad_weights, grad_bias.reshape(own))


def solution(mesh):
    in_specs = (
        P(("groups", "rep"), "tiles", None, None),
        P(),
        P(None, "chan", None),
        P("chan"),
        P(("groups", "rep"), "tiles", "chan", None),
    )
    out_specs = (
        P(("groups", "rep"), "tiles", "chan", None),
        P(("groups", "rep"), "tiles", "chan", None),
        P("groups", "chan", None),
        P(("groups", "chan")),
    )
    return jax.shard_map(
        on_device, mesh=mesh, in_specs=in_specs, out_specs=out_specs, check_vma=False
    )
```

```python
import math

import jax
import jax.numpy as jnp
from jax import lax
from jax.experimental import pallas as pl
from jax.experimental.pallas import tpu as pltpu
from jax.sharding import PartitionSpec as P

C = 128
TS = 16
SLOTS = 3
CELLS = TS * TS
FRAME = 384
EDGE = TS + 2
EAST = SLOTS * EDGE
FOLD = 2 * SLOTS * EDGE
F32 = jnp.float32
BF16 = jnp.bfloat16
GELU_C = math.sqrt(2.0 / math.pi)
GELU_K = 0.044715


def iota(shape, dim):
    return lax.broadcasted_iota(jnp.int32, shape, dim)


def halo_plans(count):
    if count == 4:
        return [
            (lambda d: 3 - d, ("side", "fold")),
            (lambda d: d ^ 2, ("corner",)),
            (lambda d: d ^ 1, ("side",)),
            (None, ("corner",)),
        ]
    return [
        (lambda d: (d + 1) % count, ("west",)),
        (lambda d: (d + count - 1) % count, ("east",)),
        (lambda d: count - 1 - d, ("fold",)),
        (lambda d: (count - d) % count, ("corner_west",)),
        (lambda d: (2 * count - 2 - d) % count, ("corner_east",)),
    ]


def sum_routes(count):
    if count == 4:
        return [lambda d: d ^ 2, lambda d: d ^ 1]
    return [lambda d, s=1 << i: d ^ s for i in range(count.bit_length() - 1)]


def halo_sources(rows, count, source, target, roles):
    lane = iota((8, 128), 1)
    top = 2 * SLOTS - 1
    east = (lane >= EAST) & (lane < FOLD)
    at = lane - jnp.where(east, EAST, 0)
    k = jnp.where(at >= EDGE, 1, 0) + jnp.where(at >= 2 * EDGE, 1, 0)
    p = at - EDGE * k
    rim = lane < FOLD
    row = jnp.where(k == 0, rows[target, 0], jnp.where(k == 1, rows[target, 1], rows[target, 2]))
    row = jnp.where(rim, row, -1)
    src = jnp.full((8, 128), -1, jnp.int32)
    sides = [name for name in ("west", "east") if name in roles or "side" in roles]
    if sides:
        wanted = row + jnp.where(p == TS + 1, 1, 0) - jnp.where(p == 0, 1, 0)
        slot = jnp.full((8, 128), -1, jnp.int32)
        present = (p > 0) & (p <= TS)
        for l in range(SLOTS):
            slot = jnp.where(wanted == rows[source, l], l, slot)
            present = present | (wanted == rows[target, l])
        cell = jnp.where(p == 0, CELLS - TS, jnp.where(p == TS + 1, 0, TS * (p - 1))) + jnp.where(east, 0, TS - 1)
        good = present & (row >= 0) & (wanted >= 0) & (slot >= 0)
        from_west = target == (source + 1) % count if "west" in sides else False
        from_east = target == (source + count - 1) % count if "east" in sides else False
        good = good & ((jnp.logical_not(east) & from_west) | (east & from_east))
        src = jnp.where(good, slot * CELLS + cell, src)

    def top_slot(column):
        found = jnp.int32(-1)
        for l in range(SLOTS):
            found = jnp.where(rows[column, l] == top, l, found)
        return found

    if sides and len(sides) == len(roles) and "side" not in roles or roles == ("side",):
        return src
    mine = top_slot(source)
    if "fold" in roles:
        good = (lane >= FOLD) & (lane < FOLD + TS) & (mine >= 0) & (target == count - 1 - source)
        src = jnp.where(good, mine * CELLS + (CELLS - 1 + FOLD) - lane, src)
    corners = [name for name in ("west", "east") if "corner" in roles or f"corner_{name}" in roles]
    if corners:
        good = (row == top) & (p == TS + 1) & (mine >= 0) & (top_slot(count - 1 - target) >= 0)
        from_west = target == (count - source) % count if "west" in corners else False
        from_east = target == (2 * count - 2 - source) % count if "east" in corners else False
        good = good & ((jnp.logical_not(east) & from_west) | (east & from_east))
        src = jnp.where(good, mine * CELLS + CELLS - TS + jnp.where(east, TS - 1, 0), src)
    return src


def halo_map(rows, count, source, plan):
    route, roles = plan
    target = source if route is None else route(source)
    src = halo_sources(rows, count, source, target, roles)
    hits = iota((SLOTS * CELLS, 128), 0) == src[0:1, :]
    return jnp.where(hits, 1.0, 0.0).astype(BF16)


def dot(lhs, rhs, dims=((1,), (0,))):
    return lax.dot_general(lhs, rhs, (dims, ((), ())), preferred_element_type=F32)


def message_views(ref, own):
    taps = [ref.at[t * own : (t + 1) * own] for t in range(9)]
    base = 9 * own
    halves = [
        [ref.at[base + (2 * k + h) * own : base + (2 * k + h + 1) * own] for h in range(2)] for k in range(SLOTS)
    ]
    at = base + 2 * SLOTS * own
    return taps, halves, ref.at[at : at + 16]


def pack_kernel(rows_hbm, fields_hbm, weights_hbm, bias_hbm, cot_hbm, *refs, count):
    n = len(halo_plans(count))
    rows_out, fields_out, shared = refs[:3]
    outs = refs[3 : 3 + n]
    maps = refs[3 + n : 3 + 2 * n]
    rows, bias, sem = refs[3 + 2 * n :]
    own = weights_hbm.shape[1]
    taps, halves, pieces = message_views(shared, own)
    get_rows = pltpu.make_async_copy(rows_hbm, rows, sem.at[0])
    get_rows.start()
    get_fields = pltpu.make_async_copy(fields_hbm.at[0], fields_out, sem.at[1])
    get_fields.start()
    get_bias = pltpu.make_async_copy(bias_hbm, bias, sem.at[2])
    get_bias.start()
    more = [pltpu.make_async_copy(weights_hbm.at[t], taps[t], sem.at[3 + t]) for t in range(9)]
    for k in range(SLOTS):
        for h in range(2):
            source = cot_hbm.at[0, k, :, h * 128 : h * 128 + 128]
            more.append(pltpu.make_async_copy(source, halves[k][h], sem.at[12 + 2 * k + h]))
    for copy in more:
        copy.start()
    get_rows.wait()
    position = lax.axis_index("tiles")
    plans = halo_plans(count)
    for plan, out in zip(plans, maps):
        out[...] = halo_map(rows, count, position, plan)
    put_rows = pltpu.make_async_copy(rows, rows_out, sem.at[0])
    put_rows.start()
    get_bias.wait()
    line = jnp.concatenate([bias[...], jnp.zeros((1, 128 - own), F32)], axis=1)
    high = line.astype(BF16).astype(F32)
    middle = (line - high).astype(BF16).astype(F32)
    low = line - high - middle
    pieces[...] = jnp.concatenate([high, middle, low, jnp.zeros((13, 128), F32)], axis=0).astype(BF16)
    get_fields.wait()
    cells = jnp.concatenate([fields_out[k] for k in range(SLOTS)], axis=1)
    for out, hits in zip(outs, maps):
        out[...] = dot(cells, hits[...]).astype(BF16)
    for copy in more:
        copy.wait()
    put_rows.wait()


def flag(condition):
    return jnp.where(condition, 1.0, 0.0).astype(F32)


def slot_flags(rows):
    position = lax.axis_index("tiles")
    row = [rows[position, k] for k in range(SLOTS)]
    full = [flag(r >= 0) for r in row]
    at_top = [flag(r == 2 * SLOTS - 1) for r in row]
    above = [[flag((row[k] >= 0) & (row[l] == row[k] + 1)) for l in range(SLOTS)] for k in range(SLOTS)]
    return full, at_top, above


def window_kernel(rows, fields, shared, windows, spreads, kernel):
    own = kernel.shape[0] // 3
    taps, _, _ = message_views(shared, own)
    full, _, above = slot_flags(rows)
    column = iota((1, FRAME), 1) % TS
    lane128 = iota((1, 128), 1)
    tiles = [fields[k].astype(F32) * full[k] for k in range(SLOTS)]
    for k in range(SLOTS):
        north = jnp.zeros((C, 128), F32)
        south = jnp.zeros((C, 128), F32)
        for l in range(SLOTS):
            if l != k:
                north = north + above[k][l] * tiles[l][:, :128]
                south = south + above[l][k] * tiles[l][:, 128:]
        ends = jnp.where(lane128 < TS, north, jnp.where(lane128 >= 128 - TS, south, 0.0))
        centre = jnp.concatenate([tiles[k], ends], axis=1)
        windows[k, :C] = jnp.where(column == 0, 0.0, pltpu.roll(centre, 1, 1)).astype(BF16)
        windows[k, C : 2 * C] = centre.astype(BF16)
        windows[k, 2 * C :] = jnp.where(column == TS - 1, 0.0, pltpu.roll(centre, FRAME - 1, 1)).astype(BF16)
    p_at = iota((128, FRAME), 0)
    frame_lane = iota((128, FRAME), 1)
    for side in range(2):
        for k in range(SLOTS):
            p = p_at - (side * EAST + k * EDGE)
            spot = jnp.where(p == 0, FRAME - TS, TS * (p - 1)) + side * (TS - 1)
            hits = (p >= 0) & (p < EDGE) & (frame_lane == spot)
            spreads[side, k] = jnp.where(hits, 1.0, 0.0).astype(BF16)
    for a in range(3):
        for b in range(3):
            kernel[a * own : (a + 1) * own, b * C : (b + 1) * C] = taps[3 * a + b][...]


def column_of(pieces, own):
    eye = iota((own, 128), 0) == iota((own, 128), 1)
    parts = pieces[...].astype(F32)
    line = parts[0:1] + parts[1:2] + parts[2:3]
    return jnp.sum(jnp.where(eye, line, 0.0), axis=1, keepdims=True)


def activation(kernel, window, bias_column, up):
    own = bias_column.shape[0]
    sums = dot(kernel, window)
    pre = (
        pltpu.roll(sums[:own], TS, 1)[:, :CELLS]
        + sums[own : 2 * own, :CELLS]
        + pltpu.roll(sums[2 * own :], FRAME - TS, 1)[:, :CELLS]
        + bias_column
    )
    square = pre * pre
    tanh = jnp.tanh(GELU_C * (pre * (1.0 + GELU_K * square)))
    half = 0.5 + 0.5 * tanh
    slope = half + (0.5 * pre) * (1.0 - tanh * tanh) * (GELU_C + (3.0 * GELU_C * GELU_K) * square)
    return pre * half, (up * slope).astype(BF16).astype(F32)


def frame_of(slopes):
    own = slopes.shape[0]
    wide = jnp.concatenate([slopes, jnp.zeros((own, FRAME - CELLS), F32)], axis=1)
    return jnp.concatenate([pltpu.roll(wide, FRAME - TS, 1), wide, pltpu.roll(wide, TS, 1)], axis=0).astype(BF16)


def upstream_of(halves, k, full):
    return jnp.concatenate([halves[k][0][...], halves[k][1][...]], axis=1).astype(F32) * full[k]


def forward_kernel(rows, fields, shared, kernel, spreads, windows, *refs, n_halos, half_rows):
    halos = refs[:n_halos]
    full_windows, frames, result, keep, send = refs[n_halos:]
    own = kernel.shape[0] // 3
    full, at_top, _ = slot_flags(rows)
    start = pl.multiple_of(lax.axis_index("chan") * own, own)
    rep = lax.axis_index("rep")
    lane128 = iota((1, 128), 1)
    _, halves, pieces = message_views(shared, own)
    bias_column = column_of(pieces, own)
    halo = halos[0][...].astype(F32)
    for ref in halos[1:]:
        halo = halo + ref[...].astype(F32)
    turned = pltpu.roll(halo, 128 - FOLD, 1)
    fold = jnp.where(lane128 < TS, turned, 0.0)
    fold_left = jnp.where((lane128 > 0) & (lane128 < TS), pltpu.roll(turned, 1, 1), 0.0)
    fold_right = jnp.where(lane128 < TS - 1, pltpu.roll(turned, 127, 1), 0.0)
    halo = halo.astype(BF16)
    grads = jnp.zeros((3 * own, 3 * C), F32)
    slope_sum = jnp.zeros((own, CELLS), F32)
    for k in range(SLOTS):
        west = dot(halo, spreads[0, k])
        east = dot(halo, spreads[1, k])
        rest = jnp.zeros((C, CELLS), F32)
        left = windows[k, :C] + (west + jnp.concatenate([rest, at_top[k] * fold_left], axis=1)).astype(BF16)
        right = windows[k, 2 * C :] + (east + jnp.concatenate([rest, at_top[k] * fold_right], axis=1)).astype(BF16)
        centre = windows[k, C : 2 * C] + jnp.concatenate([rest, at_top[k] * fold], axis=1).astype(BF16)
        window = jnp.concatenate([left, centre, right], axis=0)
        full_windows[k] = window
        up = upstream_of(halves, k, full)
        gelu, slopes = activation(kernel[...], window, bias_column, up)
        result[k] = (full[k] * (fields[k, pl.ds(start, own), :].astype(F32) + gelu)).astype(BF16)
        slope_sum = slope_sum + slopes
        frame = frame_of(slopes)
        frames[k] = frame
        grads = grads + dot(frame, window, ((1,), (1,)))
    blocks = [grads[a * own : (a + 1) * own, b * C : (b + 1) * C] for a in range(3) for b in range(3)]
    eye = iota((own, 128), 0) == iota((own, 128), 1)
    bias_line = jnp.sum(jnp.where(eye, jnp.sum(slope_sum, axis=1, keepdims=True), 0.0), axis=0, keepdims=True)
    blocks.append(bias_line)
    blocks.append(jnp.zeros((2 * half_rows - 9 * own - 1, 128), F32))
    sums = jnp.concatenate(blocks, axis=0)
    low, high = sums[:half_rows], sums[half_rows:]
    keep[...] = jnp.where(rep == 0, low, high)
    send[...] = jnp.where(rep == 0, high, low)


def backward_kernel(rows, shared, kernel, spreads, windows, frames, result, *refs, n_others):
    others = refs[:n_others]
    base, edges, result_out, turned, sem = refs[n_others:]
    own = kernel.shape[0] // 3
    put = pltpu.make_async_copy(result, result_out.at[0], sem)
    put.start()
    full, at_top, above = slot_flags(rows)
    start = pl.multiple_of(lax.axis_index("chan") * own, own)
    column = iota((1, FRAME), 1) % TS
    lane128 = iota((1, 128), 1)
    kernels = [kernel[...]]
    columns, ups = [], []
    for ref in others:
        taps, halves, pieces = message_views(ref, own)
        kernels.append(
            jnp.concatenate(
                [jnp.concatenate([taps[3 * a + b][...] for b in range(3)], axis=1) for a in range(3)], axis=0
            )
        )
        columns.append(column_of(pieces, own))
        ups.append(halves)
    turned[...] = jnp.transpose(jnp.concatenate(kernels, axis=0).astype(F32)).astype(BF16)
    back_kernel = jnp.concatenate([turned[pl.ds(b * C + start, own), :] for b in range(3)], axis=0)
    edge_sum = jnp.zeros((own, 128), F32)
    pads = []
    for k in range(SLOTS):
        stack = [frames[k]]
        for other_kernel, bias_column, halves in zip(kernels[1:], columns, ups):
            _, slopes = activation(other_kernel, windows[k], bias_column, upstream_of(halves, k, full))
            stack.append(frame_of(slopes))
        spread = dot(back_kernel, jnp.concatenate(stack, axis=0))
        first, second, third = spread[:own], spread[own : 2 * own], spread[2 * own :]
        pad = (
            second
            + jnp.where(column < TS - 1, pltpu.roll(first, FRAME - 1, 1), 0.0)
            + jnp.where(column > 0, pltpu.roll(third, 1, 1), 0.0)
        )
        pads.append(pad)
        edge_sum = edge_sum + dot(first.astype(BF16), spreads[0, k], ((1,), (1,)))
        edge_sum = edge_sum + dot(third.astype(BF16), spreads[1, k], ((1,), (1,)))
        crest = jnp.where(lane128 < TS, pad[:, CELLS:], 0.0) * at_top[k]
        edge_sum = edge_sum + pltpu.roll(crest, FOLD, 1)
    edges[...] = edge_sum.astype(BF16)
    _, halves, _ = message_views(shared, own)
    for k in range(SLOTS):
        first = pads[k][:, :128]
        second = pads[k][:, 128:CELLS]
        for l in range(SLOTS):
            if l != k:
                ends = pads[l][:, CELLS:]
                first = first + jnp.where(lane128 < TS, ends, 0.0) * above[l][k]
                second = second + jnp.where(lane128 >= 128 - TS, ends, 0.0) * above[k][l]
        base[k] = upstream_of(halves, k, full) + jnp.concatenate([first, second], axis=1)
    put.wait()


def finish_kernel(base, *refs):
    out = refs[-1]
    n = len(refs) // 2
    total = None
    for received, hits in zip(refs[:n], refs[n:]):
        part = dot(received[...], hits[...], ((1,), (1,)))
        total = part if total is None else total + part
    for k in range(SLOTS):
        out[0, k] = (base[k] + total[:, k * CELLS : (k + 1) * CELLS]).astype(BF16)


def gather_kernel(mine, theirs, weights_out, bias_out):
    rep = lax.axis_index("rep")
    own = weights_out.shape[1]
    low = jnp.where(rep == 0, mine[...], theirs[...])
    high = jnp.where(rep == 0, theirs[...], mine[...])
    sums = jnp.concatenate([low, high], axis=0)
    for t in range(9):
        weights_out[t] = sums[t * own : (t + 1) * own]
    bias_out[...] = sums[9 * own : 9 * own + 1, :own]


SMEM = pl.BlockSpec(memory_space=pltpu.SMEM)
VMEM = pl.BlockSpec(memory_space=pltpu.VMEM)
HBM = pl.BlockSpec(memory_space=pltpu.HBM)


def call(kernel, specs, outs, scratch=(), out_specs=None):
    return pl.pallas_call(
        kernel,
        in_specs=specs,
        out_specs=out_specs or [VMEM] * len(outs),
        out_shape=outs,
        scratch_shapes=list(scratch),
        compiler_params=pltpu.CompilerParams(vmem_limit_bytes=40 << 20),
    )


def struct(shape, dtype):
    return jax.ShapeDtypeStruct(shape, dtype)


def on_device(fields, tile_rows, weights, bias, cotangent):
    own = weights.shape[1]
    count = lax.axis_size("tiles")
    chans = lax.axis_size("chan")
    reps = lax.axis_size("rep")
    plans = halo_plans(count)
    n = len(plans)
    shared_rows = 9 * own + 2 * SLOTS * own + 16
    half_rows = -(-(9 * own + 1) // 32) * 16
    swap = [(0, 1), (1, 0)]

    pinned = [
        pltpu.with_memory_space_constraint(x, pltpu.HBM)
        for x in (tile_rows, fields, weights, bias.reshape(1, own), cotangent)
    ]
    rows, tiles, shared, *packed = call(
        lambda *refs: pack_kernel(*refs, count=count),
        [HBM] * 5,
        [
            struct(tile_rows.shape, jnp.int32),
            struct((SLOTS, C, CELLS), BF16),
            struct((shared_rows, 128), BF16),
        ]
        + [struct((C, 128), BF16)] * n
        + [struct((SLOTS * CELLS, 128), BF16)] * n,
        [
            pltpu.SMEM(tile_rows.shape, jnp.int32),
            pltpu.VMEM((1, own), F32),
            pltpu.SemaphoreType.DMA((12 + 2 * SLOTS,)),
        ],
    )(*pinned)
    messages, maps = packed[:n], packed[n:]
    halos = []
    for (route, _), message in zip(plans, messages):
        if route is None:
            halos.append(message)
        else:
            halos.append(lax.ppermute(message, "tiles", [(i, route(i)) for i in range(count)]))

    windows, spreads, kernel = call(
        window_kernel,
        [SMEM] + [VMEM] * 2,
        [
            struct((SLOTS, 3 * C, FRAME), BF16),
            struct((2, SLOTS, 128, FRAME), BF16),
            struct((3 * own, 3 * C), BF16),
        ],
    )(rows, tiles, shared)
    others = [lax.ppermute(shared, "chan", [(i, (i + s) % chans) for i in range(chans)]) for s in range(1, chans)]

    windows, frames, result, keep, send = call(
        lambda *refs: forward_kernel(*refs, n_halos=n, half_rows=half_rows),
        [SMEM] + [VMEM] * (5 + n),
        [
            struct((SLOTS, 3 * C, FRAME), BF16),
            struct((SLOTS, 3 * own, FRAME), BF16),
            struct((SLOTS, own, CELLS), BF16),
            struct((half_rows, 128), F32),
            struct((half_rows, 128), F32),
        ],
    )(rows, tiles, shared, kernel, spreads, windows, *halos)

    send, others = lax.optimization_barrier((send, others))
    sums = keep + lax.ppermute(send, "rep", swap)
    rounded = sums.astype(BF16)
    frames, rounded = lax.optimization_barrier((frames, rounded))

    base, edges, result = call(
        lambda *refs: backward_kernel(*refs, n_others=len(others)),
        [SMEM] + [VMEM] * (6 + len(others)),
        [
            struct((SLOTS, own, CELLS), F32),
            struct((own, 128), BF16),
            struct((1, SLOTS, own, CELLS), BF16),
        ],
        [pltpu.VMEM((3 * C, 3 * own * chans), BF16), pltpu.SemaphoreType.DMA],
        out_specs=[VMEM, VMEM, HBM],
    )(rows, shared, kernel, spreads, windows, frames, result, *others)

    merged = None
    routes = sum_routes(count)
    for step, route in enumerate(routes):
        pairs = [(i, route(i)) for i in range(count)]
        if step == 1:
            rounded, edges = lax.optimization_barrier((rounded, edges))
        if count == 4 and step == 1:
            both = lax.ppermute(jnp.concatenate([rounded, edges], axis=0), "tiles", pairs)
            other, merged = both[:half_rows], both[half_rows:]
        else:
            other = lax.ppermute(rounded, "tiles", pairs)
        sums = rounded.astype(F32) + other.astype(F32)
        rounded = sums.astype(BF16)
    grad_scale = 1.0 / math.sqrt(reps * fields.shape[0] * count * SLOTS * CELLS)
    sums = sums * grad_scale
    returned = []
    for i, (route, _) in enumerate(plans):
        if route is None:
            returned.append(edges)
        elif merged is not None and i == 2:
            returned.append(merged)
        else:
            returned.append(lax.ppermute(edges, "tiles", [(route(j), j) for j in range(count)]))
    sums, returned = lax.optimization_barrier((sums, returned))
    grad_fields = call(
        finish_kernel,
        [VMEM] * (1 + 2 * n),
        [struct((1, SLOTS, own, CELLS), BF16)],
    )(base, *returned, *maps)[0]
    grad_weights, grad_bias = call(
        gather_kernel,
        [VMEM, VMEM],
        [struct((9, own, C), F32), struct((1, own), F32)],
    )(sums, lax.ppermute(sums, "rep", swap))
    return (result, grad_fields, grad_weights, grad_bias.reshape(own))


def solution(mesh):
    in_specs = (
        P(("groups", "rep"), "tiles", None, None),
        P(),
        P(None, "chan", None),
        P("chan"),
        P(("groups", "rep"), "tiles", "chan", None),
    )
    out_specs = (
        P(("groups", "rep"), "tiles", "chan", None),
        P(("groups", "rep"), "tiles", "chan", None),
        P("groups", "chan", None),
        P(("groups", "chan")),
    )
    return jax.shard_map(
        on_device, mesh=mesh, in_specs=in_specs, out_specs=out_specs, check_vma=False
    )
```

```python
import math

import jax
import jax.numpy as jnp
from jax import lax
from jax.experimental import pallas as pl
from jax.experimental.pallas import tpu as pltpu
from jax.sharding import PartitionSpec as P

C = 128
TS = 16
SLOTS = 3
CELLS = TS * TS
FRAME = 384
EDGE = TS + 2
EAST = SLOTS * EDGE
FOLD = 2 * SLOTS * EDGE
F32 = jnp.float32
BF16 = jnp.bfloat16
GELU_C = math.sqrt(2.0 / math.pi)
GELU_K = 0.044715


def iota(shape, dim):
    return lax.broadcasted_iota(jnp.int32, shape, dim)


def halo_plans(count):
    if count == 4:
        return [
            (lambda d: d ^ 1, ("side",)),
            (lambda d: 3 - d, ("side", "fold")),
            (lambda d: d ^ 2, ("corner",)),
            (None, ("corner",)),
        ]
    return [
        (lambda d: (d + 1) % count, ("west",)),
        (lambda d: (d + count - 1) % count, ("east",)),
        (lambda d: count - 1 - d, ("fold",)),
        (lambda d: (count - d) % count, ("corner_west",)),
        (lambda d: (2 * count - 2 - d) % count, ("corner_east",)),
    ]


def sum_routes(count):
    if count == 4:
        return [lambda d: d ^ 2, lambda d: d ^ 1]
    return [lambda d, s=1 << i: d ^ s for i in range(count.bit_length() - 1)]


def halo_sources(rows, count, source, target, roles):
    lane = iota((8, 128), 1)
    top = 2 * SLOTS - 1
    east = (lane >= EAST) & (lane < FOLD)
    at = lane - jnp.where(east, EAST, 0)
    k = jnp.where(at >= EDGE, 1, 0) + jnp.where(at >= 2 * EDGE, 1, 0)
    p = at - EDGE * k
    rim = lane < FOLD
    row = jnp.where(k == 0, rows[target, 0], jnp.where(k == 1, rows[target, 1], rows[target, 2]))
    row = jnp.where(rim, row, -1)
    src = jnp.full((8, 128), -1, jnp.int32)
    sides = [name for name in ("west", "east") if name in roles or "side" in roles]
    if sides:
        wanted = row + jnp.where(p == TS + 1, 1, 0) - jnp.where(p == 0, 1, 0)
        slot = jnp.full((8, 128), -1, jnp.int32)
        present = (p > 0) & (p <= TS)
        for l in range(SLOTS):
            slot = jnp.where(wanted == rows[source, l], l, slot)
            present = present | (wanted == rows[target, l])
        cell = jnp.where(p == 0, CELLS - TS, jnp.where(p == TS + 1, 0, TS * (p - 1))) + jnp.where(east, 0, TS - 1)
        good = present & (row >= 0) & (wanted >= 0) & (slot >= 0)
        from_west = target == (source + 1) % count if "west" in sides else False
        from_east = target == (source + count - 1) % count if "east" in sides else False
        good = good & ((jnp.logical_not(east) & from_west) | (east & from_east))
        src = jnp.where(good, slot * CELLS + cell, src)

    def top_slot(column):
        found = jnp.int32(-1)
        for l in range(SLOTS):
            found = jnp.where(rows[column, l] == top, l, found)
        return found

    if sides and len(sides) == len(roles) and "side" not in roles or roles == ("side",):
        return src
    mine = top_slot(source)
    if "fold" in roles:
        good = (lane >= FOLD) & (lane < FOLD + TS) & (mine >= 0) & (target == count - 1 - source)
        src = jnp.where(good, mine * CELLS + (CELLS - 1 + FOLD) - lane, src)
    corners = [name for name in ("west", "east") if "corner" in roles or f"corner_{name}" in roles]
    if corners:
        good = (row == top) & (p == TS + 1) & (mine >= 0) & (top_slot(count - 1 - target) >= 0)
        from_west = target == (count - source) % count if "west" in corners else False
        from_east = target == (2 * count - 2 - source) % count if "east" in corners else False
        good = good & ((jnp.logical_not(east) & from_west) | (east & from_east))
        src = jnp.where(good, mine * CELLS + CELLS - TS + jnp.where(east, TS - 1, 0), src)
    return src


def halo_map(rows, count, source, plan):
    route, roles = plan
    target = source if route is None else route(source)
    src = halo_sources(rows, count, source, target, roles)
    hits = iota((SLOTS * CELLS, 128), 0) == src[0:1, :]
    return jnp.where(hits, 1.0, 0.0).astype(BF16)


def dot(lhs, rhs, dims=((1,), (0,))):
    return lax.dot_general(lhs, rhs, (dims, ((), ())), preferred_element_type=F32)


def pack_kernel(rows_hbm, fields_hbm, weights_hbm, bias_hbm, cot_hbm, *refs, count, chans, joined):
    n = len(halo_plans(count))
    rows_out, fields_out, weights_out, bias_out, cot_out = refs[:5]
    outs = refs[5 : 5 + n]
    maps = refs[5 + n : 5 + 2 * n]
    shares = list(refs[5 + 2 * n : -2])
    rows, sem = refs[-2:]
    own = weights_hbm.shape[1]
    moves = [
        (rows_hbm, rows),
        (fields_hbm.at[0], fields_out),
        (weights_hbm, weights_out),
        (bias_hbm, bias_out),
        (cot_hbm.at[0], cot_out),
    ]
    copies = [pltpu.make_async_copy(src, dst, sem.at[i]) for i, (src, dst) in enumerate(moves)]
    for copy in copies:
        copy.start()
    copies[0].wait()
    position = lax.axis_index("tiles")
    plans = halo_plans(count)
    for plan, out in zip(plans, maps):
        out[...] = halo_map(rows, count, position, plan)
    put_rows = pltpu.make_async_copy(rows, rows_out, sem.at[0])
    put_rows.start()
    copies[1].wait()
    cells = jnp.concatenate([fields_out[k] for k in range(SLOTS)], axis=1)
    for out, hits in zip(outs, maps):
        out[:C, :] = dot(cells, hits[...]).astype(BF16)
    copies[2].wait()
    if joined:
        shares = [outs[0].at[C:, :]]
    chan = lax.axis_index("chan")
    each = 128 // own
    place = iota((1, 128), 1) // own
    for step, share in enumerate(shares):
        start = (chan + step + 1) % chans * own
        for block in range(-(-9 // each)):
            packed = jnp.zeros((own, 128), F32)
            for j in range(min(each, 9 - block * each)):
                tap = pltpu.roll(weights_out[block * each + j].astype(F32), (j * own + 128 - start) % 128, 1)
                packed = jnp.where(place == j, tap, packed)
            share[block * own : (block + 1) * own, :] = packed.astype(BF16)
    for copy in copies[3:]:
        copy.wait()
    put_rows.wait()


def flag(condition):
    return jnp.where(condition, 1.0, 0.0).astype(F32)


def slot_flags(rows):
    position = lax.axis_index("tiles")
    row = [rows[position, k] for k in range(SLOTS)]
    full = [flag(r >= 0) for r in row]
    at_top = [flag(r == 2 * SLOTS - 1) for r in row]
    above = [[flag((row[k] >= 0) & (row[l] == row[k] + 1)) for l in range(SLOTS)] for k in range(SLOTS)]
    return full, at_top, above


def window_kernel(rows, fields, weights, windows, spreads, gathers, kernel, back_kernel, turned):
    own = weights.shape[1]
    full, _, above = slot_flags(rows)
    column = iota((1, FRAME), 1) % TS
    lane128 = iota((1, 128), 1)
    tiles = [fields[k].astype(F32) * full[k] for k in range(SLOTS)]
    for k in range(SLOTS):
        north = jnp.zeros((C, 128), F32)
        south = jnp.zeros((C, 128), F32)
        for l in range(SLOTS):
            if l != k:
                north = north + above[k][l] * tiles[l][:, :128]
                south = south + above[l][k] * tiles[l][:, 128:]
        ends = jnp.where(lane128 < TS, north, jnp.where(lane128 >= 128 - TS, south, 0.0))
        centre = jnp.concatenate([tiles[k], ends], axis=1)
        windows[k, :C] = jnp.where(column == 0, 0.0, pltpu.roll(centre, 1, 1)).astype(BF16)
        windows[k, C : 2 * C] = centre.astype(BF16)
        windows[k, 2 * C :] = jnp.where(column == TS - 1, 0.0, pltpu.roll(centre, FRAME - 1, 1)).astype(BF16)
    for refs, shape, halo_dim in ((spreads, (128, FRAME), 0), (gathers, (FRAME, 128), 1)):
        p_at = iota(shape, halo_dim)
        frame_lane = iota(shape, 1 - halo_dim)
        for side in range(2):
            for k in range(SLOTS):
                p = p_at - (side * EAST + k * EDGE)
                spot = jnp.where(p == 0, FRAME - TS, TS * (p - 1)) + side * (TS - 1)
                hits = (p >= 0) & (p < EDGE) & (frame_lane == spot)
                refs[side, k] = jnp.where(hits, 1.0, 0.0).astype(BF16)
    stack = jnp.concatenate(
        [jnp.concatenate([weights[3 * a + b] for b in range(3)], axis=1) for a in range(3)], axis=0
    )
    kernel[...] = stack
    turned[...] = jnp.transpose(stack.astype(F32))
    start = pl.multiple_of(lax.axis_index("chan") * own, own)
    for b in range(3):
        back_kernel[b * own : (b + 1) * own, :] = turned[pl.ds(b * C + start, own), :].astype(BF16)


def column_of(line):
    own = line.shape[1]
    eye = iota((own, own), 0) == iota((own, own), 1)
    return jnp.sum(jnp.where(eye, line, 0.0), axis=1, keepdims=True)


def activation(kernel, window, bias_column, up):
    own = bias_column.shape[0]
    sums = dot(kernel, window)
    pre = (
        pltpu.roll(sums[:own], TS, 1)[:, :CELLS]
        + sums[own : 2 * own, :CELLS]
        + pltpu.roll(sums[2 * own :], FRAME - TS, 1)[:, :CELLS]
        + bias_column
    )
    square = pre * pre
    tanh = jnp.tanh(GELU_C * (pre * (1.0 + GELU_K * square)))
    half = 0.5 + 0.5 * tanh
    slope = half + (0.5 * pre) * (1.0 - tanh * tanh) * (GELU_C + (3.0 * GELU_C * GELU_K) * square)
    return pre * half, (up * slope).astype(BF16).astype(F32)


def frame_of(slopes):
    own = slopes.shape[0]
    wide = jnp.concatenate([slopes, jnp.zeros((own, FRAME - CELLS), F32)], axis=1)
    return jnp.concatenate([pltpu.roll(wide, FRAME - TS, 1), wide, pltpu.roll(wide, TS, 1)], axis=0).astype(BF16)


def forward_kernel(rows, fields, bias, cot, kernel, spreads, windows, *refs, n_halos, half_rows):
    halos = refs[:n_halos]
    frames, slopes_out, result, keep, send = refs[n_halos:]
    own = kernel.shape[0] // 3
    full, at_top, _ = slot_flags(rows)
    start = pl.multiple_of(lax.axis_index("chan") * own, own)
    rep = lax.axis_index("rep")
    lane128 = iota((1, 128), 1)
    bias_column = column_of(bias[...])
    halo = halos[0][:C, :].astype(F32)
    for ref in halos[1:]:
        halo = halo + ref[:C, :].astype(F32)
    turned = pltpu.roll(halo, 128 - FOLD, 1)
    fold = jnp.where(lane128 < TS, turned, 0.0)
    fold_left = jnp.where((lane128 > 0) & (lane128 < TS), pltpu.roll(turned, 1, 1), 0.0)
    fold_right = jnp.where(lane128 < TS - 1, pltpu.roll(turned, 127, 1), 0.0)
    halo = halo.astype(BF16)
    grads = jnp.zeros((3 * own, 3 * C), F32)
    slope_sum = jnp.zeros((own, CELLS), F32)
    for k in range(SLOTS):
        west = dot(halo, spreads[0, k])
        east = dot(halo, spreads[1, k])
        rest = jnp.zeros((C, CELLS), F32)
        left = windows[k, :C] + (west + jnp.concatenate([rest, at_top[k] * fold_left], axis=1)).astype(BF16)
        right = windows[k, 2 * C :] + (east + jnp.concatenate([rest, at_top[k] * fold_right], axis=1)).astype(BF16)
        centre = windows[k, C : 2 * C] + jnp.concatenate([rest, at_top[k] * fold], axis=1).astype(BF16)
        window = jnp.concatenate([left, centre, right], axis=0)
        up = cot[k].astype(F32) * full[k]
        gelu, slopes = activation(kernel[...], window, bias_column, up)
        result[k] = (full[k] * (fields[k, pl.ds(start, own), :].astype(F32) + gelu)).astype(BF16)
        slope_sum = slope_sum + slopes
        slopes_out[k * own : (k + 1) * own, :] = slopes.astype(BF16)
        frame = frame_of(slopes)
        frames[k] = frame
        grads = grads + dot(frame, window, ((1,), (1,)))
    blocks = [grads[a * own : (a + 1) * own, b * C : (b + 1) * C] for a in range(3) for b in range(3)]
    eye = iota((own, 128), 0) == iota((own, 128), 1)
    bias_line = jnp.sum(jnp.where(eye, jnp.sum(slope_sum, axis=1, keepdims=True), 0.0), axis=0, keepdims=True)
    blocks.append(bias_line)
    blocks.append(jnp.zeros((2 * half_rows - 9 * own - 1, 128), F32))
    sums = jnp.concatenate(blocks, axis=0)
    low, high = sums[:half_rows], sums[half_rows:]
    keep[...] = jnp.where(rep == 0, low, high)
    send[...] = jnp.where(rep == 0, high, low)


def backward_kernel(rows, cot, back_kernel, gathers, frames, result, *refs, joined):
    base, edges, result_out, turned, sem = refs[-5:]
    n = (len(refs) - 5) // 2
    own = cot.shape[1]
    put = pltpu.make_async_copy(result, result_out.at[0], sem)
    put.start()
    full, at_top, above = slot_flags(rows)
    column = iota((1, FRAME), 1) % TS
    lane128 = iota((1, 128), 1)
    each = 128 // own
    back_kernels = [back_kernel[...]]
    for ref in refs[:n]:
        taps = ref.at[C:, :] if joined else ref
        for block in range(-(-9 // each)):
            turned[block * 128 : (block + 1) * 128, :] = jnp.transpose(
                taps[block * own : (block + 1) * own, :].astype(F32)
            )
        back_kernels.append(
            jnp.concatenate(
                [
                    jnp.concatenate([turned[t * own : (t + 1) * own, :] for t in (b, 3 + b, 6 + b)], axis=1)
                    for b in range(3)
                ],
                axis=0,
            ).astype(BF16)
        )
    edge_sum = jnp.zeros((own, 128), F32)
    pads = []
    for k in range(SLOTS):
        spread = dot(back_kernels[0], frames[k])
        for other_kernel, slopes in zip(back_kernels[1:], refs[n : 2 * n]):
            spread = spread + dot(other_kernel, frame_of(slopes[k * own : (k + 1) * own, :].astype(F32)))
        first, second, third = spread[:own], spread[own : 2 * own], spread[2 * own :]
        pad = (
            second
            + jnp.where(column < TS - 1, pltpu.roll(first, FRAME - 1, 1), 0.0)
            + jnp.where(column > 0, pltpu.roll(third, 1, 1), 0.0)
        )
        pads.append(pad)
        edge_sum = edge_sum + dot(first.astype(BF16), gathers[0, k])
        edge_sum = edge_sum + dot(third.astype(BF16), gathers[1, k])
        crest = jnp.where(lane128 < TS, pad[:, CELLS:], 0.0) * at_top[k]
        edge_sum = edge_sum + pltpu.roll(crest, FOLD, 1)
    edges[...] = edge_sum.astype(BF16)
    for k in range(SLOTS):
        first = pads[k][:, :128]
        second = pads[k][:, 128:CELLS]
        for l in range(SLOTS):
            if l != k:
                ends = pads[l][:, CELLS:]
                first = first + jnp.where(lane128 < TS, ends, 0.0) * above[l][k]
                second = second + jnp.where(lane128 >= 128 - TS, ends, 0.0) * above[k][l]
        base[k] = cot[k].astype(F32) * full[k] + jnp.concatenate([first, second], axis=1)
    put.wait()


def finish_kernel(base, *refs):
    out = refs[-1]
    n = len(refs) // 2
    total = None
    for received, hits in zip(refs[:n], refs[n:]):
        part = dot(received[...], hits[...], ((1,), (1,)))
        total = part if total is None else total + part
    for k in range(SLOTS):
        out[0, k] = (base[k] + total[:, k * CELLS : (k + 1) * CELLS]).astype(BF16)


def gather_kernel(mine, theirs, weights_out, bias_out):
    rep = lax.axis_index("rep")
    own = weights_out.shape[1]
    low = jnp.where(rep == 0, mine[...], theirs[...])
    high = jnp.where(rep == 0, theirs[...], mine[...])
    sums = jnp.concatenate([low, high], axis=0)
    for t in range(9):
        weights_out[t] = sums[t * own : (t + 1) * own]
    bias_out[...] = sums[9 * own : 9 * own + 1, :own]


SMEM = pl.BlockSpec(memory_space=pltpu.SMEM)
VMEM = pl.BlockSpec(memory_space=pltpu.VMEM)
HBM = pl.BlockSpec(memory_space=pltpu.HBM)


def call(kernel, specs, outs, scratch=(), out_specs=None):
    return pl.pallas_call(
        kernel,
        in_specs=specs,
        out_specs=out_specs or [VMEM] * len(outs),
        out_shape=outs,
        scratch_shapes=list(scratch),
        compiler_params=pltpu.CompilerParams(vmem_limit_bytes=40 << 20),
    )


def struct(shape, dtype):
    return jax.ShapeDtypeStruct(shape, dtype)


def on_device(fields, tile_rows, weights, bias, cotangent):
    own = weights.shape[1]
    count = lax.axis_size("tiles")
    chans = lax.axis_size("chan")
    reps = lax.axis_size("rep")
    plans = halo_plans(count)
    n = len(plans)
    half_rows = -(-(9 * own + 1) // 32) * 16
    swap = [(0, 1), (1, 0)]
    joined = count == 4 and chans == 2
    share_rows = -(-9 // (128 // own)) * own

    pinned = [
        pltpu.with_memory_space_constraint(x, pltpu.HBM)
        for x in (tile_rows, fields, weights, bias.reshape(1, own), cotangent)
    ]
    heights = [C + share_rows * (joined and i == 0) for i in range(n)]
    rows, tiles, taps, bias_line, cot, *packed = call(
        lambda *refs: pack_kernel(*refs, count=count, chans=chans, joined=joined),
        [HBM] * 5,
        [
            struct(tile_rows.shape, jnp.int32),
            struct((SLOTS, C, CELLS), BF16),
            struct((9, own, C), BF16),
            struct((1, own), F32),
            struct((SLOTS, own, CELLS), BF16),
        ]
        + [struct((height, 128), BF16) for height in heights]
        + [struct((SLOTS * CELLS, 128), BF16)] * n
        + [struct((share_rows, 128), BF16)] * (0 if joined else chans - 1),
        [pltpu.SMEM(tile_rows.shape, jnp.int32), pltpu.SemaphoreType.DMA((5,))],
    )(*pinned)
    messages, maps, shares = packed[:n], packed[n : 2 * n], packed[2 * n :]
    halos = []
    for i, ((route, _), message) in enumerate(zip(plans, messages)):
        if route is None:
            halos.append(message)
        elif joined and i == 0:
            pairs = [(2 * d + c, 2 * route(d) + 1 - c) for d in range(count) for c in range(2)]
            halos.append(lax.ppermute(message, ("tiles", "chan"), pairs))
        else:
            halos.append(lax.ppermute(message, "tiles", [(d, route(d)) for d in range(count)]))
    ring = [[(c, (c + s) % chans) for c in range(chans)] for s in range(1, chans)]
    others = [halos[0]] if joined else [lax.ppermute(x, "chan", pairs) for x, pairs in zip(shares, ring)]

    windows, spreads, gathers, kernel, back_kernel = call(
        window_kernel,
        [SMEM] + [VMEM] * 2,
        [
            struct((SLOTS, 3 * C, FRAME), BF16),
            struct((2, SLOTS, 128, FRAME), BF16),
            struct((2, SLOTS, FRAME, 128), BF16),
            struct((3 * own, 3 * C), BF16),
            struct((3 * own, 3 * own), BF16),
        ],
        [pltpu.VMEM((3 * C, 3 * own), F32)],
    )(rows, tiles, taps)

    frames, slopes, result, keep, send = call(
        lambda *refs: forward_kernel(*refs, n_halos=n, half_rows=half_rows),
        [SMEM] + [VMEM] * (6 + n),
        [
            struct((SLOTS, 3 * own, FRAME), BF16),
            struct((SLOTS * own, CELLS), BF16),
            struct((SLOTS, own, CELLS), BF16),
            struct((half_rows, 128), F32),
            struct((half_rows, 128), F32),
        ],
    )(rows, tiles, bias_line, cot, kernel, spreads, windows, *halos)

    sums = keep + lax.ppermute(send, "rep", swap)
    rounded = sums.astype(BF16)
    frames, rounded = lax.optimization_barrier((frames, rounded))
    met = [lax.ppermute(slopes, "chan", pairs) for pairs in ring]

    base, edges, result = call(
        lambda *refs: backward_kernel(*refs, joined=joined),
        [SMEM] + [VMEM] * (5 + 2 * len(met)),
        [
            struct((SLOTS, own, CELLS), F32),
            struct((own, 128), BF16),
            struct((1, SLOTS, own, CELLS), BF16),
        ],
        [pltpu.VMEM((share_rows // own * 128, own), F32), pltpu.SemaphoreType.DMA],
        out_specs=[VMEM, VMEM, HBM],
    )(rows, cot, back_kernel, gathers, frames, result, *others, *met)

    merged = None
    routes = sum_routes(count)
    for step, route in enumerate(routes):
        pairs = [(i, route(i)) for i in range(count)]
        if step == 1:
            rounded, edges = lax.optimization_barrier((rounded, edges))
        if count == 4 and step == 1:
            both = lax.ppermute(jnp.concatenate([rounded, edges], axis=0), "tiles", pairs)
            other, merged = both[:half_rows], both[half_rows:]
        else:
            other = lax.ppermute(rounded, "tiles", pairs)
        sums = rounded.astype(F32) + other.astype(F32)
        rounded = sums.astype(BF16)
    grad_scale = 1.0 / math.sqrt(reps * fields.shape[0] * count * SLOTS * CELLS)
    sums = sums * grad_scale
    returned = []
    for i, (route, _) in enumerate(plans):
        if route is None:
            returned.append(edges)
        elif merged is not None and i == 0:
            returned.append(merged)
        else:
            returned.append(lax.ppermute(edges, "tiles", [(route(j), j) for j in range(count)]))
    sums, returned = lax.optimization_barrier((sums, returned))
    grad_fields = call(
        finish_kernel,
        [VMEM] * (1 + 2 * n),
        [struct((1, SLOTS, own, CELLS), BF16)],
    )(base, *returned, *maps)[0]
    grad_weights, grad_bias = call(
        gather_kernel,
        [VMEM, VMEM],
        [struct((9, own, C), F32), struct((1, own), F32)],
    )(sums, lax.ppermute(sums, "rep", swap))
    return (result, grad_fields, grad_weights, grad_bias.reshape(own))


def solution(mesh):
    in_specs = (
        P(("groups", "rep"), "tiles", None, None),
        P(),
        P(None, "chan", None),
        P("chan"),
        P(("groups", "rep"), "tiles", "chan", None),
    )
    out_specs = (
        P(("groups", "rep"), "tiles", "chan", None),
        P(("groups", "rep"), "tiles", "chan", None),
        P("groups", "chan", None),
        P(("groups", "chan")),
    )
    return jax.shard_map(
        on_device, mesh=mesh, in_specs=in_specs, out_specs=out_specs, check_vma=False
    )
```

```python
import math

import jax
import jax.numpy as jnp
from jax import lax
from jax.experimental import pallas as pl
from jax.experimental.pallas import tpu as pltpu
from jax.sharding import PartitionSpec as P

C = 128
TS = 16
SLOTS = 3
CELLS = TS * TS
FRAME = 384
EDGE = TS + 2
EAST = SLOTS * EDGE
FOLD = 2 * SLOTS * EDGE
F32 = jnp.float32
BF16 = jnp.bfloat16
GELU_C = math.sqrt(2.0 / math.pi)
GELU_K = 0.044715


def iota(shape, dim):
    return lax.broadcasted_iota(jnp.int32, shape, dim)


def halo_plans(count):
    if count == 4:
        return [
            (lambda d: d ^ 1, ("side",)),
            (lambda d: 3 - d, ("side", "fold")),
            (lambda d: d ^ 2, ("corner",)),
            (None, ("corner",)),
        ]
    return [
        (lambda d: (d + 1) % count, ("west",)),
        (lambda d: (d + count - 1) % count, ("east",)),
        (lambda d: count - 1 - d, ("fold",)),
        (lambda d: (count - d) % count, ("corner_west",)),
        (lambda d: (2 * count - 2 - d) % count, ("corner_east",)),
    ]


def halo_sources(rows, count, source, target, roles):
    lane = iota((8, 128), 1)
    top = 2 * SLOTS - 1
    east = (lane >= EAST) & (lane < FOLD)
    at = lane - jnp.where(east, EAST, 0)
    k = jnp.where(at >= EDGE, 1, 0) + jnp.where(at >= 2 * EDGE, 1, 0)
    p = at - EDGE * k
    rim = lane < FOLD
    row = jnp.where(k == 0, rows[target, 0], jnp.where(k == 1, rows[target, 1], rows[target, 2]))
    row = jnp.where(rim, row, -1)
    src = jnp.full((8, 128), -1, jnp.int32)
    sides = [name for name in ("west", "east") if name in roles or "side" in roles]
    if sides:
        wanted = row + jnp.where(p == TS + 1, 1, 0) - jnp.where(p == 0, 1, 0)
        slot = jnp.full((8, 128), -1, jnp.int32)
        present = (p > 0) & (p <= TS)
        for l in range(SLOTS):
            slot = jnp.where(wanted == rows[source, l], l, slot)
            present = present | (wanted == rows[target, l])
        cell = jnp.where(p == 0, CELLS - TS, jnp.where(p == TS + 1, 0, TS * (p - 1))) + jnp.where(east, 0, TS - 1)
        good = present & (row >= 0) & (wanted >= 0) & (slot >= 0)
        from_west = target == (source + 1) % count if "west" in sides else False
        from_east = target == (source + count - 1) % count if "east" in sides else False
        good = good & ((jnp.logical_not(east) & from_west) | (east & from_east))
        src = jnp.where(good, slot * CELLS + cell, src)

    def top_slot(column):
        found = jnp.int32(-1)
        for l in range(SLOTS):
            found = jnp.where(rows[column, l] == top, l, found)
        return found

    if sides and len(sides) == len(roles) and "side" not in roles or roles == ("side",):
        return src
    mine = top_slot(source)
    if "fold" in roles:
        good = (lane >= FOLD) & (lane < FOLD + TS) & (mine >= 0) & (target == count - 1 - source)
        src = jnp.where(good, mine * CELLS + (CELLS - 1 + FOLD) - lane, src)
    corners = [name for name in ("west", "east") if "corner" in roles or f"corner_{name}" in roles]
    if corners:
        good = (row == top) & (p == TS + 1) & (mine >= 0) & (top_slot(count - 1 - target) >= 0)
        from_west = target == (count - source) % count if "west" in corners else False
        from_east = target == (2 * count - 2 - source) % count if "east" in corners else False
        good = good & ((jnp.logical_not(east) & from_west) | (east & from_east))
        src = jnp.where(good, mine * CELLS + CELLS - TS + jnp.where(east, TS - 1, 0), src)
    return src


def halo_map(rows, count, source, plan):
    route, roles = plan
    target = source if route is None else route(source)
    src = halo_sources(rows, count, source, target, roles)
    hits = iota((SLOTS * CELLS, 128), 0) == src[0:1, :]
    return jnp.where(hits, 1.0, 0.0).astype(BF16)


def dot(lhs, rhs, dims=((1,), (0,))):
    return lax.dot_general(lhs, rhs, (dims, ((), ())), preferred_element_type=F32)


def message_views(ref, own):
    taps = [ref.at[t * own : (t + 1) * own] for t in range(9)]
    base = 9 * own
    halves = [
        [ref.at[base + (2 * k + h) * own : base + (2 * k + h + 1) * own] for h in range(2)] for k in range(SLOTS)
    ]
    at = base + 2 * SLOTS * own
    return taps, halves, ref.at[at : at + 16]


def pack_kernel(rows_hbm, fields_hbm, weights_hbm, bias_hbm, cot_hbm, *refs, count):
    n = len(halo_plans(count))
    rows_out, fields_out, shared = refs[:3]
    maps = refs[3 : 3 + n]
    outs = refs[3 + n : -3]
    if count == 4:
        outs = [outs[0].at[:C, :], outs[0].at[C:, :], *outs[1:]]
    rows, bias, sem = refs[-3:]
    own = weights_hbm.shape[1]
    taps, halves, pieces = message_views(shared, own)
    get_rows = pltpu.make_async_copy(rows_hbm, rows, sem.at[0])
    get_rows.start()
    get_fields = pltpu.make_async_copy(fields_hbm.at[0], fields_out, sem.at[1])
    get_fields.start()
    get_bias = pltpu.make_async_copy(bias_hbm, bias, sem.at[2])
    get_bias.start()
    more = [pltpu.make_async_copy(weights_hbm.at[t], taps[t], sem.at[3 + t]) for t in range(9)]
    for k in range(SLOTS):
        for h in range(2):
            source = cot_hbm.at[0, k, :, h * 128 : h * 128 + 128]
            more.append(pltpu.make_async_copy(source, halves[k][h], sem.at[12 + 2 * k + h]))
    for copy in more:
        copy.start()
    get_rows.wait()
    position = lax.axis_index("tiles")
    plans = halo_plans(count)
    for plan, out in zip(plans, maps):
        out[...] = halo_map(rows, count, position, plan)
    put_rows = pltpu.make_async_copy(rows, rows_out, sem.at[0])
    put_rows.start()
    get_bias.wait()
    line = jnp.concatenate([bias[...], jnp.zeros((1, 128 - own), F32)], axis=1)
    high = line.astype(BF16).astype(F32)
    middle = (line - high).astype(BF16).astype(F32)
    low = line - high - middle
    pieces[...] = jnp.concatenate([high, middle, low, jnp.zeros((13, 128), F32)], axis=0).astype(BF16)
    get_fields.wait()
    cells = jnp.concatenate([fields_out[k] for k in range(SLOTS)], axis=1)
    for out, hits in zip(outs, maps):
        out[...] = dot(cells, hits[...]).astype(BF16)
    for copy in more:
        copy.wait()
    put_rows.wait()


def flag(condition):
    return jnp.where(condition, 1.0, 0.0).astype(F32)


def slot_flags(rows):
    position = lax.axis_index("tiles")
    row = [rows[position, k] for k in range(SLOTS)]
    full = [flag(r >= 0) for r in row]
    at_top = [flag(r == 2 * SLOTS - 1) for r in row]
    above = [[flag((row[k] >= 0) & (row[l] == row[k] + 1)) for l in range(SLOTS)] for k in range(SLOTS)]
    return full, at_top, above


def turn(stack, turned):
    own = stack.shape[0] // 3
    start = pl.multiple_of(lax.axis_index("chan") * own, own)
    turned[...] = jnp.transpose(stack.astype(F32))
    return jnp.concatenate([turned[pl.ds(b * C + start, own), :] for b in range(3)], axis=0).astype(BF16)


def stack_of(taps):
    return jnp.concatenate(
        [jnp.concatenate([taps[3 * a + b][...] for b in range(3)], axis=1) for a in range(3)], axis=0
    )


def window_kernel(rows, fields, shared, windows, spreads, gathers, kernel, back_kernel, turned):
    own = kernel.shape[0] // 3
    full, _, above = slot_flags(rows)
    column = iota((1, FRAME), 1) % TS
    lane128 = iota((1, 128), 1)
    tiles = [fields[k].astype(F32) * full[k] for k in range(SLOTS)]
    for k in range(SLOTS):
        north = jnp.zeros((C, 128), F32)
        south = jnp.zeros((C, 128), F32)
        for l in range(SLOTS):
            if l != k:
                north = north + above[k][l] * tiles[l][:, :128]
                south = south + above[l][k] * tiles[l][:, 128:]
        ends = jnp.where(lane128 < TS, north, jnp.where(lane128 >= 128 - TS, south, 0.0))
        centre = jnp.concatenate([tiles[k], ends], axis=1)
        windows[k, :C] = jnp.where(column == 0, 0.0, pltpu.roll(centre, 1, 1)).astype(BF16)
        windows[k, C : 2 * C] = centre.astype(BF16)
        windows[k, 2 * C :] = jnp.where(column == TS - 1, 0.0, pltpu.roll(centre, FRAME - 1, 1)).astype(BF16)
    for refs, shape, halo_dim in ((spreads, (128, FRAME), 0), (gathers, (FRAME, 128), 1)):
        p_at = iota(shape, halo_dim)
        frame_lane = iota(shape, 1 - halo_dim)
        for side in range(2):
            for k in range(SLOTS):
                p = p_at - (side * EAST + k * EDGE)
                spot = jnp.where(p == 0, FRAME - TS, TS * (p - 1)) + side * (TS - 1)
                hits = (p >= 0) & (p < EDGE) & (frame_lane == spot)
                refs[side, k] = jnp.where(hits, 1.0, 0.0).astype(BF16)
    stack = stack_of(message_views(shared, own)[0])
    kernel[...] = stack
    back_kernel[...] = turn(stack, turned)


def column_of(pieces, own):
    eye = iota((own, 128), 0) == iota((own, 128), 1)
    parts = pieces[...].astype(F32)
    line = parts[0:1] + parts[1:2] + parts[2:3]
    return jnp.sum(jnp.where(eye, line, 0.0), axis=1, keepdims=True)


def activation(kernel, window, bias_column, up):
    own = bias_column.shape[0]
    sums = dot(kernel, window)
    pre = (
        pltpu.roll(sums[:own], TS, 1)[:, :CELLS]
        + sums[own : 2 * own, :CELLS]
        + pltpu.roll(sums[2 * own :], FRAME - TS, 1)[:, :CELLS]
        + bias_column
    )
    square = pre * pre
    tanh = jnp.tanh(GELU_C * (pre * (1.0 + GELU_K * square)))
    half = 0.5 + 0.5 * tanh
    slope = half + (0.5 * pre) * (1.0 - tanh * tanh) * (GELU_C + (3.0 * GELU_C * GELU_K) * square)
    return pre * half, (up * slope).astype(BF16).astype(F32)


def frame_of(slopes):
    own = slopes.shape[0]
    wide = jnp.concatenate([slopes, jnp.zeros((own, FRAME - CELLS), F32)], axis=1)
    return jnp.concatenate([pltpu.roll(wide, FRAME - TS, 1), wide, pltpu.roll(wide, TS, 1)], axis=0).astype(BF16)


def upstream_of(halves, k, full):
    return jnp.concatenate([halves[k][0][...], halves[k][1][...]], axis=1).astype(F32) * full[k]


def forward_kernel(rows, fields, shared, kernel, spreads, windows, *refs, n_halos, half_rows):
    halos = refs[:n_halos]
    full_windows, frames, result, keep, send = refs[n_halos:]
    own = kernel.shape[0] // 3
    full, at_top, _ = slot_flags(rows)
    start = pl.multiple_of(lax.axis_index("chan") * own, own)
    rep = lax.axis_index("rep")
    lane128 = iota((1, 128), 1)
    _, halves, pieces = message_views(shared, own)
    bias_column = column_of(pieces, own)
    halo = halos[0][...].astype(F32)
    for ref in halos[1:]:
        halo = halo + ref[...].astype(F32)
    turned = pltpu.roll(halo, 128 - FOLD, 1)
    fold = jnp.where(lane128 < TS, turned, 0.0)
    fold_left = jnp.where((lane128 > 0) & (lane128 < TS), pltpu.roll(turned, 1, 1), 0.0)
    fold_right = jnp.where(lane128 < TS - 1, pltpu.roll(turned, 127, 1), 0.0)
    halo = halo.astype(BF16)
    grads = jnp.zeros((3 * own, 3 * C), F32)
    slope_sum = jnp.zeros((own, CELLS), F32)
    for k in range(SLOTS):
        west = dot(halo, spreads[0, k])
        east = dot(halo, spreads[1, k])
        rest = jnp.zeros((C, CELLS), F32)
        left = windows[k, :C] + (west + jnp.concatenate([rest, at_top[k] * fold_left], axis=1)).astype(BF16)
        right = windows[k, 2 * C :] + (east + jnp.concatenate([rest, at_top[k] * fold_right], axis=1)).astype(BF16)
        centre = windows[k, C : 2 * C] + jnp.concatenate([rest, at_top[k] * fold], axis=1).astype(BF16)
        window = jnp.concatenate([left, centre, right], axis=0)
        full_windows[k] = window
        up = upstream_of(halves, k, full)
        gelu, slopes = activation(kernel[...], window, bias_column, up)
        result[k] = (full[k] * (fields[k, pl.ds(start, own), :].astype(F32) + gelu)).astype(BF16)
        slope_sum = slope_sum + slopes
        frame = frame_of(slopes)
        frames[k] = frame
        grads = grads + dot(frame, window, ((1,), (1,)))
    blocks = [grads[a * own : (a + 1) * own, b * C : (b + 1) * C] for a in range(3) for b in range(3)]
    eye = iota((own, 128), 0) == iota((own, 128), 1)
    bias_line = jnp.sum(jnp.where(eye, jnp.sum(slope_sum, axis=1, keepdims=True), 0.0), axis=0, keepdims=True)
    blocks.append(bias_line)
    blocks.append(jnp.zeros((2 * half_rows - 9 * own - 1, 128), F32))
    sums = jnp.concatenate(blocks, axis=0)
    low, high = sums[:half_rows], sums[half_rows:]
    keep[...] = jnp.where(rep == 0, low, high)
    send[...] = jnp.where(rep == 0, high, low)


def other_kernel(rows, windows, *refs):
    n = (len(refs) - 1) // 3
    turned = refs[-1]
    full = slot_flags(rows)[0]
    for ref, frames, back_kernel in zip(refs[:n], refs[n : 2 * n], refs[2 * n : 3 * n]):
        own = back_kernel.shape[0] // 3
        taps, halves, pieces = message_views(ref, own)
        stack = stack_of(taps)
        bias_column = column_of(pieces, own)
        for k in range(SLOTS):
            _, slopes = activation(stack, windows[k], bias_column, upstream_of(halves, k, full))
            frames[k] = frame_of(slopes)
        back_kernel[...] = turn(stack, turned)


def backward_kernel(rows, shared, gathers, result, *refs):
    base, edges, result_out, sem = refs[-4:]
    n = (len(refs) - 4) // 2
    frames, back_kernels = refs[:n], refs[n : 2 * n]
    own = back_kernels[0].shape[0] // 3
    put = pltpu.make_async_copy(result, result_out.at[0], sem)
    put.start()
    full, at_top, above = slot_flags(rows)
    column = iota((1, FRAME), 1) % TS
    lane128 = iota((1, 128), 1)
    edge_sum = jnp.zeros((own, 128), F32)
    pads = []
    for k in range(SLOTS):
        spread = dot(back_kernels[0][...], frames[0][k])
        for frame, back_kernel in zip(frames[1:], back_kernels[1:]):
            spread = spread + dot(back_kernel[...], frame[k])
        first, second, third = spread[:own], spread[own : 2 * own], spread[2 * own :]
        pad = (
            second
            + jnp.where(column < TS - 1, pltpu.roll(first, FRAME - 1, 1), 0.0)
            + jnp.where(column > 0, pltpu.roll(third, 1, 1), 0.0)
        )
        pads.append(pad)
        edge_sum = edge_sum + dot(first.astype(BF16), gathers[0, k])
        edge_sum = edge_sum + dot(third.astype(BF16), gathers[1, k])
        crest = jnp.where(lane128 < TS, pad[:, CELLS:], 0.0) * at_top[k]
        edge_sum = edge_sum + pltpu.roll(crest, FOLD, 1)
    edges[...] = edge_sum.astype(BF16)
    _, halves, _ = message_views(shared, own)
    for k in range(SLOTS):
        first = pads[k][:, :128]
        second = pads[k][:, 128:CELLS]
        for l in range(SLOTS):
            if l != k:
                ends = pads[l][:, CELLS:]
                first = first + jnp.where(lane128 < TS, ends, 0.0) * above[l][k]
                second = second + jnp.where(lane128 >= 128 - TS, ends, 0.0) * above[k][l]
        base[k] = upstream_of(halves, k, full) + jnp.concatenate([first, second], axis=1)
    put.wait()


def finish_kernel(base, *refs):
    out = refs[-1]
    n = len(refs) // 2
    total = None
    for received, hits in zip(refs[:n], refs[n:]):
        part = dot(received[...], hits[...], ((1,), (1,)))
        total = part if total is None else total + part
    for k in range(SLOTS):
        out[0, k] = (base[k] + total[:, k * CELLS : (k + 1) * CELLS]).astype(BF16)


def gather_kernel(mine, theirs, weights_out, bias_out):
    rep = lax.axis_index("rep")
    own = weights_out.shape[1]
    low = jnp.where(rep == 0, mine[...], theirs[...])
    high = jnp.where(rep == 0, theirs[...], mine[...])
    sums = jnp.concatenate([low, high], axis=0)
    for t in range(9):
        weights_out[t] = sums[t * own : (t + 1) * own]
    bias_out[...] = sums[9 * own : 9 * own + 1, :own]


SMEM = pl.BlockSpec(memory_space=pltpu.SMEM)
VMEM = pl.BlockSpec(memory_space=pltpu.VMEM)
HBM = pl.BlockSpec(memory_space=pltpu.HBM)


def call(kernel, specs, outs, scratch=(), out_specs=None):
    return pl.pallas_call(
        kernel,
        in_specs=specs,
        out_specs=out_specs or [VMEM] * len(outs),
        out_shape=outs,
        scratch_shapes=list(scratch),
        compiler_params=pltpu.CompilerParams(vmem_limit_bytes=40 << 20),
    )


def struct(shape, dtype):
    return jax.ShapeDtypeStruct(shape, dtype)


def on_device(fields, tile_rows, weights, bias, cotangent):
    own = weights.shape[1]
    count = lax.axis_size("tiles")
    chans = lax.axis_size("chan")
    reps = lax.axis_size("rep")
    plans = halo_plans(count)
    n = len(plans)
    shared_rows = 9 * own + 2 * SLOTS * own + 16
    half_rows = -(-(9 * own + 1) // 32) * 16
    swap = [(0, 1), (1, 0)]

    pinned = [
        pltpu.with_memory_space_constraint(x, pltpu.HBM)
        for x in (tile_rows, fields, weights, bias.reshape(1, own), cotangent)
    ]
    heights = [2 * C, C, C] if count == 4 else [C] * n
    rows, tiles, shared, *packed = call(
        lambda *refs: pack_kernel(*refs, count=count),
        [HBM] * 5,
        [
            struct(tile_rows.shape, jnp.int32),
            struct((SLOTS, C, CELLS), BF16),
            struct((shared_rows, 128), BF16),
        ]
        + [struct((SLOTS * CELLS, 128), BF16)] * n
        + [struct((height, 128), BF16) for height in heights],
        [
            pltpu.SMEM(tile_rows.shape, jnp.int32),
            pltpu.VMEM((1, own), F32),
            pltpu.SemaphoreType.DMA((12 + 2 * SLOTS,)),
        ],
    )(*pinned)
    maps, messages = packed[:n], packed[n:]

    def move(x, route):
        return lax.ppermute(x, "tiles", [(i, route(i)) for i in range(count)])

    if count == 4:
        near = move(messages[0], lambda d: d ^ 1)
        halos = [near[:C], move(messages[1] + near[C:], lambda d: d ^ 2), messages[2]]
    else:
        halos = [move(message, route) for message, (route, _) in zip(messages, plans)]
    others = [lax.ppermute(shared, "chan", [(i, (i + s) % chans) for i in range(chans)]) for s in range(1, chans)]

    windows, spreads, gathers, kernel, back_kernel = call(
        window_kernel,
        [SMEM] + [VMEM] * 2,
        [
            struct((SLOTS, 3 * C, FRAME), BF16),
            struct((2, SLOTS, 128, FRAME), BF16),
            struct((2, SLOTS, FRAME, 128), BF16),
            struct((3 * own, 3 * C), BF16),
            struct((3 * own, 3 * own), BF16),
        ],
        [pltpu.VMEM((3 * C, 3 * own), F32)],
    )(rows, tiles, shared)

    windows, frames, result, keep, send = call(
        lambda *refs: forward_kernel(*refs, n_halos=len(halos), half_rows=half_rows),
        [SMEM] + [VMEM] * (5 + len(halos)),
        [
            struct((SLOTS, 3 * C, FRAME), BF16),
            struct((SLOTS, 3 * own, FRAME), BF16),
            struct((SLOTS, own, CELLS), BF16),
            struct((half_rows, 128), F32),
            struct((half_rows, 128), F32),
        ],
    )(rows, tiles, shared, kernel, spreads, windows, *halos)

    send, others = lax.optimization_barrier((send, others))
    sums = keep + lax.ppermute(send, "rep", swap)
    other_frames = call(
        other_kernel,
        [SMEM, VMEM] + [VMEM] * len(others),
        [struct((SLOTS, 3 * own, FRAME), BF16)] * len(others) + [struct((3 * own, 3 * own), BF16)] * len(others),
        [pltpu.VMEM((3 * C, 3 * own), F32)],
    )(rows, windows, *others)
    other_frames, other_back = other_frames[: len(others)], other_frames[len(others) :]
    rounded = sums.astype(BF16)
    frames, rounded, other_frames = lax.optimization_barrier((frames, rounded, other_frames))

    base, edges, result = call(
        backward_kernel,
        [SMEM] + [VMEM] * (5 + 2 * len(others)),
        [
            struct((SLOTS, own, CELLS), F32),
            struct((own, 128), BF16),
            struct((1, SLOTS, own, CELLS), BF16),
        ],
        [pltpu.SemaphoreType.DMA],
        out_specs=[VMEM, VMEM, HBM],
    )(rows, shared, gathers, result, frames, *other_frames, back_kernel, *other_back)

    if count == 4:
        across = move(edges, lambda d: d ^ 2)
        other = move(rounded, lambda d: d ^ 2)
        rounded = (rounded.astype(F32) + other.astype(F32)).astype(BF16)
        rounded, across = lax.optimization_barrier((rounded, across))
        both = move(jnp.concatenate([rounded, edges, across], axis=0), lambda d: d ^ 1)
        sums = rounded.astype(F32) + both[:half_rows].astype(F32)
        returned = [both[half_rows : half_rows + own], both[half_rows + own :], across, edges]
    else:
        for step in range(count.bit_length() - 1):
            other = move(rounded, lambda d: d ^ (1 << step))
            sums = rounded.astype(F32) + other.astype(F32)
            rounded = sums.astype(BF16)
        returned = [
            lax.ppermute(edges, "tiles", [(route(j), j) for j in range(count)]) for route, _ in plans
        ]
    grad_scale = 1.0 / math.sqrt(reps * fields.shape[0] * count * SLOTS * CELLS)
    sums = sums * grad_scale
    grad_fields = call(
        finish_kernel,
        [VMEM] * (1 + 2 * n),
        [struct((1, SLOTS, own, CELLS), BF16)],
    )(base, *returned, *maps)[0]
    grad_weights, grad_bias = call(
        gather_kernel,
        [VMEM, VMEM],
        [struct((9, own, C), F32), struct((1, own), F32)],
    )(sums, lax.ppermute(sums, "rep", swap))
    return (result, grad_fields, grad_weights, grad_bias.reshape(own))


def solution(mesh):
    in_specs = (
        P(("groups", "rep"), "tiles", None, None),
        P(),
        P(None, "chan", None),
        P("chan"),
        P(("groups", "rep"), "tiles", "chan", None),
    )
    out_specs = (
        P(("groups", "rep"), "tiles", "chan", None),
        P(("groups", "rep"), "tiles", "chan", None),
        P("groups", "chan", None),
        P(("groups", "chan")),
    )
    return jax.shard_map(
        on_device, mesh=mesh, in_specs=in_specs, out_specs=out_specs, check_vma=False
    )
```

```python
import math

import jax
import jax.numpy as jnp
from jax import lax
from jax.experimental import pallas as pl
from jax.experimental.pallas import tpu as pltpu
from jax.sharding import PartitionSpec as P

C = 128
TS = 16
SLOTS = 3
CELLS = TS * TS
FRAME = 384
EDGE = TS + 2
EAST = SLOTS * EDGE
FOLD = 2 * SLOTS * EDGE
F32 = jnp.float32
BF16 = jnp.bfloat16
GELU_C = math.sqrt(2.0 / math.pi)
GELU_K = 0.044715


def iota(shape, dim):
    return lax.broadcasted_iota(jnp.int32, shape, dim)


def halo_plans(count):
    if count == 4:
        return [
            (lambda d: d ^ 1, ("side",)),
            (lambda d: 3 - d, ("side", "fold")),
            (lambda d: d ^ 2, ("corner",)),
            (None, ("corner",)),
        ]
    return [
        (lambda d: (d + 1) % count, ("west",)),
        (lambda d: (d + count - 1) % count, ("east",)),
        (lambda d: count - 1 - d, ("fold",)),
        (lambda d: (count - d) % count, ("corner_west",)),
        (lambda d: (2 * count - 2 - d) % count, ("corner_east",)),
    ]


def halo_sources(rows, count, source, target, roles):
    lane = iota((8, 128), 1)
    top = 2 * SLOTS - 1
    east = (lane >= EAST) & (lane < FOLD)
    at = lane - jnp.where(east, EAST, 0)
    k = jnp.where(at >= EDGE, 1, 0) + jnp.where(at >= 2 * EDGE, 1, 0)
    p = at - EDGE * k
    rim = lane < FOLD
    row = jnp.where(k == 0, rows[target, 0], jnp.where(k == 1, rows[target, 1], rows[target, 2]))
    row = jnp.where(rim, row, -1)
    src = jnp.full((8, 128), -1, jnp.int32)
    sides = [name for name in ("west", "east") if name in roles or "side" in roles]
    if sides:
        wanted = row + jnp.where(p == TS + 1, 1, 0) - jnp.where(p == 0, 1, 0)
        slot = jnp.full((8, 128), -1, jnp.int32)
        present = (p > 0) & (p <= TS)
        for l in range(SLOTS):
            slot = jnp.where(wanted == rows[source, l], l, slot)
            present = present | (wanted == rows[target, l])
        cell = jnp.where(p == 0, CELLS - TS, jnp.where(p == TS + 1, 0, TS * (p - 1))) + jnp.where(east, 0, TS - 1)
        good = present & (row >= 0) & (wanted >= 0) & (slot >= 0)
        from_west = target == (source + 1) % count if "west" in sides else False
        from_east = target == (source + count - 1) % count if "east" in sides else False
        good = good & ((jnp.logical_not(east) & from_west) | (east & from_east))
        src = jnp.where(good, slot * CELLS + cell, src)

    def top_slot(column):
        found = jnp.int32(-1)
        for l in range(SLOTS):
            found = jnp.where(rows[column, l] == top, l, found)
        return found

    if sides and len(sides) == len(roles) and "side" not in roles or roles == ("side",):
        return src
    mine = top_slot(source)
    if "fold" in roles:
        good = (lane >= FOLD) & (lane < FOLD + TS) & (mine >= 0) & (target == count - 1 - source)
        src = jnp.where(good, mine * CELLS + (CELLS - 1 + FOLD) - lane, src)
    corners = [name for name in ("west", "east") if "corner" in roles or f"corner_{name}" in roles]
    if corners:
        good = (row == top) & (p == TS + 1) & (mine >= 0) & (top_slot(count - 1 - target) >= 0)
        from_west = target == (count - source) % count if "west" in corners else False
        from_east = target == (2 * count - 2 - source) % count if "east" in corners else False
        good = good & ((jnp.logical_not(east) & from_west) | (east & from_east))
        src = jnp.where(good, mine * CELLS + CELLS - TS + jnp.where(east, TS - 1, 0), src)
    return src


def halo_map(rows, count, source, plan):
    route, roles = plan
    target = source if route is None else route(source)
    src = halo_sources(rows, count, source, target, roles)
    hits = iota((SLOTS * CELLS, 128), 0) == src[0:1, :]
    return jnp.where(hits, 1.0, 0.0).astype(BF16)


def dot(lhs, rhs, dims=((1,), (0,))):
    return lax.dot_general(lhs, rhs, (dims, ((), ())), preferred_element_type=F32)


def message_views(ref, own):
    taps = [ref.at[t * own : (t + 1) * own] for t in range(9)]
    base = 9 * own
    halves = [
        [ref.at[base + (2 * k + h) * own : base + (2 * k + h + 1) * own] for h in range(2)] for k in range(SLOTS)
    ]
    at = base + 2 * SLOTS * own
    return taps, halves, ref.at[at : at + 16]


def pack_kernel(rows_hbm, fields_hbm, weights_hbm, bias_hbm, cot_hbm, *refs, count):
    n = len(halo_plans(count))
    rows_out, fields_out, shared = refs[:3]
    maps = refs[3 : 3 + n]
    outs = refs[3 + n : -3]
    if count == 4:
        outs = [outs[0].at[:C, :], outs[0].at[C:, :], *outs[1:]]
    rows, bias, sem = refs[-3:]
    own = weights_hbm.shape[1]
    taps, halves, pieces = message_views(shared, own)
    get_rows = pltpu.make_async_copy(rows_hbm, rows, sem.at[0])
    get_rows.start()
    get_fields = pltpu.make_async_copy(fields_hbm.at[0], fields_out, sem.at[1])
    get_fields.start()
    get_bias = pltpu.make_async_copy(bias_hbm, bias, sem.at[2])
    get_bias.start()
    more = [pltpu.make_async_copy(weights_hbm.at[t], taps[t], sem.at[3 + t]) for t in range(9)]
    for k in range(SLOTS):
        for h in range(2):
            source = cot_hbm.at[0, k, :, h * 128 : h * 128 + 128]
            more.append(pltpu.make_async_copy(source, halves[k][h], sem.at[12 + 2 * k + h]))
    for copy in more:
        copy.start()
    get_rows.wait()
    position = lax.axis_index("tiles")
    plans = halo_plans(count)
    for plan, out in zip(plans, maps):
        out[...] = halo_map(rows, count, position, plan)
    put_rows = pltpu.make_async_copy(rows, rows_out, sem.at[0])
    put_rows.start()
    get_bias.wait()
    line = jnp.concatenate([bias[...], jnp.zeros((1, 128 - own), F32)], axis=1)
    high = line.astype(BF16).astype(F32)
    middle = (line - high).astype(BF16).astype(F32)
    low = line - high - middle
    pieces[...] = jnp.concatenate([high, middle, low, jnp.zeros((13, 128), F32)], axis=0).astype(BF16)
    get_fields.wait()
    cells = jnp.concatenate([fields_out[k] for k in range(SLOTS)], axis=1)
    for out, hits in zip(outs, maps):
        out[...] = dot(cells, hits[...]).astype(BF16)
    for copy in more:
        copy.wait()
    put_rows.wait()


def flag(condition):
    return jnp.where(condition, 1.0, 0.0).astype(F32)


def slot_flags(rows):
    position = lax.axis_index("tiles")
    row = [rows[position, k] for k in range(SLOTS)]
    full = [flag(r >= 0) for r in row]
    at_top = [flag(r == 2 * SLOTS - 1) for r in row]
    above = [[flag((row[k] >= 0) & (row[l] == row[k] + 1)) for l in range(SLOTS)] for k in range(SLOTS)]
    return full, at_top, above


def turn(stack, turned):
    own = stack.shape[0] // 3
    start = pl.multiple_of(lax.axis_index("chan") * own, own)
    turned[...] = jnp.transpose(stack.astype(F32))
    return jnp.concatenate([turned[pl.ds(b * C + start, own), :] for b in range(3)], axis=0).astype(BF16)


def stack_of(taps):
    return jnp.concatenate(
        [jnp.concatenate([taps[3 * a + b][...] for b in range(3)], axis=1) for a in range(3)], axis=0
    )


def window_kernel(rows, fields, shared, windows, spreads, gathers, kernel, back_kernel, turned):
    own = kernel.shape[0] // 3
    full, _, above = slot_flags(rows)
    column = iota((1, FRAME), 1) % TS
    lane128 = iota((1, 128), 1)
    tiles = [fields[k].astype(F32) * full[k] for k in range(SLOTS)]
    for k in range(SLOTS):
        north = jnp.zeros((C, 128), F32)
        south = jnp.zeros((C, 128), F32)
        for l in range(SLOTS):
            if l != k:
                north = north + above[k][l] * tiles[l][:, :128]
                south = south + above[l][k] * tiles[l][:, 128:]
        ends = jnp.where(lane128 < TS, north, jnp.where(lane128 >= 128 - TS, south, 0.0))
        centre = jnp.concatenate([tiles[k], ends], axis=1)
        windows[k, :C] = jnp.where(column == 0, 0.0, pltpu.roll(centre, 1, 1)).astype(BF16)
        windows[k, C : 2 * C] = centre.astype(BF16)
        windows[k, 2 * C :] = jnp.where(column == TS - 1, 0.0, pltpu.roll(centre, FRAME - 1, 1)).astype(BF16)
    for refs, shape, halo_dim in ((spreads, (128, FRAME), 0), (gathers, (FRAME, 128), 1)):
        p_at = iota(shape, halo_dim)
        frame_lane = iota(shape, 1 - halo_dim)
        for side in range(2):
            for k in range(SLOTS):
                p = p_at - (side * EAST + k * EDGE)
                spot = jnp.where(p == 0, FRAME - TS, TS * (p - 1)) + side * (TS - 1)
                hits = (p >= 0) & (p < EDGE) & (frame_lane == spot)
                refs[side, k] = jnp.where(hits, 1.0, 0.0).astype(BF16)
    stack = stack_of(message_views(shared, own)[0])
    kernel[...] = stack
    back_kernel[...] = turn(stack, turned)


def column_of(pieces, own):
    eye = iota((own, 128), 0) == iota((own, 128), 1)
    parts = pieces[...].astype(F32)
    line = parts[0:1] + parts[1:2] + parts[2:3]
    return jnp.sum(jnp.where(eye, line, 0.0), axis=1, keepdims=True)


def activation(kernel, window, bias_column, up):
    own = bias_column.shape[0]
    sums = dot(kernel, window)
    pre = (
        pltpu.roll(sums[:own], TS, 1)[:, :CELLS]
        + sums[own : 2 * own, :CELLS]
        + pltpu.roll(sums[2 * own :], FRAME - TS, 1)[:, :CELLS]
        + bias_column
    )
    square = pre * pre
    tanh = jnp.tanh(GELU_C * (pre * (1.0 + GELU_K * square)))
    half = 0.5 + 0.5 * tanh
    slope = half + (0.5 * pre) * (1.0 - tanh * tanh) * (GELU_C + (3.0 * GELU_C * GELU_K) * square)
    return pre * half, (up * slope).astype(BF16).astype(F32)


def frame_of(slopes):
    own = slopes.shape[0]
    wide = jnp.concatenate([slopes, jnp.zeros((own, FRAME - CELLS), F32)], axis=1)
    return jnp.concatenate([pltpu.roll(wide, FRAME - TS, 1), wide, pltpu.roll(wide, TS, 1)], axis=0).astype(BF16)


def upstream_of(halves, k, full):
    return jnp.concatenate([halves[k][0][...], halves[k][1][...]], axis=1).astype(F32) * full[k]


def half_of(count):
    position = lax.axis_index("tiles")
    rep = lax.axis_index("rep")
    if count == 4:
        return (rep + position + position // 2) % 2
    return rep


def forward_kernel(rows, fields, shared, kernel, spreads, windows, *refs, n_halos, half_rows, count):
    halos = refs[:n_halos]
    full_windows, frames, result, keep, send = refs[n_halos:]
    own = kernel.shape[0] // 3
    full, at_top, _ = slot_flags(rows)
    start = pl.multiple_of(lax.axis_index("chan") * own, own)
    half = half_of(count)
    lane128 = iota((1, 128), 1)
    _, halves, pieces = message_views(shared, own)
    bias_column = column_of(pieces, own)
    halo = halos[0][...].astype(F32)
    for ref in halos[1:]:
        halo = halo + ref[...].astype(F32)
    turned = pltpu.roll(halo, 128 - FOLD, 1)
    fold = jnp.where(lane128 < TS, turned, 0.0)
    fold_left = jnp.where((lane128 > 0) & (lane128 < TS), pltpu.roll(turned, 1, 1), 0.0)
    fold_right = jnp.where(lane128 < TS - 1, pltpu.roll(turned, 127, 1), 0.0)
    halo = halo.astype(BF16)
    grads = jnp.zeros((3 * own, 3 * C), F32)
    slope_sum = jnp.zeros((own, CELLS), F32)
    for k in range(SLOTS):
        west = dot(halo, spreads[0, k])
        east = dot(halo, spreads[1, k])
        rest = jnp.zeros((C, CELLS), F32)
        left = windows[k, :C] + (west + jnp.concatenate([rest, at_top[k] * fold_left], axis=1)).astype(BF16)
        right = windows[k, 2 * C :] + (east + jnp.concatenate([rest, at_top[k] * fold_right], axis=1)).astype(BF16)
        centre = windows[k, C : 2 * C] + jnp.concatenate([rest, at_top[k] * fold], axis=1).astype(BF16)
        window = jnp.concatenate([left, centre, right], axis=0)
        full_windows[k] = window
        up = upstream_of(halves, k, full)
        gelu, slopes = activation(kernel[...], window, bias_column, up)
        result[k] = (full[k] * (fields[k, pl.ds(start, own), :].astype(F32) + gelu)).astype(BF16)
        slope_sum = slope_sum + slopes
        frame = frame_of(slopes)
        frames[k] = frame
        grads = grads + dot(frame, window, ((1,), (1,)))
    blocks = [grads[a * own : (a + 1) * own, b * C : (b + 1) * C] for a in range(3) for b in range(3)]
    eye = iota((own, 128), 0) == iota((own, 128), 1)
    bias_line = jnp.sum(jnp.where(eye, jnp.sum(slope_sum, axis=1, keepdims=True), 0.0), axis=0, keepdims=True)
    blocks.append(bias_line)
    blocks.append(jnp.zeros((2 * half_rows - 9 * own - 1, 128), F32))
    sums = jnp.concatenate(blocks, axis=0)
    low, high = sums[:half_rows], sums[half_rows:]
    keep[...] = jnp.where(half == 0, low, high)
    send[...] = jnp.where(half == 0, high, low)


def other_kernel(rows, windows, *refs):
    n = (len(refs) - 1) // 3
    turned = refs[-1]
    full = slot_flags(rows)[0]
    for ref, frames, back_kernel in zip(refs[:n], refs[n : 2 * n], refs[2 * n : 3 * n]):
        own = back_kernel.shape[0] // 3
        taps, halves, pieces = message_views(ref, own)
        stack = stack_of(taps)
        bias_column = column_of(pieces, own)
        for k in range(SLOTS):
            _, slopes = activation(stack, windows[k], bias_column, upstream_of(halves, k, full))
            frames[k] = frame_of(slopes)
        back_kernel[...] = turn(stack, turned)


def backward_kernel(rows, shared, gathers, result, *refs):
    base, edges, result_out, sem = refs[-4:]
    n = (len(refs) - 4) // 2
    frames, back_kernels = refs[:n], refs[n : 2 * n]
    own = back_kernels[0].shape[0] // 3
    put = pltpu.make_async_copy(result, result_out.at[0], sem)
    put.start()
    full, at_top, above = slot_flags(rows)
    column = iota((1, FRAME), 1) % TS
    lane128 = iota((1, 128), 1)
    edge_sum = jnp.zeros((own, 128), F32)
    pads = []
    for k in range(SLOTS):
        spread = dot(back_kernels[0][...], frames[0][k])
        for frame, back_kernel in zip(frames[1:], back_kernels[1:]):
            spread = spread + dot(back_kernel[...], frame[k])
        first, second, third = spread[:own], spread[own : 2 * own], spread[2 * own :]
        pad = (
            second
            + jnp.where(column < TS - 1, pltpu.roll(first, FRAME - 1, 1), 0.0)
            + jnp.where(column > 0, pltpu.roll(third, 1, 1), 0.0)
        )
        pads.append(pad)
        edge_sum = edge_sum + dot(first.astype(BF16), gathers[0, k])
        edge_sum = edge_sum + dot(third.astype(BF16), gathers[1, k])
        crest = jnp.where(lane128 < TS, pad[:, CELLS:], 0.0) * at_top[k]
        edge_sum = edge_sum + pltpu.roll(crest, FOLD, 1)
    edges[...] = edge_sum.astype(BF16)
    _, halves, _ = message_views(shared, own)
    for k in range(SLOTS):
        first = pads[k][:, :128]
        second = pads[k][:, 128:CELLS]
        for l in range(SLOTS):
            if l != k:
                ends = pads[l][:, CELLS:]
                first = first + jnp.where(lane128 < TS, ends, 0.0) * above[l][k]
                second = second + jnp.where(lane128 >= 128 - TS, ends, 0.0) * above[k][l]
        base[k] = upstream_of(halves, k, full) + jnp.concatenate([first, second], axis=1)
    put.wait()


def finish_kernel(base, *refs):
    out = refs[-1]
    n = len(refs) // 2
    total = None
    for received, hits in zip(refs[:n], refs[n:]):
        part = dot(received[...], hits[...], ((1,), (1,)))
        total = part if total is None else total + part
    for k in range(SLOTS):
        out[0, k] = (base[k] + total[:, k * CELLS : (k + 1) * CELLS]).astype(BF16)


def gather_kernel(mine, theirs, weights_out, bias_out, *, count):
    half = half_of(count)
    own = weights_out.shape[1]
    low = jnp.where(half == 0, mine[...], theirs[...])
    high = jnp.where(half == 0, theirs[...], mine[...])
    sums = jnp.concatenate([low, high], axis=0)
    for t in range(9):
        weights_out[t] = sums[t * own : (t + 1) * own]
    bias_out[...] = sums[9 * own : 9 * own + 1, :own]


SMEM = pl.BlockSpec(memory_space=pltpu.SMEM)
VMEM = pl.BlockSpec(memory_space=pltpu.VMEM)
HBM = pl.BlockSpec(memory_space=pltpu.HBM)


def call(kernel, specs, outs, scratch=(), out_specs=None):
    return pl.pallas_call(
        kernel,
        in_specs=specs,
        out_specs=out_specs or [VMEM] * len(outs),
        out_shape=outs,
        scratch_shapes=list(scratch),
        compiler_params=pltpu.CompilerParams(vmem_limit_bytes=40 << 20),
    )


def struct(shape, dtype):
    return jax.ShapeDtypeStruct(shape, dtype)


def on_device(fields, tile_rows, weights, bias, cotangent):
    own = weights.shape[1]
    count = lax.axis_size("tiles")
    chans = lax.axis_size("chan")
    reps = lax.axis_size("rep")
    plans = halo_plans(count)
    n = len(plans)
    shared_rows = 9 * own + 2 * SLOTS * own + 16
    half_rows = -(-(9 * own + 1) // 32) * 16
    swap = [(0, 1), (1, 0)]

    pinned = [
        pltpu.with_memory_space_constraint(x, pltpu.HBM)
        for x in (tile_rows, fields, weights, bias.reshape(1, own), cotangent)
    ]
    heights = [2 * C, C, C] if count == 4 else [C] * n
    rows, tiles, shared, *packed = call(
        lambda *refs: pack_kernel(*refs, count=count),
        [HBM] * 5,
        [
            struct(tile_rows.shape, jnp.int32),
            struct((SLOTS, C, CELLS), BF16),
            struct((shared_rows, 128), BF16),
        ]
        + [struct((SLOTS * CELLS, 128), BF16)] * n
        + [struct((height, 128), BF16) for height in heights],
        [
            pltpu.SMEM(tile_rows.shape, jnp.int32),
            pltpu.VMEM((1, own), F32),
            pltpu.SemaphoreType.DMA((12 + 2 * SLOTS,)),
        ],
    )(*pinned)
    maps, messages = packed[:n], packed[n:]

    def move(x, route):
        return lax.ppermute(x, "tiles", [(i, route(i)) for i in range(count)])

    if count == 4:
        near = move(messages[0], lambda d: d ^ 1)
        halos = [near[:C], move(messages[1] + near[C:], lambda d: d ^ 2), messages[2]]
    else:
        halos = [move(message, route) for message, (route, _) in zip(messages, plans)]
    others = [lax.ppermute(shared, "chan", [(i, (i + s) % chans) for i in range(chans)]) for s in range(1, chans)]

    windows, spreads, gathers, kernel, back_kernel = call(
        window_kernel,
        [SMEM] + [VMEM] * 2,
        [
            struct((SLOTS, 3 * C, FRAME), BF16),
            struct((2, SLOTS, 128, FRAME), BF16),
            struct((2, SLOTS, FRAME, 128), BF16),
            struct((3 * own, 3 * C), BF16),
            struct((3 * own, 3 * own), BF16),
        ],
        [pltpu.VMEM((3 * C, 3 * own), F32)],
    )(rows, tiles, shared)

    windows, frames, result, keep, send = call(
        lambda *refs: forward_kernel(*refs, n_halos=len(halos), half_rows=half_rows, count=count),
        [SMEM] + [VMEM] * (5 + len(halos)),
        [
            struct((SLOTS, 3 * C, FRAME), BF16),
            struct((SLOTS, 3 * own, FRAME), BF16),
            struct((SLOTS, own, CELLS), BF16),
            struct((half_rows, 128), F32),
            struct((half_rows, 128), F32),
        ],
    )(rows, tiles, shared, kernel, spreads, windows, *halos)

    send, others = lax.optimization_barrier((send, others))
    sums = keep + lax.ppermute(send, "rep", swap)
    other_frames = call(
        other_kernel,
        [SMEM, VMEM] + [VMEM] * len(others),
        [struct((SLOTS, 3 * own, FRAME), BF16)] * len(others) + [struct((3 * own, 3 * own), BF16)] * len(others),
        [pltpu.VMEM((3 * C, 3 * own), F32)],
    )(rows, windows, *others)
    other_frames, other_back = other_frames[: len(others)], other_frames[len(others) :]
    rounded = sums.astype(BF16)
    frames, rounded, other_frames = lax.optimization_barrier((frames, rounded, other_frames))

    base, edges, result = call(
        backward_kernel,
        [SMEM] + [VMEM] * (5 + 2 * len(others)),
        [
            struct((SLOTS, own, CELLS), F32),
            struct((own, 128), BF16),
            struct((1, SLOTS, own, CELLS), BF16),
        ],
        [pltpu.SemaphoreType.DMA],
        out_specs=[VMEM, VMEM, HBM],
    )(rows, shared, gathers, result, frames, *other_frames, back_kernel, *other_back)

    if count == 4:

        def cross(x, route):
            pairs = [(2 * d + r, 2 * route(d) + 1 - r) for d in range(count) for r in range(2)]
            return lax.ppermute(x, ("tiles", "rep"), pairs)

        across = cross(edges, lambda d: d ^ 2)
        beside = lax.ppermute(edges, "rep", swap)
        other = cross(rounded, lambda d: d ^ 2)
        rounded = (rounded.astype(F32) + other.astype(F32)).astype(BF16)
        both = cross(jnp.concatenate([rounded, beside, across], axis=0), lambda d: d ^ 1)
        sums = rounded.astype(F32) + both[:half_rows].astype(F32)
        across = lax.ppermute(across, "rep", swap)
        returned = [both[half_rows : half_rows + own], both[half_rows + own :], across, edges]
    else:
        for step in range(count.bit_length() - 1):
            other = move(rounded, lambda d: d ^ (1 << step))
            sums = rounded.astype(F32) + other.astype(F32)
            rounded = sums.astype(BF16)
        returned = [
            lax.ppermute(edges, "tiles", [(route(j), j) for j in range(count)]) for route, _ in plans
        ]
    grad_scale = 1.0 / math.sqrt(reps * fields.shape[0] * count * SLOTS * CELLS)
    sums = sums * grad_scale
    grad_fields = call(
        finish_kernel,
        [VMEM] * (1 + 2 * n),
        [struct((1, SLOTS, own, CELLS), BF16)],
    )(base, *returned, *maps)[0]
    grad_weights, grad_bias = call(
        lambda *refs: gather_kernel(*refs, count=count),
        [VMEM, VMEM],
        [struct((9, own, C), F32), struct((1, own), F32)],
    )(sums, lax.ppermute(sums, "rep", swap))
    return (result, grad_fields, grad_weights, grad_bias.reshape(own))


def solution(mesh):
    in_specs = (
        P(("groups", "rep"), "tiles", None, None),
        P(),
        P(None, "chan", None),
        P("chan"),
        P(("groups", "rep"), "tiles", "chan", None),
    )
    out_specs = (
        P(("groups", "rep"), "tiles", "chan", None),
        P(("groups", "rep"), "tiles", "chan", None),
        P("groups", "chan", None),
        P(("groups", "chan")),
    )
    return jax.shard_map(
        on_device, mesh=mesh, in_specs=in_specs, out_specs=out_specs, check_vma=False
    )
```

```python
import math

import jax
import jax.numpy as jnp
from jax import lax
from jax.experimental import pallas as pl
from jax.experimental.pallas import tpu as pltpu
from jax.sharding import PartitionSpec as P

C = 128
TS = 16
SLOTS = 3
CELLS = TS * TS
FRAME = 384
EDGE = TS + 2
EAST = SLOTS * EDGE
FOLD = 2 * SLOTS * EDGE
F32 = jnp.float32
BF16 = jnp.bfloat16
GELU_C = math.sqrt(2.0 / math.pi)
GELU_K = 0.044715


def iota(shape, dim):
    return lax.broadcasted_iota(jnp.int32, shape, dim)


def halo_plans(count):
    if count == 4:
        return [
            (lambda d: 3 - d, ("side", "fold")),
            (lambda d: d ^ 2, ("corner",)),
            (lambda d: d ^ 1, ("side",)),
            (None, ("corner",)),
        ]
    return [
        (lambda d: (d + 1) % count, ("west",)),
        (lambda d: (d + count - 1) % count, ("east",)),
        (lambda d: count - 1 - d, ("fold",)),
        (lambda d: (count - d) % count, ("corner_west",)),
        (lambda d: (2 * count - 2 - d) % count, ("corner_east",)),
    ]


def halo_sources(rows, count, source, target, roles):
    lane = iota((8, 128), 1)
    top = 2 * SLOTS - 1
    east = (lane >= EAST) & (lane < FOLD)
    at = lane - jnp.where(east, EAST, 0)
    k = jnp.where(at >= EDGE, 1, 0) + jnp.where(at >= 2 * EDGE, 1, 0)
    p = at - EDGE * k
    rim = lane < FOLD
    row = jnp.where(k == 0, rows[target, 0], jnp.where(k == 1, rows[target, 1], rows[target, 2]))
    row = jnp.where(rim, row, -1)
    src = jnp.full((8, 128), -1, jnp.int32)
    sides = [name for name in ("west", "east") if name in roles or "side" in roles]
    if sides:
        wanted = row + jnp.where(p == TS + 1, 1, 0) - jnp.where(p == 0, 1, 0)
        slot = jnp.full((8, 128), -1, jnp.int32)
        present = (p > 0) & (p <= TS)
        for l in range(SLOTS):
            slot = jnp.where(wanted == rows[source, l], l, slot)
            present = present | (wanted == rows[target, l])
        cell = jnp.where(p == 0, CELLS - TS, jnp.where(p == TS + 1, 0, TS * (p - 1))) + jnp.where(east, 0, TS - 1)
        good = present & (row >= 0) & (wanted >= 0) & (slot >= 0)
        from_west = target == (source + 1) % count if "west" in sides else False
        from_east = target == (source + count - 1) % count if "east" in sides else False
        good = good & ((jnp.logical_not(east) & from_west) | (east & from_east))
        src = jnp.where(good, slot * CELLS + cell, src)

    def top_slot(column):
        found = jnp.int32(-1)
        for l in range(SLOTS):
            found = jnp.where(rows[column, l] == top, l, found)
        return found

    if sides and len(sides) == len(roles) and "side" not in roles or roles == ("side",):
        return src
    mine = top_slot(source)
    if "fold" in roles:
        good = (lane >= FOLD) & (lane < FOLD + TS) & (mine >= 0) & (target == count - 1 - source)
        src = jnp.where(good, mine * CELLS + (CELLS - 1 + FOLD) - lane, src)
    corners = [name for name in ("west", "east") if "corner" in roles or f"corner_{name}" in roles]
    if corners:
        good = (row == top) & (p == TS + 1) & (mine >= 0) & (top_slot(count - 1 - target) >= 0)
        from_west = target == (count - source) % count if "west" in corners else False
        from_east = target == (2 * count - 2 - source) % count if "east" in corners else False
        good = good & ((jnp.logical_not(east) & from_west) | (east & from_east))
        src = jnp.where(good, mine * CELLS + CELLS - TS + jnp.where(east, TS - 1, 0), src)
    return src


def halo_map(rows, count, source, plan):
    route, roles = plan
    target = source if route is None else route(source)
    src = halo_sources(rows, count, source, target, roles)
    hits = iota((SLOTS * CELLS, 128), 0) == src[0:1, :]
    return jnp.where(hits, 1.0, 0.0).astype(BF16)


def dot(lhs, rhs, dims=((1,), (0,))):
    return lax.dot_general(lhs, rhs, (dims, ((), ())), preferred_element_type=F32)


def message_views(ref, own):
    taps = [ref.at[t * own : (t + 1) * own] for t in range(9)]
    base = 9 * own
    halves = [
        [ref.at[base + (2 * k + h) * own : base + (2 * k + h + 1) * own] for h in range(2)] for k in range(SLOTS)
    ]
    at = base + 2 * SLOTS * own
    return taps, halves, ref.at[at : at + 16]


def pack_kernel(rows_hbm, fields_hbm, weights_hbm, bias_hbm, cot_hbm, *refs, count):
    n = len(halo_plans(count))
    rows_out, fields_out, shared = refs[:3]
    maps = refs[3 : 3 + n]
    outs = refs[3 + n : -3]
    rows, bias, sem = refs[-3:]
    own = weights_hbm.shape[1]
    taps, halves, pieces = message_views(shared, own)
    get_rows = pltpu.make_async_copy(rows_hbm, rows, sem.at[0])
    get_rows.start()
    get_fields = pltpu.make_async_copy(fields_hbm.at[0], fields_out, sem.at[1])
    get_fields.start()
    get_bias = pltpu.make_async_copy(bias_hbm, bias, sem.at[2])
    get_bias.start()
    more = [pltpu.make_async_copy(weights_hbm.at[t], taps[t], sem.at[3 + t]) for t in range(9)]
    for k in range(SLOTS):
        for h in range(2):
            source = cot_hbm.at[0, k, :, h * 128 : h * 128 + 128]
            more.append(pltpu.make_async_copy(source, halves[k][h], sem.at[12 + 2 * k + h]))
    for copy in more:
        copy.start()
    get_rows.wait()
    position = lax.axis_index("tiles")
    plans = halo_plans(count)
    for plan, out in zip(plans, maps):
        out[...] = halo_map(rows, count, position, plan)
    put_rows = pltpu.make_async_copy(rows, rows_out, sem.at[0])
    put_rows.start()
    get_bias.wait()
    line = jnp.concatenate([bias[...], jnp.zeros((1, 128 - own), F32)], axis=1)
    high = line.astype(BF16).astype(F32)
    middle = (line - high).astype(BF16).astype(F32)
    low = line - high - middle
    pieces[...] = jnp.concatenate([high, middle, low, jnp.zeros((13, 128), F32)], axis=0).astype(BF16)
    get_fields.wait()
    cells = jnp.concatenate([fields_out[k] for k in range(SLOTS)], axis=1)
    for out, hits in zip(outs, maps):
        out[...] = dot(cells, hits[...]).astype(BF16)
    for copy in more:
        copy.wait()
    put_rows.wait()


def flag(condition):
    return jnp.where(condition, 1.0, 0.0).astype(F32)


def slot_flags(rows):
    position = lax.axis_index("tiles")
    row = [rows[position, k] for k in range(SLOTS)]
    full = [flag(r >= 0) for r in row]
    at_top = [flag(r == 2 * SLOTS - 1) for r in row]
    above = [[flag((row[k] >= 0) & (row[l] == row[k] + 1)) for l in range(SLOTS)] for k in range(SLOTS)]
    return full, at_top, above


def turn(stack, turned):
    own = stack.shape[0] // 3
    start = pl.multiple_of(lax.axis_index("chan") * own, own)
    turned[...] = jnp.transpose(stack.astype(F32))
    return jnp.concatenate([turned[pl.ds(b * C + start, own), :] for b in range(3)], axis=0).astype(BF16)


def stack_of(taps):
    return jnp.concatenate(
        [jnp.concatenate([taps[3 * a + b][...] for b in range(3)], axis=1) for a in range(3)], axis=0
    )


def window_kernel(rows, fields, shared, windows, spreads, gathers, kernel, back_kernel, turned):
    own = kernel.shape[0] // 3
    full, _, above = slot_flags(rows)
    column = iota((1, FRAME), 1) % TS
    lane128 = iota((1, 128), 1)
    tiles = [fields[k].astype(F32) * full[k] for k in range(SLOTS)]
    for k in range(SLOTS):
        north = jnp.zeros((C, 128), F32)
        south = jnp.zeros((C, 128), F32)
        for l in range(SLOTS):
            if l != k:
                north = north + above[k][l] * tiles[l][:, :128]
                south = south + above[l][k] * tiles[l][:, 128:]
        ends = jnp.where(lane128 < TS, north, jnp.where(lane128 >= 128 - TS, south, 0.0))
        centre = jnp.concatenate([tiles[k], ends], axis=1)
        windows[k, :C] = jnp.where(column == 0, 0.0, pltpu.roll(centre, 1, 1)).astype(BF16)
        windows[k, C : 2 * C] = centre.astype(BF16)
        windows[k, 2 * C :] = jnp.where(column == TS - 1, 0.0, pltpu.roll(centre, FRAME - 1, 1)).astype(BF16)
    for refs, shape, halo_dim in ((spreads, (128, FRAME), 0), (gathers, (FRAME, 128), 1)):
        p_at = iota(shape, halo_dim)
        frame_lane = iota(shape, 1 - halo_dim)
        for side in range(2):
            for k in range(SLOTS):
                p = p_at - (side * EAST + k * EDGE)
                spot = jnp.where(p == 0, FRAME - TS, TS * (p - 1)) + side * (TS - 1)
                hits = (p >= 0) & (p < EDGE) & (frame_lane == spot)
                refs[side, k] = jnp.where(hits, 1.0, 0.0).astype(BF16)
    stack = stack_of(message_views(shared, own)[0])
    kernel[...] = stack
    back_kernel[...] = turn(stack, turned)


def column_of(pieces, own):
    eye = iota((own, 128), 0) == iota((own, 128), 1)
    parts = pieces[...].astype(F32)
    line = parts[0:1] + parts[1:2] + parts[2:3]
    return jnp.sum(jnp.where(eye, line, 0.0), axis=1, keepdims=True)


def activation(kernel, window, bias_column, up):
    own = bias_column.shape[0]
    sums = dot(kernel, window)
    pre = (
        pltpu.roll(sums[:own], TS, 1)[:, :CELLS]
        + sums[own : 2 * own, :CELLS]
        + pltpu.roll(sums[2 * own :], FRAME - TS, 1)[:, :CELLS]
        + bias_column
    )
    square = pre * pre
    tanh = jnp.tanh(GELU_C * (pre * (1.0 + GELU_K * square)))
    half = 0.5 + 0.5 * tanh
    slope = half + (0.5 * pre) * (1.0 - tanh * tanh) * (GELU_C + (3.0 * GELU_C * GELU_K) * square)
    return pre * half, (up * slope).astype(BF16).astype(F32)


def frame_of(slopes):
    own = slopes.shape[0]
    wide = jnp.concatenate([slopes, jnp.zeros((own, FRAME - CELLS), F32)], axis=1)
    return jnp.concatenate([pltpu.roll(wide, FRAME - TS, 1), wide, pltpu.roll(wide, TS, 1)], axis=0).astype(BF16)


def upstream_of(halves, k, full):
    return jnp.concatenate([halves[k][0][...], halves[k][1][...]], axis=1).astype(F32) * full[k]


def half_of(count):
    position = lax.axis_index("tiles")
    rep = lax.axis_index("rep")
    if count == 4:
        return (rep + position + position // 2) % 2
    return rep


def forward_kernel(rows, fields, shared, kernel, spreads, windows, *refs, n_halos, half_rows, count):
    halos = refs[:n_halos]
    full_windows, frames, result, keep, send = refs[n_halos:]
    own = kernel.shape[0] // 3
    full, at_top, _ = slot_flags(rows)
    start = pl.multiple_of(lax.axis_index("chan") * own, own)
    half = half_of(count)
    lane128 = iota((1, 128), 1)
    _, halves, pieces = message_views(shared, own)
    bias_column = column_of(pieces, own)
    halo = halos[0][...].astype(F32)
    for ref in halos[1:]:
        halo = halo + ref[...].astype(F32)
    turned = pltpu.roll(halo, 128 - FOLD, 1)
    fold = jnp.where(lane128 < TS, turned, 0.0)
    fold_left = jnp.where((lane128 > 0) & (lane128 < TS), pltpu.roll(turned, 1, 1), 0.0)
    fold_right = jnp.where(lane128 < TS - 1, pltpu.roll(turned, 127, 1), 0.0)
    halo = halo.astype(BF16)
    grads = jnp.zeros((3 * own, 3 * C), F32)
    slope_sum = jnp.zeros((own, CELLS), F32)
    for k in range(SLOTS):
        west = dot(halo, spreads[0, k])
        east = dot(halo, spreads[1, k])
        rest = jnp.zeros((C, CELLS), F32)
        left = windows[k, :C] + (west + jnp.concatenate([rest, at_top[k] * fold_left], axis=1)).astype(BF16)
        right = windows[k, 2 * C :] + (east + jnp.concatenate([rest, at_top[k] * fold_right], axis=1)).astype(BF16)
        centre = windows[k, C : 2 * C] + jnp.concatenate([rest, at_top[k] * fold], axis=1).astype(BF16)
        window = jnp.concatenate([left, centre, right], axis=0)
        full_windows[k] = window
        up = upstream_of(halves, k, full)
        gelu, slopes = activation(kernel[...], window, bias_column, up)
        result[k] = (full[k] * (fields[k, pl.ds(start, own), :].astype(F32) + gelu)).astype(BF16)
        slope_sum = slope_sum + slopes
        frame = frame_of(slopes)
        frames[k] = frame
        grads = grads + dot(frame, window, ((1,), (1,)))
    blocks = [grads[a * own : (a + 1) * own, b * C : (b + 1) * C] for a in range(3) for b in range(3)]
    eye = iota((own, 128), 0) == iota((own, 128), 1)
    bias_line = jnp.sum(jnp.where(eye, jnp.sum(slope_sum, axis=1, keepdims=True), 0.0), axis=0, keepdims=True)
    blocks.append(bias_line)
    blocks.append(jnp.zeros((2 * half_rows - 9 * own - 1, 128), F32))
    sums = jnp.concatenate(blocks, axis=0)
    low, high = sums[:half_rows], sums[half_rows:]
    keep[...] = jnp.where(half == 0, low, high)
    send[...] = jnp.where(half == 0, high, low)


def other_kernel(rows, windows, *refs):
    n = (len(refs) - 1) // 3
    turned = refs[-1]
    full = slot_flags(rows)[0]
    for ref, frames, back_kernel in zip(refs[:n], refs[n : 2 * n], refs[2 * n : 3 * n]):
        own = back_kernel.shape[0] // 3
        taps, halves, pieces = message_views(ref, own)
        stack = stack_of(taps)
        bias_column = column_of(pieces, own)
        for k in range(SLOTS):
            _, slopes = activation(stack, windows[k], bias_column, upstream_of(halves, k, full))
            frames[k] = frame_of(slopes)
        back_kernel[...] = turn(stack, turned)


def backward_kernel(rows, shared, gathers, result, *refs):
    base, edges, result_out, sem = refs[-4:]
    n = (len(refs) - 4) // 2
    frames, back_kernels = refs[:n], refs[n : 2 * n]
    own = back_kernels[0].shape[0] // 3
    put = pltpu.make_async_copy(result, result_out.at[0], sem)
    put.start()
    full, at_top, above = slot_flags(rows)
    column = iota((1, FRAME), 1) % TS
    lane128 = iota((1, 128), 1)
    edge_sum = jnp.zeros((own, 128), F32)
    pads = []
    for k in range(SLOTS):
        spread = dot(back_kernels[0][...], frames[0][k])
        for frame, back_kernel in zip(frames[1:], back_kernels[1:]):
            spread = spread + dot(back_kernel[...], frame[k])
        first, second, third = spread[:own], spread[own : 2 * own], spread[2 * own :]
        pad = (
            second
            + jnp.where(column < TS - 1, pltpu.roll(first, FRAME - 1, 1), 0.0)
            + jnp.where(column > 0, pltpu.roll(third, 1, 1), 0.0)
        )
        pads.append(pad)
        edge_sum = edge_sum + dot(first.astype(BF16), gathers[0, k])
        edge_sum = edge_sum + dot(third.astype(BF16), gathers[1, k])
        crest = jnp.where(lane128 < TS, pad[:, CELLS:], 0.0) * at_top[k]
        edge_sum = edge_sum + pltpu.roll(crest, FOLD, 1)
    edges[...] = edge_sum.astype(BF16)
    _, halves, _ = message_views(shared, own)
    for k in range(SLOTS):
        first = pads[k][:, :128]
        second = pads[k][:, 128:CELLS]
        for l in range(SLOTS):
            if l != k:
                ends = pads[l][:, CELLS:]
                first = first + jnp.where(lane128 < TS, ends, 0.0) * above[l][k]
                second = second + jnp.where(lane128 >= 128 - TS, ends, 0.0) * above[k][l]
        base[k] = upstream_of(halves, k, full) + jnp.concatenate([first, second], axis=1)
    put.wait()


def finish_kernel(base, *refs):
    out = refs[-1]
    n = len(refs) // 2
    total = None
    for received, hits in zip(refs[:n], refs[n:]):
        part = dot(received[...], hits[...], ((1,), (1,)))
        total = part if total is None else total + part
    for k in range(SLOTS):
        out[0, k] = (base[k] + total[:, k * CELLS : (k + 1) * CELLS]).astype(BF16)


def gather_kernel(mine, theirs, weights_out, bias_out, *, count):
    half = half_of(count)
    own = weights_out.shape[1]
    low = jnp.where(half == 0, mine[...], theirs[...])
    high = jnp.where(half == 0, theirs[...], mine[...])
    sums = jnp.concatenate([low, high], axis=0)
    for t in range(9):
        weights_out[t] = sums[t * own : (t + 1) * own]
    bias_out[...] = sums[9 * own : 9 * own + 1, :own]


SMEM = pl.BlockSpec(memory_space=pltpu.SMEM)
VMEM = pl.BlockSpec(memory_space=pltpu.VMEM)
HBM = pl.BlockSpec(memory_space=pltpu.HBM)


def call(kernel, specs, outs, scratch=(), out_specs=None, cost=None):
    return pl.pallas_call(
        kernel,
        in_specs=specs,
        out_specs=out_specs or [VMEM] * len(outs),
        out_shape=outs,
        scratch_shapes=list(scratch),
        cost_estimate=cost,
        compiler_params=pltpu.CompilerParams(vmem_limit_bytes=40 << 20),
    )


def struct(shape, dtype):
    return jax.ShapeDtypeStruct(shape, dtype)


def on_device(fields, tile_rows, weights, bias, cotangent):
    own = weights.shape[1]
    count = lax.axis_size("tiles")
    chans = lax.axis_size("chan")
    reps = lax.axis_size("rep")
    plans = halo_plans(count)
    n = len(plans)
    shared_rows = 9 * own + 2 * SLOTS * own + 16
    half_rows = -(-(9 * own + 1) // 32) * 16
    swap = [(0, 1), (1, 0)]

    pinned = [
        pltpu.with_memory_space_constraint(x, pltpu.HBM)
        for x in (tile_rows, fields, weights, bias.reshape(1, own), cotangent)
    ]
    rows, tiles, shared, *packed = call(
        lambda *refs: pack_kernel(*refs, count=count),
        [HBM] * 5,
        [
            struct(tile_rows.shape, jnp.int32),
            struct((SLOTS, C, CELLS), BF16),
            struct((shared_rows, 128), BF16),
        ]
        + [struct((SLOTS * CELLS, 128), BF16)] * n
        + [struct((C, 128), BF16)] * n,
        [
            pltpu.SMEM(tile_rows.shape, jnp.int32),
            pltpu.VMEM((1, own), F32),
            pltpu.SemaphoreType.DMA((12 + 2 * SLOTS,)),
        ],
    )(*pinned)
    maps, messages = packed[:n], packed[n:]

    def move(x, route):
        return lax.ppermute(x, "tiles", [(i, route(i)) for i in range(count)])

    halos = [x if route is None else move(x, route) for x, (route, _) in zip(messages, plans)]
    others = [lax.ppermute(shared, "chan", [(i, (i + s) % chans) for i in range(chans)]) for s in range(1, chans)]

    windows, spreads, gathers, kernel, back_kernel = call(
        window_kernel,
        [SMEM] + [VMEM] * 2,
        [
            struct((SLOTS, 3 * C, FRAME), BF16),
            struct((2, SLOTS, 128, FRAME), BF16),
            struct((2, SLOTS, FRAME, 128), BF16),
            struct((3 * own, 3 * C), BF16),
            struct((3 * own, 3 * own), BF16),
        ],
        [pltpu.VMEM((3 * C, 3 * own), F32)],
    )(rows, tiles, shared)

    windows, frames, result, keep, send = call(
        lambda *refs: forward_kernel(*refs, n_halos=len(halos), half_rows=half_rows, count=count),
        [SMEM] + [VMEM] * (5 + len(halos)),
        [
            struct((SLOTS, 3 * C, FRAME), BF16),
            struct((SLOTS, 3 * own, FRAME), BF16),
            struct((SLOTS, own, CELLS), BF16),
            struct((half_rows, 128), F32),
            struct((half_rows, 128), F32),
        ],
        cost=pl.CostEstimate(flops=4 * 10**9, transcendentals=0, bytes_accessed=0),
    )(rows, tiles, shared, kernel, spreads, windows, *halos)

    send, others = lax.optimization_barrier((send, others))
    sums = keep + lax.ppermute(send, "rep", swap)
    other_frames = call(
        other_kernel,
        [SMEM, VMEM] + [VMEM] * len(others),
        [struct((SLOTS, 3 * own, FRAME), BF16)] * len(others) + [struct((3 * own, 3 * own), BF16)] * len(others),
        [pltpu.VMEM((3 * C, 3 * own), F32)],
    )(rows, windows, *others)
    other_frames, other_back = other_frames[: len(others)], other_frames[len(others) :]
    rounded = sums.astype(BF16)
    frames, rounded, other_frames = lax.optimization_barrier((frames, rounded, other_frames))

    base, edges, result = call(
        backward_kernel,
        [SMEM] + [VMEM] * (5 + 2 * len(others)),
        [
            struct((SLOTS, own, CELLS), F32),
            struct((own, 128), BF16),
            struct((1, SLOTS, own, CELLS), BF16),
        ],
        [pltpu.SemaphoreType.DMA],
        out_specs=[VMEM, VMEM, HBM],
    )(rows, shared, gathers, result, frames, *other_frames, back_kernel, *other_back)

    if count == 4:

        def cross(x, route):
            pairs = [(2 * d + r, 2 * route(d) + 1 - r) for d in range(count) for r in range(2)]
            return lax.ppermute(x, ("tiles", "rep"), pairs)

        across = cross(edges, lambda d: d ^ 2)
        beside = lax.ppermute(edges, "rep", swap)
        other = cross(rounded, lambda d: d ^ 2)
        rounded = (rounded.astype(F32) + other.astype(F32)).astype(BF16)
        both = cross(jnp.concatenate([rounded, beside, across], axis=0), lambda d: d ^ 1)
        sums = rounded.astype(F32) + both[:half_rows].astype(F32)
        across = lax.ppermute(across, "rep", swap)
        returned = [both[half_rows + own :], across, both[half_rows : half_rows + own], edges]
    else:
        for step in range(count.bit_length() - 1):
            other = move(rounded, lambda d: d ^ (1 << step))
            sums = rounded.astype(F32) + other.astype(F32)
            rounded = sums.astype(BF16)
        returned = [
            lax.ppermute(edges, "tiles", [(route(j), j) for j in range(count)]) for route, _ in plans
        ]
    grad_scale = 1.0 / math.sqrt(reps * fields.shape[0] * count * SLOTS * CELLS)
    sums = sums * grad_scale
    grad_fields = call(
        finish_kernel,
        [VMEM] * (1 + 2 * n),
        [struct((1, SLOTS, own, CELLS), BF16)],
    )(base, *returned, *maps)[0]
    grad_weights, grad_bias = call(
        lambda *refs: gather_kernel(*refs, count=count),
        [VMEM, VMEM],
        [struct((9, own, C), F32), struct((1, own), F32)],
    )(sums, lax.ppermute(sums, "rep", swap))
    return (result, grad_fields, grad_weights, grad_bias.reshape(own))


def solution(mesh):
    in_specs = (
        P(("groups", "rep"), "tiles", None, None),
        P(),
        P(None, "chan", None),
        P("chan"),
        P(("groups", "rep"), "tiles", "chan", None),
    )
    out_specs = (
        P(("groups", "rep"), "tiles", "chan", None),
        P(("groups", "rep"), "tiles", "chan", None),
        P("groups", "chan", None),
        P(("groups", "chan")),
    )
    return jax.shard_map(
        on_device, mesh=mesh, in_specs=in_specs, out_specs=out_specs, check_vma=False
    )
```

```python
import math

import jax
import jax.numpy as jnp
from jax import lax
from jax.experimental import pallas as pl
from jax.experimental.pallas import tpu as pltpu
from jax.sharding import PartitionSpec as P

C = 128
TS = 16
SLOTS = 3
CELLS = TS * TS
FRAME = 384
EDGE = TS + 2
EAST = SLOTS * EDGE
FOLD = 2 * SLOTS * EDGE
F32 = jnp.float32
BF16 = jnp.bfloat16
GELU_C = math.sqrt(2.0 / math.pi)
GELU_K = 0.044715


def iota(shape, dim):
    return lax.broadcasted_iota(jnp.int32, shape, dim)


def halo_plans(count):
    if count == 4:
        return [
            (lambda d: 3 - d, ("side", "fold")),
            (lambda d: d ^ 2, ("corner",)),
            (lambda d: d ^ 1, ("side",)),
            (None, ("corner",)),
        ]
    return [
        (lambda d: (d + 1) % count, ("west",)),
        (lambda d: (d + count - 1) % count, ("east",)),
        (lambda d: count - 1 - d, ("fold",)),
        (lambda d: (count - d) % count, ("corner_west",)),
        (lambda d: (2 * count - 2 - d) % count, ("corner_east",)),
    ]


def halo_sources(rows, count, source, target, roles):
    lane = iota((8, 128), 1)
    top = 2 * SLOTS - 1
    east = (lane >= EAST) & (lane < FOLD)
    at = lane - jnp.where(east, EAST, 0)
    k = jnp.where(at >= EDGE, 1, 0) + jnp.where(at >= 2 * EDGE, 1, 0)
    p = at - EDGE * k
    rim = lane < FOLD
    row = jnp.where(k == 0, rows[target, 0], jnp.where(k == 1, rows[target, 1], rows[target, 2]))
    row = jnp.where(rim, row, -1)
    src = jnp.full((8, 128), -1, jnp.int32)
    sides = [name for name in ("west", "east") if name in roles or "side" in roles]
    if sides:
        wanted = row + jnp.where(p == TS + 1, 1, 0) - jnp.where(p == 0, 1, 0)
        slot = jnp.full((8, 128), -1, jnp.int32)
        present = (p > 0) & (p <= TS)
        for l in range(SLOTS):
            slot = jnp.where(wanted == rows[source, l], l, slot)
            present = present | (wanted == rows[target, l])
        cell = jnp.where(p == 0, CELLS - TS, jnp.where(p == TS + 1, 0, TS * (p - 1))) + jnp.where(east, 0, TS - 1)
        good = present & (row >= 0) & (wanted >= 0) & (slot >= 0)
        from_west = target == (source + 1) % count if "west" in sides else False
        from_east = target == (source + count - 1) % count if "east" in sides else False
        good = good & ((jnp.logical_not(east) & from_west) | (east & from_east))
        src = jnp.where(good, slot * CELLS + cell, src)

    def top_slot(column):
        found = jnp.int32(-1)
        for l in range(SLOTS):
            found = jnp.where(rows[column, l] == top, l, found)
        return found

    if sides and len(sides) == len(roles) and "side" not in roles or roles == ("side",):
        return src
    mine = top_slot(source)
    if "fold" in roles:
        good = (lane >= FOLD) & (lane < FOLD + TS) & (mine >= 0) & (target == count - 1 - source)
        src = jnp.where(good, mine * CELLS + (CELLS - 1 + FOLD) - lane, src)
    corners = [name for name in ("west", "east") if "corner" in roles or f"corner_{name}" in roles]
    if corners:
        good = (row == top) & (p == TS + 1) & (mine >= 0) & (top_slot(count - 1 - target) >= 0)
        from_west = target == (count - source) % count if "west" in corners else False
        from_east = target == (2 * count - 2 - source) % count if "east" in corners else False
        good = good & ((jnp.logical_not(east) & from_west) | (east & from_east))
        src = jnp.where(good, mine * CELLS + CELLS - TS + jnp.where(east, TS - 1, 0), src)
    return src


def halo_map(rows, count, source, plan):
    route, roles = plan
    target = source if route is None else route(source)
    src = halo_sources(rows, count, source, target, roles)
    hits = iota((SLOTS * CELLS, 128), 0) == src[0:1, :]
    return jnp.where(hits, 1.0, 0.0).astype(BF16)


def dot(lhs, rhs, dims=((1,), (0,))):
    return lax.dot_general(lhs, rhs, (dims, ((), ())), preferred_element_type=F32)


def message_views(ref, own):
    taps = [ref.at[t * own : (t + 1) * own] for t in range(9)]
    base = 9 * own
    halves = [
        [ref.at[base + (2 * k + h) * own : base + (2 * k + h + 1) * own] for h in range(2)] for k in range(SLOTS)
    ]
    at = base + 2 * SLOTS * own
    return taps, halves, ref.at[at : at + 16]


def pack_kernel(rows_hbm, fields_hbm, weights_hbm, bias_hbm, cot_hbm, *refs, count):
    n = len(halo_plans(count))
    rows_out, fields_out, shared = refs[:3]
    maps = refs[3 : 3 + n]
    outs = refs[3 + n : -3]
    rows, bias, sem = refs[-3:]
    own = weights_hbm.shape[1]
    taps, halves, pieces = message_views(shared, own)
    get_rows = pltpu.make_async_copy(rows_hbm, rows, sem.at[0])
    get_rows.start()
    get_fields = pltpu.make_async_copy(fields_hbm.at[0], fields_out, sem.at[1])
    get_fields.start()
    get_bias = pltpu.make_async_copy(bias_hbm, bias, sem.at[2])
    get_bias.start()
    more = [pltpu.make_async_copy(weights_hbm.at[t], taps[t], sem.at[3 + t]) for t in range(9)]
    for k in range(SLOTS):
        for h in range(2):
            source = cot_hbm.at[0, k, :, h * 128 : h * 128 + 128]
            more.append(pltpu.make_async_copy(source, halves[k][h], sem.at[12 + 2 * k + h]))
    for copy in more:
        copy.start()
    get_rows.wait()
    position = lax.axis_index("tiles")
    plans = halo_plans(count)
    for plan, out in zip(plans, maps):
        out[...] = halo_map(rows, count, position, plan)
    put_rows = pltpu.make_async_copy(rows, rows_out, sem.at[0])
    put_rows.start()
    get_bias.wait()
    line = jnp.concatenate([bias[...], jnp.zeros((1, 128 - own), F32)], axis=1)
    high = line.astype(BF16).astype(F32)
    middle = (line - high).astype(BF16).astype(F32)
    low = line - high - middle
    pieces[...] = jnp.concatenate([high, middle, low, jnp.zeros((13, 128), F32)], axis=0).astype(BF16)
    get_fields.wait()
    cells = jnp.concatenate([fields_out[k] for k in range(SLOTS)], axis=1)
    for out, hits in zip(outs, maps):
        out[...] = dot(cells, hits[...]).astype(BF16)
    for copy in more:
        copy.wait()
    put_rows.wait()


def flag(condition):
    return jnp.where(condition, 1.0, 0.0).astype(F32)


def slot_flags(rows):
    position = lax.axis_index("tiles")
    row = [rows[position, k] for k in range(SLOTS)]
    full = [flag(r >= 0) for r in row]
    at_top = [flag(r == 2 * SLOTS - 1) for r in row]
    above = [[flag((row[k] >= 0) & (row[l] == row[k] + 1)) for l in range(SLOTS)] for k in range(SLOTS)]
    return full, at_top, above


def turn(stack, turned):
    own = stack.shape[0] // 3
    start = pl.multiple_of(lax.axis_index("chan") * own, own)
    turned[...] = jnp.transpose(stack.astype(F32))
    return jnp.concatenate([turned[pl.ds(b * C + start, own), :] for b in range(3)], axis=0).astype(BF16)


def stack_of(taps):
    return jnp.concatenate(
        [jnp.concatenate([taps[3 * a + b][...] for b in range(3)], axis=1) for a in range(3)], axis=0
    )


def window_kernel(rows, fields, shared, windows, spreads, gathers, kernel, back_kernel, turned):
    own = kernel.shape[0] // 3
    full, _, above = slot_flags(rows)
    column = iota((1, FRAME), 1) % TS
    lane128 = iota((1, 128), 1)
    tiles = [fields[k].astype(F32) * full[k] for k in range(SLOTS)]
    for k in range(SLOTS):
        north = jnp.zeros((C, 128), F32)
        south = jnp.zeros((C, 128), F32)
        for l in range(SLOTS):
            if l != k:
                north = north + above[k][l] * tiles[l][:, :128]
                south = south + above[l][k] * tiles[l][:, 128:]
        ends = jnp.where(lane128 < TS, north, jnp.where(lane128 >= 128 - TS, south, 0.0))
        centre = jnp.concatenate([tiles[k], ends], axis=1)
        windows[k, :C] = jnp.where(column == 0, 0.0, pltpu.roll(centre, 1, 1)).astype(BF16)
        windows[k, C : 2 * C] = centre.astype(BF16)
        windows[k, 2 * C :] = jnp.where(column == TS - 1, 0.0, pltpu.roll(centre, FRAME - 1, 1)).astype(BF16)
    for refs, shape, halo_dim in ((spreads, (128, FRAME), 0), (gathers, (FRAME, 128), 1)):
        p_at = iota(shape, halo_dim)
        frame_lane = iota(shape, 1 - halo_dim)
        for side in range(2):
            for k in range(SLOTS):
                p = p_at - (side * EAST + k * EDGE)
                spot = jnp.where(p == 0, FRAME - TS, TS * (p - 1)) + side * (TS - 1)
                hits = (p >= 0) & (p < EDGE) & (frame_lane == spot)
                refs[side, k] = jnp.where(hits, 1.0, 0.0).astype(BF16)
    stack = stack_of(message_views(shared, own)[0])
    kernel[...] = stack
    back_kernel[...] = turn(stack, turned)


def column_of(pieces, own):
    eye = iota((own, 128), 0) == iota((own, 128), 1)
    parts = pieces[...].astype(F32)
    line = parts[0:1] + parts[1:2] + parts[2:3]
    return jnp.sum(jnp.where(eye, line, 0.0), axis=1, keepdims=True)


def activation(kernel, window, bias_column, up):
    own = bias_column.shape[0]
    sums = dot(kernel, window)
    pre = (
        pltpu.roll(sums[:own], TS, 1)[:, :CELLS]
        + sums[own : 2 * own, :CELLS]
        + pltpu.roll(sums[2 * own :], FRAME - TS, 1)[:, :CELLS]
        + bias_column
    )
    square = pre * pre
    tanh = jnp.tanh(GELU_C * (pre * (1.0 + GELU_K * square)))
    half = 0.5 + 0.5 * tanh
    slope = half + (0.5 * pre) * (1.0 - tanh * tanh) * (GELU_C + (3.0 * GELU_C * GELU_K) * square)
    return pre * half, (up * slope).astype(BF16).astype(F32)


def frame_of(slopes):
    own = slopes.shape[0]
    wide = jnp.concatenate([slopes, jnp.zeros((own, FRAME - CELLS), F32)], axis=1)
    return jnp.concatenate([pltpu.roll(wide, FRAME - TS, 1), wide, pltpu.roll(wide, TS, 1)], axis=0).astype(BF16)


def upstream_of(halves, k, full):
    return jnp.concatenate([halves[k][0][...], halves[k][1][...]], axis=1).astype(F32) * full[k]


def half_of(count):
    position = lax.axis_index("tiles")
    rep = lax.axis_index("rep")
    if count == 4:
        return (rep + position + position // 2) % 2
    return rep


def forward_kernel(rows, fields, shared, kernel, spreads, windows, *refs, n_halos, half_rows, count):
    halos = refs[:n_halos]
    full_windows, frames, result, keep, send = refs[n_halos:]
    own = kernel.shape[0] // 3
    full, at_top, _ = slot_flags(rows)
    start = pl.multiple_of(lax.axis_index("chan") * own, own)
    half = half_of(count)
    lane128 = iota((1, 128), 1)
    _, halves, pieces = message_views(shared, own)
    bias_column = column_of(pieces, own)
    halo = halos[0][...].astype(F32)
    for ref in halos[1:]:
        halo = halo + ref[...].astype(F32)
    turned = pltpu.roll(halo, 128 - FOLD, 1)
    fold = jnp.where(lane128 < TS, turned, 0.0)
    fold_left = jnp.where((lane128 > 0) & (lane128 < TS), pltpu.roll(turned, 1, 1), 0.0)
    fold_right = jnp.where(lane128 < TS - 1, pltpu.roll(turned, 127, 1), 0.0)
    halo = halo.astype(BF16)
    grads = jnp.zeros((3 * own, 3 * C), F32)
    slope_sum = jnp.zeros((own, CELLS), F32)
    for k in range(SLOTS):
        west = dot(halo, spreads[0, k])
        east = dot(halo, spreads[1, k])
        rest = jnp.zeros((C, CELLS), F32)
        left = windows[k, :C] + (west + jnp.concatenate([rest, at_top[k] * fold_left], axis=1)).astype(BF16)
        right = windows[k, 2 * C :] + (east + jnp.concatenate([rest, at_top[k] * fold_right], axis=1)).astype(BF16)
        centre = windows[k, C : 2 * C] + jnp.concatenate([rest, at_top[k] * fold], axis=1).astype(BF16)
        window = jnp.concatenate([left, centre, right], axis=0)
        full_windows[k] = window
        up = upstream_of(halves, k, full)
        gelu, slopes = activation(kernel[...], window, bias_column, up)
        result[k] = (full[k] * (fields[k, pl.ds(start, own), :].astype(F32) + gelu)).astype(BF16)
        slope_sum = slope_sum + slopes
        frame = frame_of(slopes)
        frames[k] = frame
        grads = grads + dot(frame, window, ((1,), (1,)))
    blocks = [grads[a * own : (a + 1) * own, b * C : (b + 1) * C] for a in range(3) for b in range(3)]
    eye = iota((own, 128), 0) == iota((own, 128), 1)
    bias_line = jnp.sum(jnp.where(eye, jnp.sum(slope_sum, axis=1, keepdims=True), 0.0), axis=0, keepdims=True)
    blocks.append(bias_line)
    blocks.append(jnp.zeros((2 * half_rows - 9 * own - 1, 128), F32))
    sums = jnp.concatenate(blocks, axis=0)
    low, high = sums[:half_rows], sums[half_rows:]
    keep[...] = jnp.where(half == 0, low, high)
    send[...] = jnp.where(half == 0, high, low)


def other_kernel(rows, windows, *refs):
    n = (len(refs) - 1) // 3
    turned = refs[-1]
    full = slot_flags(rows)[0]
    for ref, frames, back_kernel in zip(refs[:n], refs[n : 2 * n], refs[2 * n : 3 * n]):
        own = back_kernel.shape[0] // 3
        taps, halves, pieces = message_views(ref, own)
        stack = stack_of(taps)
        bias_column = column_of(pieces, own)
        for k in range(SLOTS):
            _, slopes = activation(stack, windows[k], bias_column, upstream_of(halves, k, full))
            frames[k] = frame_of(slopes)
        back_kernel[...] = turn(stack, turned)


def backward_kernel(rows, shared, gathers, result, *refs):
    base, edges, result_out, sem = refs[-4:]
    n = (len(refs) - 4) // 2
    frames, back_kernels = refs[:n], refs[n : 2 * n]
    own = back_kernels[0].shape[0] // 3
    put = pltpu.make_async_copy(result, result_out.at[0], sem)
    put.start()
    full, at_top, above = slot_flags(rows)
    column = iota((1, FRAME), 1) % TS
    lane128 = iota((1, 128), 1)
    edge_sum = jnp.zeros((own, 128), F32)
    pads = []
    for k in range(SLOTS):
        spread = dot(back_kernels[0][...], frames[0][k])
        for frame, back_kernel in zip(frames[1:], back_kernels[1:]):
            spread = spread + dot(back_kernel[...], frame[k])
        first, second, third = spread[:own], spread[own : 2 * own], spread[2 * own :]
        pad = (
            second
            + jnp.where(column < TS - 1, pltpu.roll(first, FRAME - 1, 1), 0.0)
            + jnp.where(column > 0, pltpu.roll(third, 1, 1), 0.0)
        )
        pads.append(pad)
        edge_sum = edge_sum + dot(first.astype(BF16), gathers[0, k])
        edge_sum = edge_sum + dot(third.astype(BF16), gathers[1, k])
        crest = jnp.where(lane128 < TS, pad[:, CELLS:], 0.0) * at_top[k]
        edge_sum = edge_sum + pltpu.roll(crest, FOLD, 1)
    edges[...] = edge_sum.astype(BF16)
    _, halves, _ = message_views(shared, own)
    for k in range(SLOTS):
        first = pads[k][:, :128]
        second = pads[k][:, 128:CELLS]
        for l in range(SLOTS):
            if l != k:
                ends = pads[l][:, CELLS:]
                first = first + jnp.where(lane128 < TS, ends, 0.0) * above[l][k]
                second = second + jnp.where(lane128 >= 128 - TS, ends, 0.0) * above[k][l]
        base[k] = upstream_of(halves, k, full) + jnp.concatenate([first, second], axis=1)
    put.wait()


def finish_kernel(base, *refs):
    out = refs[-1]
    n = len(refs) // 2
    total = None
    for received, hits in zip(refs[:n], refs[n:]):
        part = dot(received[...], hits[...], ((1,), (1,)))
        total = part if total is None else total + part
    for k in range(SLOTS):
        out[0, k] = (base[k] + total[:, k * CELLS : (k + 1) * CELLS]).astype(BF16)


def gather_kernel(mine, theirs, weights_out, bias_out, *, count):
    half = half_of(count)
    own = weights_out.shape[1]
    low = jnp.where(half == 0, mine[...], theirs[...])
    high = jnp.where(half == 0, theirs[...], mine[...])
    sums = jnp.concatenate([low, high], axis=0)
    for t in range(9):
        weights_out[t] = sums[t * own : (t + 1) * own]
    bias_out[...] = sums[9 * own : 9 * own + 1, :own]


SMEM = pl.BlockSpec(memory_space=pltpu.SMEM)
VMEM = pl.BlockSpec(memory_space=pltpu.VMEM)
HBM = pl.BlockSpec(memory_space=pltpu.HBM)


def call(kernel, specs, outs, scratch=(), out_specs=None, cost=None):
    return pl.pallas_call(
        kernel,
        in_specs=specs,
        out_specs=out_specs or [VMEM] * len(outs),
        out_shape=outs,
        scratch_shapes=list(scratch),
        cost_estimate=cost,
        compiler_params=pltpu.CompilerParams(vmem_limit_bytes=40 << 20),
    )


def struct(shape, dtype):
    return jax.ShapeDtypeStruct(shape, dtype)


def on_device(fields, tile_rows, weights, bias, cotangent):
    own = weights.shape[1]
    count = lax.axis_size("tiles")
    chans = lax.axis_size("chan")
    reps = lax.axis_size("rep")
    plans = halo_plans(count)
    n = len(plans)
    shared_rows = 9 * own + 2 * SLOTS * own + 16
    half_rows = -(-(9 * own + 1) // 32) * 16
    swap = [(0, 1), (1, 0)]

    pinned = [
        pltpu.with_memory_space_constraint(x, pltpu.HBM)
        for x in (tile_rows, fields, weights, bias.reshape(1, own), cotangent)
    ]
    rows, tiles, shared, *packed = call(
        lambda *refs: pack_kernel(*refs, count=count),
        [HBM] * 5,
        [
            struct(tile_rows.shape, jnp.int32),
            struct((SLOTS, C, CELLS), BF16),
            struct((shared_rows, 128), BF16),
        ]
        + [struct((SLOTS * CELLS, 128), BF16)] * n
        + [struct((C, 128), BF16)] * n,
        [
            pltpu.SMEM(tile_rows.shape, jnp.int32),
            pltpu.VMEM((1, own), F32),
            pltpu.SemaphoreType.DMA((12 + 2 * SLOTS,)),
        ],
    )(*pinned)
    maps, messages = packed[:n], packed[n:]

    def move(x, route):
        return lax.ppermute(x, "tiles", [(i, route(i)) for i in range(count)])

    halos = [x if route is None else move(x, route) for x, (route, _) in zip(messages, plans)]
    others = [lax.ppermute(shared, "chan", [(i, (i + s) % chans) for i in range(chans)]) for s in range(1, chans)]

    windows, spreads, gathers, kernel, back_kernel = call(
        window_kernel,
        [SMEM] + [VMEM] * 2,
        [
            struct((SLOTS, 3 * C, FRAME), BF16),
            struct((2, SLOTS, 128, FRAME), BF16),
            struct((2, SLOTS, FRAME, 128), BF16),
            struct((3 * own, 3 * C), BF16),
            struct((3 * own, 3 * own), BF16),
        ],
        [pltpu.VMEM((3 * C, 3 * own), F32)],
    )(rows, tiles, shared)

    windows, frames, result, keep, send = call(
        lambda *refs: forward_kernel(*refs, n_halos=len(halos), half_rows=half_rows, count=count),
        [SMEM] + [VMEM] * (5 + len(halos)),
        [
            struct((SLOTS, 3 * C, FRAME), BF16),
            struct((SLOTS, 3 * own, FRAME), BF16),
            struct((SLOTS, own, CELLS), BF16),
            struct((half_rows, 128), F32),
            struct((half_rows, 128), F32),
        ],
        cost=pl.CostEstimate(flops=4 * 10**9, transcendentals=0, bytes_accessed=0),
    )(rows, tiles, shared, kernel, spreads, windows, *halos)

    swapped, others = lax.optimization_barrier((lax.ppermute(send, "rep", swap), others))
    sums = keep + swapped
    rounded = sums.astype(BF16)
    frames, rounded, others = lax.optimization_barrier((frames, rounded, others))
    other_frames = call(
        other_kernel,
        [SMEM, VMEM] + [VMEM] * len(others),
        [struct((SLOTS, 3 * own, FRAME), BF16)] * len(others) + [struct((3 * own, 3 * own), BF16)] * len(others),
        [pltpu.VMEM((3 * C, 3 * own), F32)],
    )(rows, windows, *others)
    other_frames, other_back = other_frames[: len(others)], other_frames[len(others) :]

    base, edges, result = call(
        backward_kernel,
        [SMEM] + [VMEM] * (5 + 2 * len(others)),
        [
            struct((SLOTS, own, CELLS), F32),
            struct((own, 128), BF16),
            struct((1, SLOTS, own, CELLS), BF16),
        ],
        [pltpu.SemaphoreType.DMA],
        out_specs=[VMEM, VMEM, HBM],
    )(rows, shared, gathers, result, frames, *other_frames, back_kernel, *other_back)

    if count == 4:

        def cross(x, route):
            pairs = [(2 * d + r, 2 * route(d) + 1 - r) for d in range(count) for r in range(2)]
            return lax.ppermute(x, ("tiles", "rep"), pairs)

        across = cross(edges, lambda d: d ^ 2)
        beside = lax.ppermute(edges, "rep", swap)
        other = cross(rounded, lambda d: d ^ 2)
        rounded = (rounded.astype(F32) + other.astype(F32)).astype(BF16)
        both = cross(jnp.concatenate([rounded, beside, across], axis=0), lambda d: d ^ 1)
        sums = rounded.astype(F32) + both[:half_rows].astype(F32)
        across = lax.ppermute(across, "rep", swap)
        returned = [both[half_rows + own :], across, both[half_rows : half_rows + own], edges]
    else:
        for step in range(count.bit_length() - 1):
            other = move(rounded, lambda d: d ^ (1 << step))
            sums = rounded.astype(F32) + other.astype(F32)
            rounded = sums.astype(BF16)
        returned = [
            lax.ppermute(edges, "tiles", [(route(j), j) for j in range(count)]) for route, _ in plans
        ]
    grad_scale = 1.0 / math.sqrt(reps * fields.shape[0] * count * SLOTS * CELLS)
    sums = sums * grad_scale
    grad_fields = call(
        finish_kernel,
        [VMEM] * (1 + 2 * n),
        [struct((1, SLOTS, own, CELLS), BF16)],
    )(base, *returned, *maps)[0]
    grad_weights, grad_bias = call(
        lambda *refs: gather_kernel(*refs, count=count),
        [VMEM, VMEM],
        [struct((9, own, C), F32), struct((1, own), F32)],
    )(sums, lax.ppermute(sums, "rep", swap))
    return (result, grad_fields, grad_weights, grad_bias.reshape(own))


def solution(mesh):
    in_specs = (
        P(("groups", "rep"), "tiles", None, None),
        P(),
        P(None, "chan", None),
        P("chan"),
        P(("groups", "rep"), "tiles", "chan", None),
    )
    out_specs = (
        P(("groups", "rep"), "tiles", "chan", None),
        P(("groups", "rep"), "tiles", "chan", None),
        P("groups", "chan", None),
        P(("groups", "chan")),
    )
    return jax.shard_map(
        on_device, mesh=mesh, in_specs=in_specs, out_specs=out_specs, check_vma=False
    )
```

```python
import math

import jax
import jax.numpy as jnp
from jax import lax
from jax.experimental import pallas as pl
from jax.experimental.pallas import tpu as pltpu
from jax.sharding import PartitionSpec as P

C = 128
TS = 16
SLOTS = 3
CELLS = TS * TS
FRAME = 384
EDGE = TS + 2
EAST = SLOTS * EDGE
FOLD = 2 * SLOTS * EDGE
F32 = jnp.float32
BF16 = jnp.bfloat16
GELU_C = math.sqrt(2.0 / math.pi)
GELU_K = 0.044715


def iota(shape, dim):
    return lax.broadcasted_iota(jnp.int32, shape, dim)


def halo_plans(count):
    if count == 4:
        return [
            (lambda d: 3 - d, ("side", "fold")),
            (lambda d: d ^ 2, ("corner",)),
            (lambda d: d ^ 1, ("side",)),
            (None, ("corner",)),
        ]
    return [
        (lambda d: (d + 1) % count, ("west",)),
        (lambda d: (d + count - 1) % count, ("east",)),
        (lambda d: count - 1 - d, ("fold",)),
        (lambda d: (count - d) % count, ("corner_west",)),
        (lambda d: (2 * count - 2 - d) % count, ("corner_east",)),
    ]


def halo_sources(rows, count, source, target, roles):
    lane = iota((8, 128), 1)
    top = 2 * SLOTS - 1
    east = (lane >= EAST) & (lane < FOLD)
    at = lane - jnp.where(east, EAST, 0)
    k = jnp.where(at >= EDGE, 1, 0) + jnp.where(at >= 2 * EDGE, 1, 0)
    p = at - EDGE * k
    rim = lane < FOLD
    row = jnp.where(k == 0, rows[target, 0], jnp.where(k == 1, rows[target, 1], rows[target, 2]))
    row = jnp.where(rim, row, -1)
    src = jnp.full((8, 128), -1, jnp.int32)
    sides = [name for name in ("west", "east") if name in roles or "side" in roles]
    if sides:
        wanted = row + jnp.where(p == TS + 1, 1, 0) - jnp.where(p == 0, 1, 0)
        slot = jnp.full((8, 128), -1, jnp.int32)
        present = (p > 0) & (p <= TS)
        for l in range(SLOTS):
            slot = jnp.where(wanted == rows[source, l], l, slot)
            present = present | (wanted == rows[target, l])
        cell = jnp.where(p == 0, CELLS - TS, jnp.where(p == TS + 1, 0, TS * (p - 1))) + jnp.where(east, 0, TS - 1)
        good = present & (row >= 0) & (wanted >= 0) & (slot >= 0)
        from_west = target == (source + 1) % count if "west" in sides else False
        from_east = target == (source + count - 1) % count if "east" in sides else False
        good = good & ((jnp.logical_not(east) & from_west) | (east & from_east))
        src = jnp.where(good, slot * CELLS + cell, src)

    def top_slot(column):
        found = jnp.int32(-1)
        for l in range(SLOTS):
            found = jnp.where(rows[column, l] == top, l, found)
        return found

    if sides and len(sides) == len(roles) and "side" not in roles or roles == ("side",):
        return src
    mine = top_slot(source)
    if "fold" in roles:
        good = (lane >= FOLD) & (lane < FOLD + TS) & (mine >= 0) & (target == count - 1 - source)
        src = jnp.where(good, mine * CELLS + (CELLS - 1 + FOLD) - lane, src)
    corners = [name for name in ("west", "east") if "corner" in roles or f"corner_{name}" in roles]
    if corners:
        good = (row == top) & (p == TS + 1) & (mine >= 0) & (top_slot(count - 1 - target) >= 0)
        from_west = target == (count - source) % count if "west" in corners else False
        from_east = target == (2 * count - 2 - source) % count if "east" in corners else False
        good = good & ((jnp.logical_not(east) & from_west) | (east & from_east))
        src = jnp.where(good, mine * CELLS + CELLS - TS + jnp.where(east, TS - 1, 0), src)
    return src


def halo_map(rows, count, source, plan):
    route, roles = plan
    target = source if route is None else route(source)
    src = halo_sources(rows, count, source, target, roles)
    hits = iota((SLOTS * CELLS, 128), 0) == src[0:1, :]
    return jnp.where(hits, 1.0, 0.0).astype(BF16)


def dot(lhs, rhs, dims=((1,), (0,))):
    return lax.dot_general(lhs, rhs, (dims, ((), ())), preferred_element_type=F32)


PART = 5


def message_views(ref, own):
    taps = [ref.at[t * own : (t + 1) * own] for t in range(PART)]
    base = PART * own
    halves = [
        [ref.at[base + (2 * k + h) * own : base + (2 * k + h + 1) * own] for h in range(2)] for k in range(SLOTS)
    ]
    at = base + 2 * SLOTS * own
    return taps, halves, ref.at[at : at + 16]


def pack_kernel(rows_hbm, fields_hbm, weights_hbm, bias_hbm, cot_hbm, *refs, count):
    n = len(halo_plans(count))
    rows_out, fields_out, shared, taps_out = refs[:4]
    maps = refs[4 : 4 + n]
    outs = refs[4 + n : -3]
    rows, bias, sem = refs[-3:]
    own = weights_hbm.shape[1]
    taps, halves, pieces = message_views(shared, own)
    get_rows = pltpu.make_async_copy(rows_hbm, rows, sem.at[0])
    get_rows.start()
    get_fields = pltpu.make_async_copy(fields_hbm.at[0], fields_out, sem.at[1])
    get_fields.start()
    get_bias = pltpu.make_async_copy(bias_hbm, bias, sem.at[2])
    get_bias.start()
    first = lax.axis_index("rep") * (9 - PART)
    more = [pltpu.make_async_copy(weights_hbm.at[first + t], taps[t], sem.at[3 + t]) for t in range(PART)]
    more.append(pltpu.make_async_copy(weights_hbm, taps_out, sem.at[3 + PART]))
    for k in range(SLOTS):
        for h in range(2):
            source = cot_hbm.at[0, k, :, h * 128 : h * 128 + 128]
            more.append(pltpu.make_async_copy(source, halves[k][h], sem.at[12 + 2 * k + h]))
    for copy in more:
        copy.start()
    get_rows.wait()
    position = lax.axis_index("tiles")
    plans = halo_plans(count)
    for plan, out in zip(plans, maps):
        out[...] = halo_map(rows, count, position, plan)
    put_rows = pltpu.make_async_copy(rows, rows_out, sem.at[0])
    put_rows.start()
    get_bias.wait()
    line = jnp.concatenate([bias[...], jnp.zeros((1, 128 - own), F32)], axis=1)
    high = line.astype(BF16).astype(F32)
    middle = (line - high).astype(BF16).astype(F32)
    low = line - high - middle
    pieces[...] = jnp.concatenate([high, middle, low, jnp.zeros((13, 128), F32)], axis=0).astype(BF16)
    get_fields.wait()
    cells = jnp.concatenate([fields_out[k] for k in range(SLOTS)], axis=1)
    for out, hits in zip(outs, maps):
        out[...] = dot(cells, hits[...]).astype(BF16)
    for copy in more:
        copy.wait()
    put_rows.wait()


def flag(condition):
    return jnp.where(condition, 1.0, 0.0).astype(F32)


def slot_flags(rows):
    position = lax.axis_index("tiles")
    row = [rows[position, k] for k in range(SLOTS)]
    full = [flag(r >= 0) for r in row]
    at_top = [flag(r == 2 * SLOTS - 1) for r in row]
    above = [[flag((row[k] >= 0) & (row[l] == row[k] + 1)) for l in range(SLOTS)] for k in range(SLOTS)]
    return full, at_top, above


def turn(stack, turned):
    own = stack.shape[0] // 3
    start = pl.multiple_of(lax.axis_index("chan") * own, own)
    turned[...] = jnp.transpose(stack.astype(F32))
    return jnp.concatenate([turned[pl.ds(b * C + start, own), :] for b in range(3)], axis=0).astype(BF16)


def stack_of(taps):
    return jnp.concatenate(
        [jnp.concatenate([taps[3 * a + b][...] for b in range(3)], axis=1) for a in range(3)], axis=0
    )


def window_kernel(rows, fields, taps, windows, spreads, gathers, kernel, back_kernel, turned):
    own = kernel.shape[0] // 3
    full, _, above = slot_flags(rows)
    column = iota((1, FRAME), 1) % TS
    lane128 = iota((1, 128), 1)
    tiles = [fields[k].astype(F32) * full[k] for k in range(SLOTS)]
    for k in range(SLOTS):
        north = jnp.zeros((C, 128), F32)
        south = jnp.zeros((C, 128), F32)
        for l in range(SLOTS):
            if l != k:
                north = north + above[k][l] * tiles[l][:, :128]
                south = south + above[l][k] * tiles[l][:, 128:]
        ends = jnp.where(lane128 < TS, north, jnp.where(lane128 >= 128 - TS, south, 0.0))
        centre = jnp.concatenate([tiles[k], ends], axis=1)
        windows[k, :C] = jnp.where(column == 0, 0.0, pltpu.roll(centre, 1, 1)).astype(BF16)
        windows[k, C : 2 * C] = centre.astype(BF16)
        windows[k, 2 * C :] = jnp.where(column == TS - 1, 0.0, pltpu.roll(centre, FRAME - 1, 1)).astype(BF16)
    for refs, shape, halo_dim in ((spreads, (128, FRAME), 0), (gathers, (FRAME, 128), 1)):
        p_at = iota(shape, halo_dim)
        frame_lane = iota(shape, 1 - halo_dim)
        for side in range(2):
            for k in range(SLOTS):
                p = p_at - (side * EAST + k * EDGE)
                spot = jnp.where(p == 0, FRAME - TS, TS * (p - 1)) + side * (TS - 1)
                hits = (p >= 0) & (p < EDGE) & (frame_lane == spot)
                refs[side, k] = jnp.where(hits, 1.0, 0.0).astype(BF16)
    stack = stack_of([taps.at[t] for t in range(9)])
    kernel[...] = stack
    back_kernel[...] = turn(stack, turned)


def column_of(pieces, own):
    eye = iota((own, 128), 0) == iota((own, 128), 1)
    parts = pieces[...].astype(F32)
    line = parts[0:1] + parts[1:2] + parts[2:3]
    return jnp.sum(jnp.where(eye, line, 0.0), axis=1, keepdims=True)


def activation(kernel, window, bias_column, up):
    own = bias_column.shape[0]
    sums = dot(kernel, window)
    pre = (
        pltpu.roll(sums[:own], TS, 1)[:, :CELLS]
        + sums[own : 2 * own, :CELLS]
        + pltpu.roll(sums[2 * own :], FRAME - TS, 1)[:, :CELLS]
        + bias_column
    )
    square = pre * pre
    tanh = jnp.tanh(GELU_C * (pre * (1.0 + GELU_K * square)))
    half = 0.5 + 0.5 * tanh
    slope = half + (0.5 * pre) * (1.0 - tanh * tanh) * (GELU_C + (3.0 * GELU_C * GELU_K) * square)
    return pre * half, (up * slope).astype(BF16).astype(F32)


def frame_of(slopes):
    own = slopes.shape[0]
    wide = jnp.concatenate([slopes, jnp.zeros((own, FRAME - CELLS), F32)], axis=1)
    return jnp.concatenate([pltpu.roll(wide, FRAME - TS, 1), wide, pltpu.roll(wide, TS, 1)], axis=0).astype(BF16)


def upstream_of(halves, k, full):
    return jnp.concatenate([halves[k][0][...], halves[k][1][...]], axis=1).astype(F32) * full[k]


def half_of(count):
    position = lax.axis_index("tiles")
    rep = lax.axis_index("rep")
    if count == 4:
        return (rep + position + position // 2) % 2
    return rep


def forward_kernel(rows, fields, shared, kernel, spreads, windows, *refs, n_halos, half_rows, count):
    halos = refs[:n_halos]
    full_windows, frames, result, keep, send = refs[n_halos:]
    own = kernel.shape[0] // 3
    full, at_top, _ = slot_flags(rows)
    start = pl.multiple_of(lax.axis_index("chan") * own, own)
    half = half_of(count)
    lane128 = iota((1, 128), 1)
    _, halves, pieces = message_views(shared, own)
    bias_column = column_of(pieces, own)
    halo = halos[0][...].astype(F32)
    for ref in halos[1:]:
        halo = halo + ref[...].astype(F32)
    turned = pltpu.roll(halo, 128 - FOLD, 1)
    fold = jnp.where(lane128 < TS, turned, 0.0)
    fold_left = jnp.where((lane128 > 0) & (lane128 < TS), pltpu.roll(turned, 1, 1), 0.0)
    fold_right = jnp.where(lane128 < TS - 1, pltpu.roll(turned, 127, 1), 0.0)
    halo = halo.astype(BF16)
    grads = jnp.zeros((3 * own, 3 * C), F32)
    slope_sum = jnp.zeros((own, CELLS), F32)
    for k in range(SLOTS):
        west = dot(halo, spreads[0, k])
        east = dot(halo, spreads[1, k])
        rest = jnp.zeros((C, CELLS), F32)
        left = windows[k, :C] + (west + jnp.concatenate([rest, at_top[k] * fold_left], axis=1)).astype(BF16)
        right = windows[k, 2 * C :] + (east + jnp.concatenate([rest, at_top[k] * fold_right], axis=1)).astype(BF16)
        centre = windows[k, C : 2 * C] + jnp.concatenate([rest, at_top[k] * fold], axis=1).astype(BF16)
        window = jnp.concatenate([left, centre, right], axis=0)
        full_windows[k] = window
        up = upstream_of(halves, k, full)
        gelu, slopes = activation(kernel[...], window, bias_column, up)
        result[k] = (full[k] * (fields[k, pl.ds(start, own), :].astype(F32) + gelu)).astype(BF16)
        slope_sum = slope_sum + slopes
        frame = frame_of(slopes)
        frames[k] = frame
        grads = grads + dot(frame, window, ((1,), (1,)))
    blocks = [grads[a * own : (a + 1) * own, b * C : (b + 1) * C] for a in range(3) for b in range(3)]
    eye = iota((own, 128), 0) == iota((own, 128), 1)
    bias_line = jnp.sum(jnp.where(eye, jnp.sum(slope_sum, axis=1, keepdims=True), 0.0), axis=0, keepdims=True)
    blocks.append(bias_line)
    blocks.append(jnp.zeros((2 * half_rows - 9 * own - 1, 128), F32))
    sums = jnp.concatenate(blocks, axis=0)
    low, high = sums[:half_rows], sums[half_rows:]
    keep[...] = jnp.where(half == 0, low, high)
    send[...] = jnp.where(half == 0, high, low)


def other_kernel(rows, windows, *refs):
    n = (len(refs) - 1) // 4
    turned = refs[-1]
    full = slot_flags(rows)[0]
    rep = lax.axis_index("rep")
    for ref, swapped, frames, back_kernel in zip(*(refs[i * n : i * n + n] for i in range(4))):
        own = back_kernel.shape[0] // 3
        part, halves, pieces = message_views(ref, own)
        mine = [tap[...] for tap in part]
        theirs = [swapped[t * own : (t + 1) * own, :] for t in range(PART)]
        taps = [jnp.where(rep == 0, mine[t], theirs[t]) for t in range(PART)]
        taps += [jnp.where(rep == 0, theirs[t], mine[t]) for t in range(2 * PART - 9, PART)]
        stack = stack_of(taps)
        bias_column = column_of(pieces, own)
        for k in range(SLOTS):
            _, slopes = activation(stack, windows[k], bias_column, upstream_of(halves, k, full))
            frames[k] = frame_of(slopes)
        back_kernel[...] = turn(stack, turned)


def backward_kernel(rows, shared, gathers, result, *refs):
    base, edges, result_out, sem = refs[-4:]
    n = (len(refs) - 4) // 2
    frames, back_kernels = refs[:n], refs[n : 2 * n]
    own = back_kernels[0].shape[0] // 3
    put = pltpu.make_async_copy(result, result_out.at[0], sem)
    put.start()
    full, at_top, above = slot_flags(rows)
    column = iota((1, FRAME), 1) % TS
    lane128 = iota((1, 128), 1)
    edge_sum = jnp.zeros((own, 128), F32)
    pads = []
    for k in range(SLOTS):
        spread = dot(back_kernels[0][...], frames[0][k])
        for frame, back_kernel in zip(frames[1:], back_kernels[1:]):
            spread = spread + dot(back_kernel[...], frame[k])
        first, second, third = spread[:own], spread[own : 2 * own], spread[2 * own :]
        pad = (
            second
            + jnp.where(column < TS - 1, pltpu.roll(first, FRAME - 1, 1), 0.0)
            + jnp.where(column > 0, pltpu.roll(third, 1, 1), 0.0)
        )
        pads.append(pad)
        edge_sum = edge_sum + dot(first.astype(BF16), gathers[0, k])
        edge_sum = edge_sum + dot(third.astype(BF16), gathers[1, k])
        crest = jnp.where(lane128 < TS, pad[:, CELLS:], 0.0) * at_top[k]
        edge_sum = edge_sum + pltpu.roll(crest, FOLD, 1)
    edges[...] = edge_sum.astype(BF16)
    _, halves, _ = message_views(shared, own)
    for k in range(SLOTS):
        first = pads[k][:, :128]
        second = pads[k][:, 128:CELLS]
        for l in range(SLOTS):
            if l != k:
                ends = pads[l][:, CELLS:]
                first = first + jnp.where(lane128 < TS, ends, 0.0) * above[l][k]
                second = second + jnp.where(lane128 >= 128 - TS, ends, 0.0) * above[k][l]
        base[k] = upstream_of(halves, k, full) + jnp.concatenate([first, second], axis=1)
    put.wait()


def finish_kernel(base, *refs):
    out = refs[-1]
    n = len(refs) // 2
    total = None
    for received, hits in zip(refs[:n], refs[n:]):
        part = dot(received[...], hits[...], ((1,), (1,)))
        total = part if total is None else total + part
    for k in range(SLOTS):
        out[0, k] = (base[k] + total[:, k * CELLS : (k + 1) * CELLS]).astype(BF16)


def gather_kernel(mine, theirs, weights_out, bias_out, *, count):
    half = half_of(count)
    own = weights_out.shape[1]
    low = jnp.where(half == 0, mine[...], theirs[...])
    high = jnp.where(half == 0, theirs[...], mine[...])
    sums = jnp.concatenate([low, high], axis=0)
    for t in range(9):
        weights_out[t] = sums[t * own : (t + 1) * own]
    bias_out[...] = sums[9 * own : 9 * own + 1, :own]


SMEM = pl.BlockSpec(memory_space=pltpu.SMEM)
VMEM = pl.BlockSpec(memory_space=pltpu.VMEM)
HBM = pl.BlockSpec(memory_space=pltpu.HBM)


def call(kernel, specs, outs, scratch=(), out_specs=None, cost=None):
    return pl.pallas_call(
        kernel,
        in_specs=specs,
        out_specs=out_specs or [VMEM] * len(outs),
        out_shape=outs,
        scratch_shapes=list(scratch),
        cost_estimate=cost,
        compiler_params=pltpu.CompilerParams(vmem_limit_bytes=40 << 20),
    )


def struct(shape, dtype):
    return jax.ShapeDtypeStruct(shape, dtype)


def on_device(fields, tile_rows, weights, bias, cotangent):
    own = weights.shape[1]
    count = lax.axis_size("tiles")
    chans = lax.axis_size("chan")
    reps = lax.axis_size("rep")
    plans = halo_plans(count)
    n = len(plans)
    shared_rows = PART * own + 2 * SLOTS * own + 16
    half_rows = -(-(9 * own + 1) // 32) * 16
    swap = [(0, 1), (1, 0)]

    pinned = [
        pltpu.with_memory_space_constraint(x, pltpu.HBM)
        for x in (tile_rows, fields, weights, bias.reshape(1, own), cotangent)
    ]
    rows, tiles, shared, taps, *packed = call(
        lambda *refs: pack_kernel(*refs, count=count),
        [HBM] * 5,
        [
            struct(tile_rows.shape, jnp.int32),
            struct((SLOTS, C, CELLS), BF16),
            struct((shared_rows, 128), BF16),
            struct((9, own, C), BF16),
        ]
        + [struct((SLOTS * CELLS, 128), BF16)] * n
        + [struct((C, 128), BF16)] * n,
        [
            pltpu.SMEM(tile_rows.shape, jnp.int32),
            pltpu.VMEM((1, own), F32),
            pltpu.SemaphoreType.DMA((12 + 2 * SLOTS,)),
        ],
    )(*pinned)
    maps, messages = packed[:n], packed[n:]

    def move(x, route):
        return lax.ppermute(x, "tiles", [(i, route(i)) for i in range(count)])

    halos = [x if route is None else move(x, route) for x, (route, _) in zip(messages, plans)]
    others = [lax.ppermute(shared, "chan", [(i, (i + s) % chans) for i in range(chans)]) for s in range(1, chans)]

    windows, spreads, gathers, kernel, back_kernel = call(
        window_kernel,
        [SMEM] + [VMEM] * 2,
        [
            struct((SLOTS, 3 * C, FRAME), BF16),
            struct((2, SLOTS, 128, FRAME), BF16),
            struct((2, SLOTS, FRAME, 128), BF16),
            struct((3 * own, 3 * C), BF16),
            struct((3 * own, 3 * own), BF16),
        ],
        [pltpu.VMEM((3 * C, 3 * own), F32)],
    )(rows, tiles, taps)

    windows, frames, result, keep, send = call(
        lambda *refs: forward_kernel(*refs, n_halos=len(halos), half_rows=half_rows, count=count),
        [SMEM] + [VMEM] * (5 + len(halos)),
        [
            struct((SLOTS, 3 * C, FRAME), BF16),
            struct((SLOTS, 3 * own, FRAME), BF16),
            struct((SLOTS, own, CELLS), BF16),
            struct((half_rows, 128), F32),
            struct((half_rows, 128), F32),
        ],
        cost=pl.CostEstimate(flops=4 * 10**9, transcendentals=0, bytes_accessed=0),
    )(rows, tiles, shared, kernel, spreads, windows, *halos)

    send, others = lax.optimization_barrier((send, others))
    sums = keep + lax.ppermute(send, "rep", swap)
    other_frames = call(
        other_kernel,
        [SMEM, VMEM] + [VMEM] * (2 * len(others)),
        [struct((SLOTS, 3 * own, FRAME), BF16)] * len(others) + [struct((3 * own, 3 * own), BF16)] * len(others),
        [pltpu.VMEM((3 * C, 3 * own), F32)],
    )(rows, windows, *others, *(lax.ppermute(x[: PART * own], "rep", swap) for x in others))
    other_frames, other_back = other_frames[: len(others)], other_frames[len(others) :]
    rounded = sums.astype(BF16)
    frames, rounded, other_frames = lax.optimization_barrier((frames, rounded, other_frames))

    base, edges, result = call(
        backward_kernel,
        [SMEM] + [VMEM] * (5 + 2 * len(others)),
        [
            struct((SLOTS, own, CELLS), F32),
            struct((own, 128), BF16),
            struct((1, SLOTS, own, CELLS), BF16),
        ],
        [pltpu.SemaphoreType.DMA],
        out_specs=[VMEM, VMEM, HBM],
    )(rows, shared, gathers, result, frames, *other_frames, back_kernel, *other_back)

    if count == 4:

        def cross(x, route):
            pairs = [(2 * d + r, 2 * route(d) + 1 - r) for d in range(count) for r in range(2)]
            return lax.ppermute(x, ("tiles", "rep"), pairs)

        across = cross(edges, lambda d: d ^ 2)
        beside = lax.ppermute(edges, "rep", swap)
        other = cross(rounded, lambda d: d ^ 2)
        rounded = (rounded.astype(F32) + other.astype(F32)).astype(BF16)
        both = cross(jnp.concatenate([rounded, beside, across], axis=0), lambda d: d ^ 1)
        sums = rounded.astype(F32) + both[:half_rows].astype(F32)
        across = lax.ppermute(across, "rep", swap)
        returned = [both[half_rows + own :], across, both[half_rows : half_rows + own], edges]
    else:
        for step in range(count.bit_length() - 1):
            other = move(rounded, lambda d: d ^ (1 << step))
            sums = rounded.astype(F32) + other.astype(F32)
            rounded = sums.astype(BF16)
        returned = [
            lax.ppermute(edges, "tiles", [(route(j), j) for j in range(count)]) for route, _ in plans
        ]
    grad_scale = 1.0 / math.sqrt(reps * fields.shape[0] * count * SLOTS * CELLS)
    sums = sums * grad_scale
    grad_fields = call(
        finish_kernel,
        [VMEM] * (1 + 2 * n),
        [struct((1, SLOTS, own, CELLS), BF16)],
    )(base, *returned, *maps)[0]
    grad_weights, grad_bias = call(
        lambda *refs: gather_kernel(*refs, count=count),
        [VMEM, VMEM],
        [struct((9, own, C), F32), struct((1, own), F32)],
    )(sums, lax.ppermute(sums, "rep", swap))
    return (result, grad_fields, grad_weights, grad_bias.reshape(own))


def solution(mesh):
    in_specs = (
        P(("groups", "rep"), "tiles", None, None),
        P(),
        P(None, "chan", None),
        P("chan"),
        P(("groups", "rep"), "tiles", "chan", None),
    )
    out_specs = (
        P(("groups", "rep"), "tiles", "chan", None),
        P(("groups", "rep"), "tiles", "chan", None),
        P("groups", "chan", None),
        P(("groups", "chan")),
    )
    return jax.shard_map(
        on_device, mesh=mesh, in_specs=in_specs, out_specs=out_specs, check_vma=False
    )
```

```python
import math

import jax
import jax.numpy as jnp
from jax import lax
from jax.experimental import pallas as pl
from jax.experimental.pallas import tpu as pltpu
from jax.sharding import PartitionSpec as P

C = 128
TS = 16
SLOTS = 3
CELLS = TS * TS
FRAME = 384
EDGE = TS + 2
EAST = SLOTS * EDGE
FOLD = 2 * SLOTS * EDGE
F32 = jnp.float32
BF16 = jnp.bfloat16
GELU_C = math.sqrt(2.0 / math.pi)
GELU_K = 0.044715


def iota(shape, dim):
    return lax.broadcasted_iota(jnp.int32, shape, dim)


def halo_plans(count):
    if count == 4:
        return [
            (lambda d: 3 - d, ("side", "fold")),
            (lambda d: d ^ 2, ("corner",)),
            (lambda d: d ^ 1, ("side",)),
            (None, ("corner",)),
        ]
    return [
        (lambda d: (d + 1) % count, ("west",)),
        (lambda d: (d + count - 1) % count, ("east",)),
        (lambda d: count - 1 - d, ("fold",)),
        (lambda d: (count - d) % count, ("corner_west",)),
        (lambda d: (2 * count - 2 - d) % count, ("corner_east",)),
    ]


def halo_sources(rows, count, source, target, roles):
    lane = iota((8, 128), 1)
    top = 2 * SLOTS - 1
    east = (lane >= EAST) & (lane < FOLD)
    at = lane - jnp.where(east, EAST, 0)
    k = jnp.where(at >= EDGE, 1, 0) + jnp.where(at >= 2 * EDGE, 1, 0)
    p = at - EDGE * k
    rim = lane < FOLD
    row = jnp.where(k == 0, rows[target, 0], jnp.where(k == 1, rows[target, 1], rows[target, 2]))
    row = jnp.where(rim, row, -1)
    src = jnp.full((8, 128), -1, jnp.int32)
    sides = [name for name in ("west", "east") if name in roles or "side" in roles]
    if sides:
        wanted = row + jnp.where(p == TS + 1, 1, 0) - jnp.where(p == 0, 1, 0)
        slot = jnp.full((8, 128), -1, jnp.int32)
        present = (p > 0) & (p <= TS)
        for l in range(SLOTS):
            slot = jnp.where(wanted == rows[source, l], l, slot)
            present = present | (wanted == rows[target, l])
        cell = jnp.where(p == 0, CELLS - TS, jnp.where(p == TS + 1, 0, TS * (p - 1))) + jnp.where(east, 0, TS - 1)
        good = present & (row >= 0) & (wanted >= 0) & (slot >= 0)
        from_west = target == (source + 1) % count if "west" in sides else False
        from_east = target == (source + count - 1) % count if "east" in sides else False
        good = good & ((jnp.logical_not(east) & from_west) | (east & from_east))
        src = jnp.where(good, slot * CELLS + cell, src)

    def top_slot(column):
        found = jnp.int32(-1)
        for l in range(SLOTS):
            found = jnp.where(rows[column, l] == top, l, found)
        return found

    if sides and len(sides) == len(roles) and "side" not in roles or roles == ("side",):
        return src
    mine = top_slot(source)
    if "fold" in roles:
        good = (lane >= FOLD) & (lane < FOLD + TS) & (mine >= 0) & (target == count - 1 - source)
        src = jnp.where(good, mine * CELLS + (CELLS - 1 + FOLD) - lane, src)
    corners = [name for name in ("west", "east") if "corner" in roles or f"corner_{name}" in roles]
    if corners:
        good = (row == top) & (p == TS + 1) & (mine >= 0) & (top_slot(count - 1 - target) >= 0)
        from_west = target == (count - source) % count if "west" in corners else False
        from_east = target == (2 * count - 2 - source) % count if "east" in corners else False
        good = good & ((jnp.logical_not(east) & from_west) | (east & from_east))
        src = jnp.where(good, mine * CELLS + CELLS - TS + jnp.where(east, TS - 1, 0), src)
    return src


def halo_map(rows, count, source, plan):
    route, roles = plan
    target = source if route is None else route(source)
    src = halo_sources(rows, count, source, target, roles)
    hits = iota((SLOTS * CELLS, 128), 0) == src[0:1, :]
    return jnp.where(hits, 1.0, 0.0).astype(BF16)


def dot(lhs, rhs, dims=((1,), (0,))):
    return lax.dot_general(lhs, rhs, (dims, ((), ())), preferred_element_type=F32)


def pack_kernel(rows_hbm, fields_hbm, weights_hbm, bias_hbm, cot_hbm, *refs, count):
    n = len(halo_plans(count))
    rows_out, fields_out, weights_out, bias_out, cot_out = refs[:5]
    maps = refs[5 : 5 + n]
    outs = refs[5 + n : -2]
    rows, sem = refs[-2:]
    moves = [
        (rows_hbm, rows),
        (fields_hbm.at[0], fields_out),
        (weights_hbm, weights_out),
        (bias_hbm, bias_out),
        (cot_hbm.at[0], cot_out),
    ]
    copies = [pltpu.make_async_copy(src, dst, sem.at[i]) for i, (src, dst) in enumerate(moves)]
    for copy in copies:
        copy.start()
    copies[0].wait()
    position = lax.axis_index("tiles")
    plans = halo_plans(count)
    for plan, out in zip(plans, maps):
        out[...] = halo_map(rows, count, position, plan)
    put_rows = pltpu.make_async_copy(rows, rows_out, sem.at[0])
    put_rows.start()
    copies[1].wait()
    cells = jnp.concatenate([fields_out[k] for k in range(SLOTS)], axis=1)
    for out, hits in zip(outs, maps):
        out[...] = dot(cells, hits[...]).astype(BF16)
    for copy in copies[2:]:
        copy.wait()
    put_rows.wait()


def flag(condition):
    return jnp.where(condition, 1.0, 0.0).astype(F32)


def slot_flags(rows):
    position = lax.axis_index("tiles")
    row = [rows[position, k] for k in range(SLOTS)]
    full = [flag(r >= 0) for r in row]
    at_top = [flag(r == 2 * SLOTS - 1) for r in row]
    above = [[flag((row[k] >= 0) & (row[l] == row[k] + 1)) for l in range(SLOTS)] for k in range(SLOTS)]
    return full, at_top, above


def turn(stack, turned):
    own = stack.shape[0] // 3
    start = pl.multiple_of(lax.axis_index("chan") * own, own)
    turned[...] = jnp.transpose(stack.astype(F32))
    return jnp.concatenate([turned[pl.ds(b * C + start, own), :] for b in range(3)], axis=0).astype(BF16)


def stack_of(taps):
    return jnp.concatenate(
        [jnp.concatenate([taps[3 * a + b] for b in range(3)], axis=1) for a in range(3)], axis=0
    )


def window_kernel(rows, fields, weights, windows, spreads, gathers, kernel, back_kernel, turned):
    own = kernel.shape[0] // 3
    full, _, above = slot_flags(rows)
    column = iota((1, FRAME), 1) % TS
    lane128 = iota((1, 128), 1)
    tiles = [fields[k].astype(F32) * full[k] for k in range(SLOTS)]
    for k in range(SLOTS):
        north = jnp.zeros((C, 128), F32)
        south = jnp.zeros((C, 128), F32)
        for l in range(SLOTS):
            if l != k:
                north = north + above[k][l] * tiles[l][:, :128]
                south = south + above[l][k] * tiles[l][:, 128:]
        ends = jnp.where(lane128 < TS, north, jnp.where(lane128 >= 128 - TS, south, 0.0))
        centre = jnp.concatenate([tiles[k], ends], axis=1)
        windows[k, :C] = jnp.where(column == 0, 0.0, pltpu.roll(centre, 1, 1)).astype(BF16)
        windows[k, C : 2 * C] = centre.astype(BF16)
        windows[k, 2 * C :] = jnp.where(column == TS - 1, 0.0, pltpu.roll(centre, FRAME - 1, 1)).astype(BF16)
    for refs, shape, halo_dim in ((spreads, (128, FRAME), 0), (gathers, (FRAME, 128), 1)):
        p_at = iota(shape, halo_dim)
        frame_lane = iota(shape, 1 - halo_dim)
        for side in range(2):
            for k in range(SLOTS):
                p = p_at - (side * EAST + k * EDGE)
                spot = jnp.where(p == 0, FRAME - TS, TS * (p - 1)) + side * (TS - 1)
                hits = (p >= 0) & (p < EDGE) & (frame_lane == spot)
                refs[side, k] = jnp.where(hits, 1.0, 0.0).astype(BF16)
    stack = stack_of(weights)
    kernel[...] = stack
    back_kernel[...] = turn(stack, turned)


def column_of(line):
    own = line.shape[1]
    eye = iota((own, own), 0) == iota((own, own), 1)
    return jnp.sum(jnp.where(eye, line, 0.0), axis=1, keepdims=True)


def activation(kernel, window, bias_column, up):
    own = bias_column.shape[0]
    sums = dot(kernel, window)
    pre = (
        pltpu.roll(sums[:own], TS, 1)[:, :CELLS]
        + sums[own : 2 * own, :CELLS]
        + pltpu.roll(sums[2 * own :], FRAME - TS, 1)[:, :CELLS]
        + bias_column
    )
    square = pre * pre
    tanh = jnp.tanh(GELU_C * (pre * (1.0 + GELU_K * square)))
    half = 0.5 + 0.5 * tanh
    slope = half + (0.5 * pre) * (1.0 - tanh * tanh) * (GELU_C + (3.0 * GELU_C * GELU_K) * square)
    return pre * half, (up * slope).astype(BF16).astype(F32)


def frame_of(slopes):
    own = slopes.shape[0]
    wide = jnp.concatenate([slopes, jnp.zeros((own, FRAME - CELLS), F32)], axis=1)
    return jnp.concatenate([pltpu.roll(wide, FRAME - TS, 1), wide, pltpu.roll(wide, TS, 1)], axis=0).astype(BF16)


def half_of(count):
    position = lax.axis_index("tiles")
    rep = lax.axis_index("rep")
    if count == 4:
        return (rep + position + position // 2) % 2
    return rep


def forward_kernel(rows, fields, bias, cot, kernel, spreads, windows, *refs, n_halos, half_rows, count):
    halos = refs[:n_halos]
    frames, slopes_out, result, keep, send = refs[n_halos:]
    own = kernel.shape[0] // 3
    full, at_top, _ = slot_flags(rows)
    start = pl.multiple_of(lax.axis_index("chan") * own, own)
    half = half_of(count)
    lane128 = iota((1, 128), 1)
    bias_column = column_of(bias[...])
    halo = halos[0][...].astype(F32)
    for ref in halos[1:]:
        halo = halo + ref[...].astype(F32)
    turned = pltpu.roll(halo, 128 - FOLD, 1)
    fold = jnp.where(lane128 < TS, turned, 0.0)
    fold_left = jnp.where((lane128 > 0) & (lane128 < TS), pltpu.roll(turned, 1, 1), 0.0)
    fold_right = jnp.where(lane128 < TS - 1, pltpu.roll(turned, 127, 1), 0.0)
    halo = halo.astype(BF16)
    grads = jnp.zeros((3 * own, 3 * C), F32)
    slope_sum = jnp.zeros((own, CELLS), F32)
    for k in range(SLOTS):
        west = dot(halo, spreads[0, k])
        east = dot(halo, spreads[1, k])
        rest = jnp.zeros((C, CELLS), F32)
        left = windows[k, :C] + (west + jnp.concatenate([rest, at_top[k] * fold_left], axis=1)).astype(BF16)
        right = windows[k, 2 * C :] + (east + jnp.concatenate([rest, at_top[k] * fold_right], axis=1)).astype(BF16)
        centre = windows[k, C : 2 * C] + jnp.concatenate([rest, at_top[k] * fold], axis=1).astype(BF16)
        window = jnp.concatenate([left, centre, right], axis=0)
        up = cot[k].astype(F32) * full[k]
        gelu, slopes = activation(kernel[...], window, bias_column, up)
        result[k] = (full[k] * (fields[k, pl.ds(start, own), :].astype(F32) + gelu)).astype(BF16)
        slope_sum = slope_sum + slopes
        slopes_out[k * own : (k + 1) * own, :] = slopes.astype(BF16)
        frame = frame_of(slopes)
        frames[k] = frame
        grads = grads + dot(frame, window, ((1,), (1,)))
    blocks = [grads[a * own : (a + 1) * own, b * C : (b + 1) * C] for a in range(3) for b in range(3)]
    eye = iota((own, 128), 0) == iota((own, 128), 1)
    bias_line = jnp.sum(jnp.where(eye, jnp.sum(slope_sum, axis=1, keepdims=True), 0.0), axis=0, keepdims=True)
    blocks.append(bias_line)
    blocks.append(jnp.zeros((2 * half_rows - 9 * own - 1, 128), F32))
    sums = jnp.concatenate(blocks, axis=0)
    low, high = sums[:half_rows], sums[half_rows:]
    keep[...] = jnp.where(half == 0, low, high)
    send[...] = jnp.where(half == 0, high, low)


def turn_kernel(*refs):
    n = (len(refs) - 1) // 2
    for ref, back_kernel in zip(refs[:n], refs[n : 2 * n]):
        back_kernel[...] = turn(stack_of(ref), refs[-1])


def backward_kernel(rows, cot, gathers, result, own_frames, *refs):
    base, edges, result_out, sem = refs[-4:]
    n = (len(refs) - 5) // 2
    slopes, back_kernels = refs[:n], refs[n : 2 * n + 1]
    own = back_kernels[0].shape[0] // 3
    put = pltpu.make_async_copy(result, result_out.at[0], sem)
    put.start()
    full, at_top, above = slot_flags(rows)
    column = iota((1, FRAME), 1) % TS
    lane128 = iota((1, 128), 1)
    edge_sum = jnp.zeros((own, 128), F32)
    pads = []
    for k in range(SLOTS):
        spread = dot(back_kernels[0][...], own_frames[k])
        for other, back_kernel in zip(slopes, back_kernels[1:]):
            frame = frame_of(other[k * own : (k + 1) * own, :].astype(F32))
            spread = spread + dot(back_kernel[...], frame)
        first, second, third = spread[:own], spread[own : 2 * own], spread[2 * own :]
        pad = (
            second
            + jnp.where(column < TS - 1, pltpu.roll(first, FRAME - 1, 1), 0.0)
            + jnp.where(column > 0, pltpu.roll(third, 1, 1), 0.0)
        )
        pads.append(pad)
        edge_sum = edge_sum + dot(first.astype(BF16), gathers[0, k])
        edge_sum = edge_sum + dot(third.astype(BF16), gathers[1, k])
        crest = jnp.where(lane128 < TS, pad[:, CELLS:], 0.0) * at_top[k]
        edge_sum = edge_sum + pltpu.roll(crest, FOLD, 1)
    edges[...] = edge_sum.astype(BF16)
    for k in range(SLOTS):
        first = pads[k][:, :128]
        second = pads[k][:, 128:CELLS]
        for l in range(SLOTS):
            if l != k:
                ends = pads[l][:, CELLS:]
                first = first + jnp.where(lane128 < TS, ends, 0.0) * above[l][k]
                second = second + jnp.where(lane128 >= 128 - TS, ends, 0.0) * above[k][l]
        base[k] = cot[k].astype(F32) * full[k] + jnp.concatenate([first, second], axis=1)
    put.wait()


def finish_kernel(base, *refs):
    out = refs[-1]
    n = len(refs) // 2
    total = None
    for received, hits in zip(refs[:n], refs[n:]):
        part = dot(received[...], hits[...], ((1,), (1,)))
        total = part if total is None else total + part
    for k in range(SLOTS):
        out[0, k] = (base[k] + total[:, k * CELLS : (k + 1) * CELLS]).astype(BF16)


def gather_kernel(mine, theirs, weights_out, bias_out, *, count):
    half = half_of(count)
    own = weights_out.shape[1]
    low = jnp.where(half == 0, mine[...], theirs[...])
    high = jnp.where(half == 0, theirs[...], mine[...])
    sums = jnp.concatenate([low, high], axis=0)
    for t in range(9):
        weights_out[t] = sums[t * own : (t + 1) * own]
    bias_out[...] = sums[9 * own : 9 * own + 1, :own]


SMEM = pl.BlockSpec(memory_space=pltpu.SMEM)
VMEM = pl.BlockSpec(memory_space=pltpu.VMEM)
HBM = pl.BlockSpec(memory_space=pltpu.HBM)


def call(kernel, specs, outs, scratch=(), out_specs=None, cost=None):
    return pl.pallas_call(
        kernel,
        in_specs=specs,
        out_specs=out_specs or [VMEM] * len(outs),
        out_shape=outs,
        scratch_shapes=list(scratch),
        cost_estimate=cost,
        compiler_params=pltpu.CompilerParams(vmem_limit_bytes=40 << 20),
    )


def struct(shape, dtype):
    return jax.ShapeDtypeStruct(shape, dtype)


def on_device(fields, tile_rows, weights, bias, cotangent):
    own = weights.shape[1]
    count = lax.axis_size("tiles")
    chans = lax.axis_size("chan")
    reps = lax.axis_size("rep")
    plans = halo_plans(count)
    n = len(plans)
    half_rows = -(-(9 * own + 1) // 32) * 16
    swap = [(0, 1), (1, 0)]

    pinned = [
        pltpu.with_memory_space_constraint(x, pltpu.HBM)
        for x in (tile_rows, fields, weights, bias.reshape(1, own), cotangent)
    ]
    rows, tiles, taps, bias_line, cot, *packed = call(
        lambda *refs: pack_kernel(*refs, count=count),
        [HBM] * 5,
        [
            struct(tile_rows.shape, jnp.int32),
            struct((SLOTS, C, CELLS), BF16),
            struct((9, own, C), BF16),
            struct((1, own), F32),
            struct((SLOTS, own, CELLS), BF16),
        ]
        + [struct((SLOTS * CELLS, 128), BF16)] * n
        + [struct((C, 128), BF16)] * n,
        [pltpu.SMEM(tile_rows.shape, jnp.int32), pltpu.SemaphoreType.DMA((5,))],
    )(*pinned)
    maps, messages = packed[:n], packed[n:]

    def move(x, route):
        return lax.ppermute(x, "tiles", [(i, route(i)) for i in range(count)])

    halos = [x if route is None else move(x, route) for x, (route, _) in zip(messages, plans)]
    ring = [[(i, (i + s) % chans) for i in range(chans)] for s in range(1, chans)]
    others = [lax.ppermute(taps, "chan", pairs) for pairs in ring]

    windows, spreads, gathers, kernel, back_kernel = call(
        window_kernel,
        [SMEM] + [VMEM] * 2,
        [
            struct((SLOTS, 3 * C, FRAME), BF16),
            struct((2, SLOTS, 128, FRAME), BF16),
            struct((2, SLOTS, FRAME, 128), BF16),
            struct((3 * own, 3 * C), BF16),
            struct((3 * own, 3 * own), BF16),
        ],
        [pltpu.VMEM((3 * C, 3 * own), F32)],
    )(rows, tiles, taps)

    frames, slopes, result, keep, send = call(
        lambda *refs: forward_kernel(*refs, n_halos=len(halos), half_rows=half_rows, count=count),
        [SMEM] + [VMEM] * (6 + len(halos)),
        [
            struct((SLOTS, 3 * own, FRAME), BF16),
            struct((SLOTS * own, CELLS), BF16),
            struct((SLOTS, own, CELLS), BF16),
            struct((half_rows, 128), F32),
            struct((half_rows, 128), F32),
        ],
        cost=pl.CostEstimate(flops=4 * 10**9, transcendentals=0, bytes_accessed=0),
    )(rows, tiles, bias_line, cot, kernel, spreads, windows, *halos)

    met = [lax.ppermute(slopes, "chan", pairs) for pairs in ring]
    send, others = lax.optimization_barrier((send, others))
    sums = keep + lax.ppermute(send, "rep", swap)
    rounded = sums.astype(BF16)
    frames, rounded, others = lax.optimization_barrier((frames, rounded, others))
    turned = call(
        turn_kernel,
        [VMEM] * len(others),
        [struct((3 * own, 3 * own), BF16)] * len(others),
        [pltpu.VMEM((3 * C, 3 * own), F32)],
    )(*others)

    base, edges, result = call(
        backward_kernel,
        [SMEM] + [VMEM] * (5 + 2 * len(others)),
        [
            struct((SLOTS, own, CELLS), F32),
            struct((own, 128), BF16),
            struct((1, SLOTS, own, CELLS), BF16),
        ],
        [pltpu.SemaphoreType.DMA],
        out_specs=[VMEM, VMEM, HBM],
    )(rows, cot, gathers, result, frames, *met, back_kernel, *turned)

    if count == 4:

        def cross(x, route):
            pairs = [(2 * d + r, 2 * route(d) + 1 - r) for d in range(count) for r in range(2)]
            return lax.ppermute(x, ("tiles", "rep"), pairs)

        across = cross(edges, lambda d: d ^ 2)
        beside = lax.ppermute(edges, "rep", swap)
        other = cross(rounded, lambda d: d ^ 2)
        rounded = (rounded.astype(F32) + other.astype(F32)).astype(BF16)
        sums = rounded.astype(F32) + cross(rounded, lambda d: d ^ 1).astype(F32)
        both = cross(jnp.concatenate([beside, across], axis=0), lambda d: d ^ 1)
        across = lax.ppermute(across, "rep", swap)
        returned = [both[own:], across, both[:own], edges]
    else:
        for step in range(count.bit_length() - 1):
            other = move(rounded, lambda d: d ^ (1 << step))
            sums = rounded.astype(F32) + other.astype(F32)
            rounded = sums.astype(BF16)
        returned = [
            lax.ppermute(edges, "tiles", [(route(j), j) for j in range(count)]) for route, _ in plans
        ]
    grad_scale = 1.0 / math.sqrt(reps * fields.shape[0] * count * SLOTS * CELLS)
    sums = sums * grad_scale
    grad_fields = call(
        finish_kernel,
        [VMEM] * (1 + 2 * n),
        [struct((1, SLOTS, own, CELLS), BF16)],
    )(base, *returned, *maps)[0]
    grad_weights, grad_bias = call(
        lambda *refs: gather_kernel(*refs, count=count),
        [VMEM, VMEM],
        [struct((9, own, C), F32), struct((1, own), F32)],
    )(sums, lax.ppermute(sums, "rep", swap))
    return (result, grad_fields, grad_weights, grad_bias.reshape(own))


def solution(mesh):
    in_specs = (
        P(("groups", "rep"), "tiles", None, None),
        P(),
        P(None, "chan", None),
        P("chan"),
        P(("groups", "rep"), "tiles", "chan", None),
    )
    out_specs = (
        P(("groups", "rep"), "tiles", "chan", None),
        P(("groups", "rep"), "tiles", "chan", None),
        P("groups", "chan", None),
        P(("groups", "chan")),
    )
    return jax.shard_map(
        on_device, mesh=mesh, in_specs=in_specs, out_specs=out_specs, check_vma=False
    )
```

```python
import math

import jax
import jax.numpy as jnp
from jax import lax
from jax.experimental import pallas as pl
from jax.experimental.pallas import tpu as pltpu
from jax.sharding import PartitionSpec as P

C = 128
TS = 16
SLOTS = 3
CELLS = TS * TS
FRAME = 384
EDGE = TS + 2
EAST = SLOTS * EDGE
FOLD = 2 * SLOTS * EDGE
F32 = jnp.float32
BF16 = jnp.bfloat16
GELU_C = math.sqrt(2.0 / math.pi)
GELU_K = 0.044715


def iota(shape, dim):
    return lax.broadcasted_iota(jnp.int32, shape, dim)


def halo_plans(count):
    if count == 4:
        return [
            (lambda d: 3 - d, ("side", "fold")),
            (lambda d: d ^ 2, ("corner",)),
            (lambda d: d ^ 1, ("side",)),
            (None, ("corner",)),
        ]
    return [
        (lambda d: (d + 1) % count, ("west",)),
        (lambda d: (d + count - 1) % count, ("east",)),
        (lambda d: count - 1 - d, ("fold",)),
        (lambda d: (count - d) % count, ("corner_west",)),
        (lambda d: (2 * count - 2 - d) % count, ("corner_east",)),
    ]


def halo_sources(rows, count, source, target, roles):
    lane = iota((8, 128), 1)
    top = 2 * SLOTS - 1
    east = (lane >= EAST) & (lane < FOLD)
    at = lane - jnp.where(east, EAST, 0)
    k = jnp.where(at >= EDGE, 1, 0) + jnp.where(at >= 2 * EDGE, 1, 0)
    p = at - EDGE * k
    rim = lane < FOLD
    row = jnp.where(k == 0, rows[target, 0], jnp.where(k == 1, rows[target, 1], rows[target, 2]))
    row = jnp.where(rim, row, -1)
    src = jnp.full((8, 128), -1, jnp.int32)
    sides = [name for name in ("west", "east") if name in roles or "side" in roles]
    if sides:
        wanted = row + jnp.where(p == TS + 1, 1, 0) - jnp.where(p == 0, 1, 0)
        slot = jnp.full((8, 128), -1, jnp.int32)
        present = (p > 0) & (p <= TS)
        for l in range(SLOTS):
            slot = jnp.where(wanted == rows[source, l], l, slot)
            present = present | (wanted == rows[target, l])
        cell = jnp.where(p == 0, CELLS - TS, jnp.where(p == TS + 1, 0, TS * (p - 1))) + jnp.where(east, 0, TS - 1)
        good = present & (row >= 0) & (wanted >= 0) & (slot >= 0)
        from_west = target == (source + 1) % count if "west" in sides else False
        from_east = target == (source + count - 1) % count if "east" in sides else False
        good = good & ((jnp.logical_not(east) & from_west) | (east & from_east))
        src = jnp.where(good, slot * CELLS + cell, src)

    def top_slot(column):
        found = jnp.int32(-1)
        for l in range(SLOTS):
            found = jnp.where(rows[column, l] == top, l, found)
        return found

    if sides and len(sides) == len(roles) and "side" not in roles or roles == ("side",):
        return src
    mine = top_slot(source)
    if "fold" in roles:
        good = (lane >= FOLD) & (lane < FOLD + TS) & (mine >= 0) & (target == count - 1 - source)
        src = jnp.where(good, mine * CELLS + (CELLS - 1 + FOLD) - lane, src)
    corners = [name for name in ("west", "east") if "corner" in roles or f"corner_{name}" in roles]
    if corners:
        good = (row == top) & (p == TS + 1) & (mine >= 0) & (top_slot(count - 1 - target) >= 0)
        from_west = target == (count - source) % count if "west" in corners else False
        from_east = target == (2 * count - 2 - source) % count if "east" in corners else False
        good = good & ((jnp.logical_not(east) & from_west) | (east & from_east))
        src = jnp.where(good, mine * CELLS + CELLS - TS + jnp.where(east, TS - 1, 0), src)
    return src


def halo_map(rows, count, source, plan):
    route, roles = plan
    target = source if route is None else route(source)
    src = halo_sources(rows, count, source, target, roles)
    hits = iota((SLOTS * CELLS, 128), 0) == src[0:1, :]
    return jnp.where(hits, 1.0, 0.0).astype(BF16)


def dot(lhs, rhs, dims=((1,), (0,))):
    return lax.dot_general(lhs, rhs, (dims, ((), ())), preferred_element_type=F32)


def pack_kernel(rows_hbm, fields_hbm, weights_hbm, bias_hbm, cot_hbm, *refs, count):
    n = len(halo_plans(count))
    rows_out, fields_out, weights_out, bias_out, cot_out = refs[:5]
    maps = refs[5 : 5 + n]
    outs = refs[5 + n : -2]
    rows, sem = refs[-2:]
    moves = [
        (rows_hbm, rows),
        (fields_hbm.at[0], fields_out),
        (weights_hbm, weights_out),
        (bias_hbm, bias_out),
        (cot_hbm.at[0], cot_out),
    ]
    copies = [pltpu.make_async_copy(src, dst, sem.at[i]) for i, (src, dst) in enumerate(moves)]
    for copy in copies:
        copy.start()
    copies[0].wait()
    position = lax.axis_index("tiles")
    plans = halo_plans(count)
    for plan, out in zip(plans, maps):
        out[...] = halo_map(rows, count, position, plan)
    put_rows = pltpu.make_async_copy(rows, rows_out, sem.at[0])
    put_rows.start()
    copies[1].wait()
    cells = jnp.concatenate([fields_out[k] for k in range(SLOTS)], axis=1)
    for out, hits in zip(outs, maps):
        out[...] = dot(cells, hits[...]).astype(BF16)
    for copy in copies[2:]:
        copy.wait()
    put_rows.wait()


def flag(condition):
    return jnp.where(condition, 1.0, 0.0).astype(F32)


def slot_flags(rows):
    position = lax.axis_index("tiles")
    row = [rows[position, k] for k in range(SLOTS)]
    full = [flag(r >= 0) for r in row]
    at_top = [flag(r == 2 * SLOTS - 1) for r in row]
    above = [[flag((row[k] >= 0) & (row[l] == row[k] + 1)) for l in range(SLOTS)] for k in range(SLOTS)]
    return full, at_top, above


def turn(stack, turned):
    own = stack.shape[0] // 3
    start = pl.multiple_of(lax.axis_index("chan") * own, own)
    turned[...] = jnp.transpose(stack.astype(F32))
    return jnp.concatenate([turned[pl.ds(b * C + start, own), :] for b in range(3)], axis=0).astype(BF16)


def stack_of(taps):
    return jnp.concatenate(
        [jnp.concatenate([taps[3 * a + b] for b in range(3)], axis=1) for a in range(3)], axis=0
    )


def window_kernel(rows, fields, weights, windows, spreads, gathers, kernel, back_kernel, turned):
    own = kernel.shape[0] // 3
    full, _, above = slot_flags(rows)
    column = iota((1, FRAME), 1) % TS
    lane128 = iota((1, 128), 1)
    tiles = [fields[k].astype(F32) * full[k] for k in range(SLOTS)]
    for k in range(SLOTS):
        north = jnp.zeros((C, 128), F32)
        south = jnp.zeros((C, 128), F32)
        for l in range(SLOTS):
            if l != k:
                north = north + above[k][l] * tiles[l][:, :128]
                south = south + above[l][k] * tiles[l][:, 128:]
        ends = jnp.where(lane128 < TS, north, jnp.where(lane128 >= 128 - TS, south, 0.0))
        centre = jnp.concatenate([tiles[k], ends], axis=1)
        windows[k, :C] = jnp.where(column == 0, 0.0, pltpu.roll(centre, 1, 1)).astype(BF16)
        windows[k, C : 2 * C] = centre.astype(BF16)
        windows[k, 2 * C :] = jnp.where(column == TS - 1, 0.0, pltpu.roll(centre, FRAME - 1, 1)).astype(BF16)
    for refs, shape, halo_dim in ((spreads, (128, FRAME), 0), (gathers, (FRAME, 128), 1)):
        p_at = iota(shape, halo_dim)
        frame_lane = iota(shape, 1 - halo_dim)
        for side in range(2):
            for k in range(SLOTS):
                p = p_at - (side * EAST + k * EDGE)
                spot = jnp.where(p == 0, FRAME - TS, TS * (p - 1)) + side * (TS - 1)
                hits = (p >= 0) & (p < EDGE) & (frame_lane == spot)
                refs[side, k] = jnp.where(hits, 1.0, 0.0).astype(BF16)
    stack = stack_of(weights)
    kernel[...] = stack
    back_kernel[...] = turn(stack, turned)


def column_of(line):
    own = line.shape[1]
    eye = iota((own, own), 0) == iota((own, own), 1)
    return jnp.sum(jnp.where(eye, line, 0.0), axis=1, keepdims=True)


def activation(kernel, window, bias_column, up):
    own = bias_column.shape[0]
    sums = dot(kernel, window)
    pre = (
        pltpu.roll(sums[:own], TS, 1)[:, :CELLS]
        + sums[own : 2 * own, :CELLS]
        + pltpu.roll(sums[2 * own :], FRAME - TS, 1)[:, :CELLS]
        + bias_column
    )
    square = pre * pre
    tanh = jnp.tanh(GELU_C * (pre * (1.0 + GELU_K * square)))
    half = 0.5 + 0.5 * tanh
    slope = half + (0.5 * pre) * (1.0 - tanh * tanh) * (GELU_C + (3.0 * GELU_C * GELU_K) * square)
    return pre * half, (up * slope).astype(BF16).astype(F32)


def frame_of(slopes):
    own = slopes.shape[0]
    wide = jnp.concatenate([slopes, jnp.zeros((own, FRAME - CELLS), F32)], axis=1)
    return jnp.concatenate([pltpu.roll(wide, FRAME - TS, 1), wide, pltpu.roll(wide, TS, 1)], axis=0).astype(BF16)


def half_of(count):
    position = lax.axis_index("tiles")
    rep = lax.axis_index("rep")
    if count == 4:
        return (rep + position + position // 2) % 2
    return rep


def forward_kernel(rows, fields, bias, cot, kernel, spreads, windows, *refs, n_halos, half_rows, count):
    halos = refs[:n_halos]
    frames, slopes_out, result, keep, send = refs[n_halos:]
    own = kernel.shape[0] // 3
    full, at_top, _ = slot_flags(rows)
    start = pl.multiple_of(lax.axis_index("chan") * own, own)
    half = half_of(count)
    lane128 = iota((1, 128), 1)
    bias_column = column_of(bias[...])
    halo = halos[0][...].astype(F32)
    for ref in halos[1:]:
        halo = halo + ref[...].astype(F32)
    turned = pltpu.roll(halo, 128 - FOLD, 1)
    fold = jnp.where(lane128 < TS, turned, 0.0)
    fold_left = jnp.where((lane128 > 0) & (lane128 < TS), pltpu.roll(turned, 1, 1), 0.0)
    fold_right = jnp.where(lane128 < TS - 1, pltpu.roll(turned, 127, 1), 0.0)
    halo = halo.astype(BF16)
    slope_frames, full_windows = [], []
    slope_sum = jnp.zeros((own, CELLS), F32)
    for k in range(SLOTS):
        west = dot(halo, spreads[0, k])
        east = dot(halo, spreads[1, k])
        rest = jnp.zeros((C, CELLS), F32)
        left = windows[k, :C] + (west + jnp.concatenate([rest, at_top[k] * fold_left], axis=1)).astype(BF16)
        right = windows[k, 2 * C :] + (east + jnp.concatenate([rest, at_top[k] * fold_right], axis=1)).astype(BF16)
        centre = windows[k, C : 2 * C] + jnp.concatenate([rest, at_top[k] * fold], axis=1).astype(BF16)
        window = jnp.concatenate([left, centre, right], axis=0)
        up = cot[k].astype(F32) * full[k]
        gelu, slopes = activation(kernel[...], window, bias_column, up)
        result[k] = (full[k] * (fields[k, pl.ds(start, own), :].astype(F32) + gelu)).astype(BF16)
        slope_sum = slope_sum + slopes
        slopes_out[k * own : (k + 1) * own, :] = slopes.astype(BF16)
        frame = frame_of(slopes)
        frames[k] = frame
        slope_frames.append(frame)
        full_windows.append(window)
    grads = dot(jnp.concatenate(slope_frames, axis=1), jnp.concatenate(full_windows, axis=1), ((1,), (1,)))
    blocks = [grads[a * own : (a + 1) * own, b * C : (b + 1) * C] for a in range(3) for b in range(3)]
    eye = iota((own, 128), 0) == iota((own, 128), 1)
    bias_line = jnp.sum(jnp.where(eye, jnp.sum(slope_sum, axis=1, keepdims=True), 0.0), axis=0, keepdims=True)
    blocks.append(bias_line)
    blocks.append(jnp.zeros((2 * half_rows - 9 * own - 1, 128), F32))
    sums = jnp.concatenate(blocks, axis=0)
    low, high = sums[:half_rows], sums[half_rows:]
    keep[...] = jnp.where(half == 0, low, high)
    send[...] = jnp.where(half == 0, high, low)


def turn_kernel(*refs):
    n = (len(refs) - 1) // 2
    for ref, back_kernel in zip(refs[:n], refs[n : 2 * n]):
        back_kernel[...] = turn(stack_of(ref), refs[-1])


def backward_kernel(rows, cot, gathers, result, own_frames, *refs):
    base, edges, result_out, sem = refs[-4:]
    n = (len(refs) - 5) // 2
    slopes, back_kernels = refs[:n], refs[n : 2 * n + 1]
    own = back_kernels[0].shape[0] // 3
    put = pltpu.make_async_copy(result, result_out.at[0], sem)
    put.start()
    full, at_top, above = slot_flags(rows)
    column = iota((1, FRAME), 1) % TS
    lane128 = iota((1, 128), 1)
    edge_sum = jnp.zeros((own, 128), F32)
    pads = []
    for k in range(SLOTS):
        spread = dot(back_kernels[0][...], own_frames[k])
        for other, back_kernel in zip(slopes, back_kernels[1:]):
            frame = frame_of(other[k * own : (k + 1) * own, :].astype(F32))
            spread = spread + dot(back_kernel[...], frame)
        first, second, third = spread[:own], spread[own : 2 * own], spread[2 * own :]
        pad = (
            second
            + jnp.where(column < TS - 1, pltpu.roll(first, FRAME - 1, 1), 0.0)
            + jnp.where(column > 0, pltpu.roll(third, 1, 1), 0.0)
        )
        pads.append(pad)
        edge_sum = edge_sum + dot(first.astype(BF16), gathers[0, k])
        edge_sum = edge_sum + dot(third.astype(BF16), gathers[1, k])
        crest = jnp.where(lane128 < TS, pad[:, CELLS:], 0.0) * at_top[k]
        edge_sum = edge_sum + pltpu.roll(crest, FOLD, 1)
    edges[...] = edge_sum.astype(BF16)
    for k in range(SLOTS):
        first = pads[k][:, :128]
        second = pads[k][:, 128:CELLS]
        for l in range(SLOTS):
            if l != k:
                ends = pads[l][:, CELLS:]
                first = first + jnp.where(lane128 < TS, ends, 0.0) * above[l][k]
                second = second + jnp.where(lane128 >= 128 - TS, ends, 0.0) * above[k][l]
        base[k] = cot[k].astype(F32) * full[k] + jnp.concatenate([first, second], axis=1)
    put.wait()


def finish_kernel(base, *refs):
    out = refs[-1]
    n = len(refs) // 2
    total = None
    for received, hits in zip(refs[:n], refs[n:]):
        part = dot(received[...], hits[...], ((1,), (1,)))
        total = part if total is None else total + part
    for k in range(SLOTS):
        out[0, k] = (base[k] + total[:, k * CELLS : (k + 1) * CELLS]).astype(BF16)


def gather_kernel(mine, theirs, weights_out, bias_out, *, count):
    half = half_of(count)
    own = weights_out.shape[1]
    low = jnp.where(half == 0, mine[...], theirs[...])
    high = jnp.where(half == 0, theirs[...], mine[...])
    sums = jnp.concatenate([low, high], axis=0)
    for t in range(9):
        weights_out[t] = sums[t * own : (t + 1) * own]
    bias_out[...] = sums[9 * own : 9 * own + 1, :own]


SMEM = pl.BlockSpec(memory_space=pltpu.SMEM)
VMEM = pl.BlockSpec(memory_space=pltpu.VMEM)
HBM = pl.BlockSpec(memory_space=pltpu.HBM)


def call(kernel, specs, outs, scratch=(), out_specs=None, cost=None):
    return pl.pallas_call(
        kernel,
        in_specs=specs,
        out_specs=out_specs or [VMEM] * len(outs),
        out_shape=outs,
        scratch_shapes=list(scratch),
        cost_estimate=cost,
        compiler_params=pltpu.CompilerParams(vmem_limit_bytes=40 << 20),
    )


def struct(shape, dtype):
    return jax.ShapeDtypeStruct(shape, dtype)


def on_device(fields, tile_rows, weights, bias, cotangent):
    own = weights.shape[1]
    count = lax.axis_size("tiles")
    chans = lax.axis_size("chan")
    reps = lax.axis_size("rep")
    plans = halo_plans(count)
    n = len(plans)
    half_rows = -(-(9 * own + 1) // 32) * 16
    swap = [(0, 1), (1, 0)]

    pinned = [
        pltpu.with_memory_space_constraint(x, pltpu.HBM)
        for x in (tile_rows, fields, weights, bias.reshape(1, own), cotangent)
    ]
    rows, tiles, taps, bias_line, cot, *packed = call(
        lambda *refs: pack_kernel(*refs, count=count),
        [HBM] * 5,
        [
            struct(tile_rows.shape, jnp.int32),
            struct((SLOTS, C, CELLS), BF16),
            struct((9, own, C), BF16),
            struct((1, own), F32),
            struct((SLOTS, own, CELLS), BF16),
        ]
        + [struct((SLOTS * CELLS, 128), BF16)] * n
        + [struct((C, 128), BF16)] * n,
        [pltpu.SMEM(tile_rows.shape, jnp.int32), pltpu.SemaphoreType.DMA((5,))],
    )(*pinned)
    maps, messages = packed[:n], packed[n:]

    def move(x, route):
        return lax.ppermute(x, "tiles", [(i, route(i)) for i in range(count)])

    halos = [x if route is None else move(x, route) for x, (route, _) in zip(messages, plans)]
    ring = [[(i, (i + s) % chans) for i in range(chans)] for s in range(1, chans)]
    others = [lax.ppermute(taps, "chan", pairs) for pairs in ring]

    windows, spreads, gathers, kernel, back_kernel = call(
        window_kernel,
        [SMEM] + [VMEM] * 2,
        [
            struct((SLOTS, 3 * C, FRAME), BF16),
            struct((2, SLOTS, 128, FRAME), BF16),
            struct((2, SLOTS, FRAME, 128), BF16),
            struct((3 * own, 3 * C), BF16),
            struct((3 * own, 3 * own), BF16),
        ],
        [pltpu.VMEM((3 * C, 3 * own), F32)],
    )(rows, tiles, taps)

    frames, slopes, result, keep, send = call(
        lambda *refs: forward_kernel(*refs, n_halos=len(halos), half_rows=half_rows, count=count),
        [SMEM] + [VMEM] * (6 + len(halos)),
        [
            struct((SLOTS, 3 * own, FRAME), BF16),
            struct((SLOTS * own, CELLS), BF16),
            struct((SLOTS, own, CELLS), BF16),
            struct((half_rows, 128), F32),
            struct((half_rows, 128), F32),
        ],
        cost=pl.CostEstimate(flops=4 * 10**9, transcendentals=0, bytes_accessed=0),
    )(rows, tiles, bias_line, cot, kernel, spreads, windows, *halos)

    met = [lax.ppermute(slopes, "chan", pairs) for pairs in ring]
    send, others = lax.optimization_barrier((send, others))
    sums = keep + lax.ppermute(send, "rep", swap)
    rounded = sums.astype(BF16)
    frames, rounded, others = lax.optimization_barrier((frames, rounded, others))
    turned = call(
        turn_kernel,
        [VMEM] * len(others),
        [struct((3 * own, 3 * own), BF16)] * len(others),
        [pltpu.VMEM((3 * C, 3 * own), F32)],
    )(*others)

    base, edges, result = call(
        backward_kernel,
        [SMEM] + [VMEM] * (5 + 2 * len(others)),
        [
            struct((SLOTS, own, CELLS), F32),
            struct((own, 128), BF16),
            struct((1, SLOTS, own, CELLS), BF16),
        ],
        [pltpu.SemaphoreType.DMA],
        out_specs=[VMEM, VMEM, HBM],
    )(rows, cot, gathers, result, frames, *met, back_kernel, *turned)

    if count == 4:

        def cross(x, route):
            pairs = [(2 * d + r, 2 * route(d) + 1 - r) for d in range(count) for r in range(2)]
            return lax.ppermute(x, ("tiles", "rep"), pairs)

        across = cross(edges, lambda d: d ^ 2)
        beside = lax.ppermute(edges, "rep", swap)
        other = cross(rounded, lambda d: d ^ 2)
        rounded = (rounded.astype(F32) + other.astype(F32)).astype(BF16)
        sums = rounded.astype(F32) + cross(rounded, lambda d: d ^ 1).astype(F32)
        both = cross(jnp.concatenate([beside, across], axis=0), lambda d: d ^ 1)
        across = lax.ppermute(across, "rep", swap)
        returned = [both[own:], across, both[:own], edges]
    else:
        for step in range(count.bit_length() - 1):
            other = move(rounded, lambda d: d ^ (1 << step))
            sums = rounded.astype(F32) + other.astype(F32)
            rounded = sums.astype(BF16)
        returned = [
            lax.ppermute(edges, "tiles", [(route(j), j) for j in range(count)]) for route, _ in plans
        ]
    grad_scale = 1.0 / math.sqrt(reps * fields.shape[0] * count * SLOTS * CELLS)
    sums = sums * grad_scale
    grad_fields = call(
        finish_kernel,
        [VMEM] * (1 + 2 * n),
        [struct((1, SLOTS, own, CELLS), BF16)],
    )(base, *returned, *maps)[0]
    grad_weights, grad_bias = call(
        lambda *refs: gather_kernel(*refs, count=count),
        [VMEM, VMEM],
        [struct((9, own, C), F32), struct((1, own), F32)],
    )(sums, lax.ppermute(sums, "rep", swap))
    return (result, grad_fields, grad_weights, grad_bias.reshape(own))


def solution(mesh):
    in_specs = (
        P(("groups", "rep"), "tiles", None, None),
        P(),
        P(None, "chan", None),
        P("chan"),
        P(("groups", "rep"), "tiles", "chan", None),
    )
    out_specs = (
        P(("groups", "rep"), "tiles", "chan", None),
        P(("groups", "rep"), "tiles", "chan", None),
        P("groups", "chan", None),
        P(("groups", "chan")),
    )
    return jax.shard_map(
        on_device, mesh=mesh, in_specs=in_specs, out_specs=out_specs, check_vma=False
    )
```

```python
import math

import jax
import jax.numpy as jnp
from jax import lax
from jax.experimental import pallas as pl
from jax.experimental.pallas import tpu as pltpu
from jax.sharding import PartitionSpec as P

C = 128
TS = 16
SLOTS = 3
CELLS = TS * TS
FRAME = 384
EDGE = TS + 2
EAST = SLOTS * EDGE
FOLD = 2 * SLOTS * EDGE
F32 = jnp.float32
BF16 = jnp.bfloat16
GELU_C = math.sqrt(2.0 / math.pi)
GELU_K = 0.044715


def iota(shape, dim):
    return lax.broadcasted_iota(jnp.int32, shape, dim)


def halo_plans(count):
    if count == 4:
        return [
            (lambda d: 3 - d, ("side", "fold")),
            (lambda d: d ^ 2, ("corner",)),
            (lambda d: d ^ 1, ("side",)),
            (None, ("corner",)),
        ]
    return [
        (lambda d: (d + 1) % count, ("west",)),
        (lambda d: (d + count - 1) % count, ("east",)),
        (lambda d: count - 1 - d, ("fold",)),
        (lambda d: (count - d) % count, ("corner_west",)),
        (lambda d: (2 * count - 2 - d) % count, ("corner_east",)),
    ]


def halo_sources(rows, count, source, target, roles):
    lane = iota((8, 128), 1)
    top = 2 * SLOTS - 1
    east = (lane >= EAST) & (lane < FOLD)
    at = lane - jnp.where(east, EAST, 0)
    k = jnp.where(at >= EDGE, 1, 0) + jnp.where(at >= 2 * EDGE, 1, 0)
    p = at - EDGE * k
    rim = lane < FOLD
    row = jnp.where(k == 0, rows[target, 0], jnp.where(k == 1, rows[target, 1], rows[target, 2]))
    row = jnp.where(rim, row, -1)
    src = jnp.full((8, 128), -1, jnp.int32)
    sides = [name for name in ("west", "east") if name in roles or "side" in roles]
    if sides:
        wanted = row + jnp.where(p == TS + 1, 1, 0) - jnp.where(p == 0, 1, 0)
        slot = jnp.full((8, 128), -1, jnp.int32)
        present = (p > 0) & (p <= TS)
        for l in range(SLOTS):
            slot = jnp.where(wanted == rows[source, l], l, slot)
            present = present | (wanted == rows[target, l])
        cell = jnp.where(p == 0, CELLS - TS, jnp.where(p == TS + 1, 0, TS * (p - 1))) + jnp.where(east, 0, TS - 1)
        good = present & (row >= 0) & (wanted >= 0) & (slot >= 0)
        from_west = target == (source + 1) % count if "west" in sides else False
        from_east = target == (source + count - 1) % count if "east" in sides else False
        good = good & ((jnp.logical_not(east) & from_west) | (east & from_east))
        src = jnp.where(good, slot * CELLS + cell, src)

    def top_slot(column):
        found = jnp.int32(-1)
        for l in range(SLOTS):
            found = jnp.where(rows[column, l] == top, l, found)
        return found

    if sides and len(sides) == len(roles) and "side" not in roles or roles == ("side",):
        return src
    mine = top_slot(source)
    if "fold" in roles:
        good = (lane >= FOLD) & (lane < FOLD + TS) & (mine >= 0) & (target == count - 1 - source)
        src = jnp.where(good, mine * CELLS + (CELLS - 1 + FOLD) - lane, src)
    corners = [name for name in ("west", "east") if "corner" in roles or f"corner_{name}" in roles]
    if corners:
        good = (row == top) & (p == TS + 1) & (mine >= 0) & (top_slot(count - 1 - target) >= 0)
        from_west = target == (count - source) % count if "west" in corners else False
        from_east = target == (2 * count - 2 - source) % count if "east" in corners else False
        good = good & ((jnp.logical_not(east) & from_west) | (east & from_east))
        src = jnp.where(good, mine * CELLS + CELLS - TS + jnp.where(east, TS - 1, 0), src)
    return src


def halo_map(rows, count, source, plan):
    route, roles = plan
    target = source if route is None else route(source)
    src = halo_sources(rows, count, source, target, roles)
    hits = iota((SLOTS * CELLS, 128), 0) == src[0:1, :]
    return jnp.where(hits, 1.0, 0.0).astype(BF16)


def dot(lhs, rhs, dims=((1,), (0,))):
    return lax.dot_general(lhs, rhs, (dims, ((), ())), preferred_element_type=F32)


def pack_kernel(rows_hbm, fields_hbm, weights_hbm, bias_hbm, cot_hbm, *refs, count):
    n = len(halo_plans(count))
    rows_out, fields_out, weights_out, bias_out, cot_out = refs[:5]
    maps = refs[5 : 5 + n]
    outs = refs[5 + n : -2]
    rows, sem = refs[-2:]
    moves = [
        (rows_hbm, rows),
        (fields_hbm.at[0], fields_out),
        (weights_hbm, weights_out),
        (bias_hbm, bias_out),
        (cot_hbm.at[0], cot_out),
    ]
    copies = [pltpu.make_async_copy(src, dst, sem.at[i]) for i, (src, dst) in enumerate(moves)]
    for copy in copies:
        copy.start()
    copies[0].wait()
    position = lax.axis_index("tiles")
    plans = halo_plans(count)
    for plan, out in zip(plans, maps):
        out[...] = halo_map(rows, count, position, plan)
    put_rows = pltpu.make_async_copy(rows, rows_out, sem.at[0])
    put_rows.start()
    copies[1].wait()
    cells = jnp.concatenate([fields_out[k] for k in range(SLOTS)], axis=1)
    for out, hits in zip(outs, maps):
        out[...] = dot(cells, hits[...]).astype(BF16)
    for copy in copies[2:]:
        copy.wait()
    put_rows.wait()


def flag(condition):
    return jnp.where(condition, 1.0, 0.0).astype(F32)


def slot_flags(rows):
    position = lax.axis_index("tiles")
    row = [rows[position, k] for k in range(SLOTS)]
    full = [flag(r >= 0) for r in row]
    at_top = [flag(r == 2 * SLOTS - 1) for r in row]
    above = [[flag((row[k] >= 0) & (row[l] == row[k] + 1)) for l in range(SLOTS)] for k in range(SLOTS)]
    return full, at_top, above


def turn(stack, turned):
    own = stack.shape[0] // 3
    start = pl.multiple_of(lax.axis_index("chan") * own, own)
    turned[...] = jnp.transpose(stack.astype(F32))
    return jnp.concatenate([turned[pl.ds(b * C + start, own), :] for b in range(3)], axis=0).astype(BF16)


def stack_of(taps):
    return jnp.concatenate(
        [jnp.concatenate([taps[3 * a + b] for b in range(3)], axis=1) for a in range(3)], axis=0
    )


def window_kernel(rows, fields, weights, windows, spreads, gathers, kernel, back_kernel, turned):
    own = kernel.shape[0] // 3
    full, _, above = slot_flags(rows)
    column = iota((1, FRAME), 1) % TS
    lane128 = iota((1, 128), 1)
    tiles = [fields[k].astype(F32) * full[k] for k in range(SLOTS)]
    for k in range(SLOTS):
        north = jnp.zeros((C, 128), F32)
        south = jnp.zeros((C, 128), F32)
        for l in range(SLOTS):
            if l != k:
                north = north + above[k][l] * tiles[l][:, :128]
                south = south + above[l][k] * tiles[l][:, 128:]
        ends = jnp.where(lane128 < TS, north, jnp.where(lane128 >= 128 - TS, south, 0.0))
        centre = jnp.concatenate([tiles[k], ends], axis=1)
        windows[k, :C] = jnp.where(column == 0, 0.0, pltpu.roll(centre, 1, 1)).astype(BF16)
        windows[k, C : 2 * C] = centre.astype(BF16)
        windows[k, 2 * C :] = jnp.where(column == TS - 1, 0.0, pltpu.roll(centre, FRAME - 1, 1)).astype(BF16)
    for refs, shape, halo_dim in ((spreads, (128, FRAME), 0), (gathers, (FRAME, 128), 1)):
        p_at = iota(shape, halo_dim)
        frame_lane = iota(shape, 1 - halo_dim)
        for side in range(2):
            for k in range(SLOTS):
                p = p_at - (side * EAST + k * EDGE)
                spot = jnp.where(p == 0, FRAME - TS, TS * (p - 1)) + side * (TS - 1)
                hits = (p >= 0) & (p < EDGE) & (frame_lane == spot)
                refs[side, k] = jnp.where(hits, 1.0, 0.0).astype(BF16)
    stack = stack_of(weights)
    kernel[...] = stack
    back_kernel[...] = turn(stack, turned)


def column_of(line):
    own = line.shape[1]
    eye = iota((own, own), 0) == iota((own, own), 1)
    return jnp.sum(jnp.where(eye, line, 0.0), axis=1, keepdims=True)


def activation(kernel, window, bias_column, up):
    own = bias_column.shape[0]
    sums = dot(kernel, window)
    pre = (
        pltpu.roll(sums[:own], TS, 1)[:, :CELLS]
        + sums[own : 2 * own, :CELLS]
        + pltpu.roll(sums[2 * own :], FRAME - TS, 1)[:, :CELLS]
        + bias_column
    )
    square = pre * pre
    tanh = jnp.tanh(GELU_C * (pre * (1.0 + GELU_K * square)))
    half = 0.5 + 0.5 * tanh
    slope = half + (0.5 * pre) * (1.0 - tanh * tanh) * (GELU_C + (3.0 * GELU_C * GELU_K) * square)
    return pre * half, (up * slope).astype(BF16).astype(F32)


def frame_of(slopes):
    own = slopes.shape[0]
    wide = jnp.concatenate([slopes, jnp.zeros((own, FRAME - CELLS), F32)], axis=1)
    return jnp.concatenate([pltpu.roll(wide, FRAME - TS, 1), wide, pltpu.roll(wide, TS, 1)], axis=0).astype(BF16)


def half_of(count):
    position = lax.axis_index("tiles")
    rep = lax.axis_index("rep")
    if count == 4:
        return (rep + position + position // 2) % 2
    return rep


def forward_kernel(rows, fields, bias, cot, kernel, spreads, windows, *refs, n_halos, half_rows, count):
    halos = refs[:n_halos]
    frames, slopes_out, result, keep, send = refs[n_halos:]
    own = kernel.shape[0] // 3
    full, at_top, _ = slot_flags(rows)
    start = pl.multiple_of(lax.axis_index("chan") * own, own)
    half = half_of(count)
    lane128 = iota((1, 128), 1)
    bias_column = column_of(bias[...])
    halo = halos[0][...].astype(F32)
    for ref in halos[1:]:
        halo = halo + ref[...].astype(F32)
    turned = pltpu.roll(halo, 128 - FOLD, 1)
    fold = jnp.where(lane128 < TS, turned, 0.0)
    fold_left = jnp.where((lane128 > 0) & (lane128 < TS), pltpu.roll(turned, 1, 1), 0.0)
    fold_right = jnp.where(lane128 < TS - 1, pltpu.roll(turned, 127, 1), 0.0)
    halo = halo.astype(BF16)
    slope_frames, full_windows = [], []
    slope_sum = jnp.zeros((own, CELLS), F32)
    for k in range(SLOTS):
        west = dot(halo, spreads[0, k])
        east = dot(halo, spreads[1, k])
        rest = jnp.zeros((C, CELLS), F32)
        left = windows[k, :C] + (west + jnp.concatenate([rest, at_top[k] * fold_left], axis=1)).astype(BF16)
        right = windows[k, 2 * C :] + (east + jnp.concatenate([rest, at_top[k] * fold_right], axis=1)).astype(BF16)
        centre = windows[k, C : 2 * C] + jnp.concatenate([rest, at_top[k] * fold], axis=1).astype(BF16)
        window = jnp.concatenate([left, centre, right], axis=0)
        up = cot[k].astype(F32) * full[k]
        gelu, slopes = activation(kernel[...], window, bias_column, up)
        result[k] = (full[k] * (fields[k, pl.ds(start, own), :].astype(F32) + gelu)).astype(BF16)
        slope_sum = slope_sum + slopes
        slopes_out[k * own : (k + 1) * own, :] = slopes.astype(BF16)
        frame = frame_of(slopes)
        frames[k] = frame
        slope_frames.append(frame)
        full_windows.append(window)
    grads = dot(jnp.concatenate(slope_frames, axis=1), jnp.concatenate(full_windows, axis=1), ((1,), (1,)))
    blocks = [grads[a * own : (a + 1) * own, b * C : (b + 1) * C] for a in range(3) for b in range(3)]
    eye = iota((own, 128), 0) == iota((own, 128), 1)
    bias_line = jnp.sum(jnp.where(eye, jnp.sum(slope_sum, axis=1, keepdims=True), 0.0), axis=0, keepdims=True)
    blocks.append(bias_line)
    blocks.append(jnp.zeros((2 * half_rows - 9 * own - 1, 128), F32))
    sums = jnp.concatenate(blocks, axis=0)
    low, high = sums[:half_rows], sums[half_rows:]
    keep[...] = jnp.where(half == 0, low, high)
    send[...] = jnp.where(half == 0, high, low)


def turn_kernel(*refs):
    n = (len(refs) - 1) // 2
    for ref, back_kernel in zip(refs[:n], refs[n : 2 * n]):
        back_kernel[...] = turn(stack_of(ref), refs[-1])


def backward_kernel(rows, cot, gathers, result, own_frames, *refs):
    base, edges, result_out, sem = refs[-4:]
    n = (len(refs) - 5) // 2
    slopes, back_kernels = refs[:n], refs[n : 2 * n + 1]
    own = back_kernels[0].shape[0] // 3
    put = pltpu.make_async_copy(result, result_out.at[0], sem)
    put.start()
    full, at_top, above = slot_flags(rows)
    column = iota((1, FRAME), 1) % TS
    lane128 = iota((1, 128), 1)
    edge_sum = jnp.zeros((own, 128), F32)
    pads, rims, places = [], [], []
    for k in range(SLOTS):
        spread = dot(back_kernels[0][...], own_frames[k])
        for other, back_kernel in zip(slopes, back_kernels[1:]):
            frame = frame_of(other[k * own : (k + 1) * own, :].astype(F32))
            spread = spread + dot(back_kernel[...], frame)
        first, second, third = spread[:own], spread[own : 2 * own], spread[2 * own :]
        pad = (
            second
            + jnp.where(column < TS - 1, pltpu.roll(first, FRAME - 1, 1), 0.0)
            + jnp.where(column > 0, pltpu.roll(third, 1, 1), 0.0)
        )
        pads.append(pad)
        rims += [first.astype(BF16), third.astype(BF16)]
        places += [gathers[0, k], gathers[1, k]]
        crest = jnp.where(lane128 < TS, pad[:, CELLS:], 0.0) * at_top[k]
        edge_sum = edge_sum + pltpu.roll(crest, FOLD, 1)
    edge_sum = edge_sum + dot(jnp.concatenate(rims, axis=1), jnp.concatenate(places, axis=0))
    edges[...] = edge_sum.astype(BF16)
    for k in range(SLOTS):
        first = pads[k][:, :128]
        second = pads[k][:, 128:CELLS]
        for l in range(SLOTS):
            if l != k:
                ends = pads[l][:, CELLS:]
                first = first + jnp.where(lane128 < TS, ends, 0.0) * above[l][k]
                second = second + jnp.where(lane128 >= 128 - TS, ends, 0.0) * above[k][l]
        base[k] = cot[k].astype(F32) * full[k] + jnp.concatenate([first, second], axis=1)
    put.wait()


def finish_kernel(base, *refs):
    out = refs[-1]
    n = len(refs) // 2
    parts = jnp.concatenate([ref[...] for ref in refs[:n]], axis=1)
    total = dot(parts, jnp.concatenate([ref[...] for ref in refs[n : 2 * n]], axis=1), ((1,), (1,)))
    for k in range(SLOTS):
        out[0, k] = (base[k] + total[:, k * CELLS : (k + 1) * CELLS]).astype(BF16)


def gather_kernel(mine, theirs, weights_out, bias_out, *, count):
    half = half_of(count)
    own = weights_out.shape[1]
    low = jnp.where(half == 0, mine[...], theirs[...])
    high = jnp.where(half == 0, theirs[...], mine[...])
    sums = jnp.concatenate([low, high], axis=0)
    for t in range(9):
        weights_out[t] = sums[t * own : (t + 1) * own]
    bias_out[...] = sums[9 * own : 9 * own + 1, :own]


SMEM = pl.BlockSpec(memory_space=pltpu.SMEM)
VMEM = pl.BlockSpec(memory_space=pltpu.VMEM)
HBM = pl.BlockSpec(memory_space=pltpu.HBM)


def call(kernel, specs, outs, scratch=(), out_specs=None, cost=None):
    return pl.pallas_call(
        kernel,
        in_specs=specs,
        out_specs=out_specs or [VMEM] * len(outs),
        out_shape=outs,
        scratch_shapes=list(scratch),
        cost_estimate=cost,
        compiler_params=pltpu.CompilerParams(vmem_limit_bytes=40 << 20),
    )


def struct(shape, dtype):
    return jax.ShapeDtypeStruct(shape, dtype)


def on_device(fields, tile_rows, weights, bias, cotangent):
    own = weights.shape[1]
    count = lax.axis_size("tiles")
    chans = lax.axis_size("chan")
    reps = lax.axis_size("rep")
    plans = halo_plans(count)
    n = len(plans)
    half_rows = -(-(9 * own + 1) // 32) * 16
    swap = [(0, 1), (1, 0)]

    pinned = [
        pltpu.with_memory_space_constraint(x, pltpu.HBM)
        for x in (tile_rows, fields, weights, bias.reshape(1, own), cotangent)
    ]
    rows, tiles, taps, bias_line, cot, *packed = call(
        lambda *refs: pack_kernel(*refs, count=count),
        [HBM] * 5,
        [
            struct(tile_rows.shape, jnp.int32),
            struct((SLOTS, C, CELLS), BF16),
            struct((9, own, C), BF16),
            struct((1, own), F32),
            struct((SLOTS, own, CELLS), BF16),
        ]
        + [struct((SLOTS * CELLS, 128), BF16)] * n
        + [struct((C, 128), BF16)] * n,
        [pltpu.SMEM(tile_rows.shape, jnp.int32), pltpu.SemaphoreType.DMA((5,))],
    )(*pinned)
    maps, messages = packed[:n], packed[n:]

    def move(x, route):
        return lax.ppermute(x, "tiles", [(i, route(i)) for i in range(count)])

    halos = [x if route is None else move(x, route) for x, (route, _) in zip(messages, plans)]
    ring = [[(i, (i + s) % chans) for i in range(chans)] for s in range(1, chans)]
    others = [lax.ppermute(taps, "chan", pairs) for pairs in ring]

    windows, spreads, gathers, kernel, back_kernel = call(
        window_kernel,
        [SMEM] + [VMEM] * 2,
        [
            struct((SLOTS, 3 * C, FRAME), BF16),
            struct((2, SLOTS, 128, FRAME), BF16),
            struct((2, SLOTS, FRAME, 128), BF16),
            struct((3 * own, 3 * C), BF16),
            struct((3 * own, 3 * own), BF16),
        ],
        [pltpu.VMEM((3 * C, 3 * own), F32)],
    )(rows, tiles, taps)

    frames, slopes, result, keep, send = call(
        lambda *refs: forward_kernel(*refs, n_halos=len(halos), half_rows=half_rows, count=count),
        [SMEM] + [VMEM] * (6 + len(halos)),
        [
            struct((SLOTS, 3 * own, FRAME), BF16),
            struct((SLOTS * own, CELLS), BF16),
            struct((SLOTS, own, CELLS), BF16),
            struct((half_rows, 128), F32),
            struct((half_rows, 128), F32),
        ],
        cost=pl.CostEstimate(flops=4 * 10**9, transcendentals=0, bytes_accessed=0),
    )(rows, tiles, bias_line, cot, kernel, spreads, windows, *halos)

    met = [lax.ppermute(slopes, "chan", pairs) for pairs in ring]
    send, others = lax.optimization_barrier((send, others))
    sums = keep + lax.ppermute(send, "rep", swap)
    rounded = sums.astype(BF16)
    frames, rounded, others = lax.optimization_barrier((frames, rounded, others))
    turned = call(
        turn_kernel,
        [VMEM] * len(others),
        [struct((3 * own, 3 * own), BF16)] * len(others),
        [pltpu.VMEM((3 * C, 3 * own), F32)],
    )(*others)

    base, edges, result = call(
        backward_kernel,
        [SMEM] + [VMEM] * (5 + 2 * len(others)),
        [
            struct((SLOTS, own, CELLS), F32),
            struct((own, 128), BF16),
            struct((1, SLOTS, own, CELLS), BF16),
        ],
        [pltpu.SemaphoreType.DMA],
        out_specs=[VMEM, VMEM, HBM],
    )(rows, cot, gathers, result, frames, *met, back_kernel, *turned)

    if count == 4:

        def cross(x, route):
            pairs = [(2 * d + r, 2 * route(d) + 1 - r) for d in range(count) for r in range(2)]
            return lax.ppermute(x, ("tiles", "rep"), pairs)

        across = cross(edges, lambda d: d ^ 2)
        beside = lax.ppermute(edges, "rep", swap)
        other = cross(rounded, lambda d: d ^ 2)
        rounded = (rounded.astype(F32) + other.astype(F32)).astype(BF16)
        sums = rounded.astype(F32) + cross(rounded, lambda d: d ^ 1).astype(F32)
        both = cross(jnp.concatenate([beside, across], axis=0), lambda d: d ^ 1)
        across = lax.ppermute(across, "rep", swap)
        returned = [both[own:], across, both[:own], edges]
    else:
        for step in range(count.bit_length() - 1):
            other = move(rounded, lambda d: d ^ (1 << step))
            sums = rounded.astype(F32) + other.astype(F32)
            rounded = sums.astype(BF16)
        returned = [
            lax.ppermute(edges, "tiles", [(route(j), j) for j in range(count)]) for route, _ in plans
        ]
    grad_scale = 1.0 / math.sqrt(reps * fields.shape[0] * count * SLOTS * CELLS)
    sums = sums * grad_scale
    grad_fields = call(
        finish_kernel,
        [VMEM] * (1 + 2 * n),
        [struct((1, SLOTS, own, CELLS), BF16)],
    )(base, *returned, *maps)[0]
    grad_weights, grad_bias = call(
        lambda *refs: gather_kernel(*refs, count=count),
        [VMEM, VMEM],
        [struct((9, own, C), F32), struct((1, own), F32)],
    )(sums, lax.ppermute(sums, "rep", swap))
    return (result, grad_fields, grad_weights, grad_bias.reshape(own))


def solution(mesh):
    in_specs = (
        P(("groups", "rep"), "tiles", None, None),
        P(),
        P(None, "chan", None),
        P("chan"),
        P(("groups", "rep"), "tiles", "chan", None),
    )
    out_specs = (
        P(("groups", "rep"), "tiles", "chan", None),
        P(("groups", "rep"), "tiles", "chan", None),
        P("groups", "chan", None),
        P(("groups", "chan")),
    )
    return jax.shard_map(
        on_device, mesh=mesh, in_specs=in_specs, out_specs=out_specs, check_vma=False
    )
```
